256 devices in a mesh: inst: 8 (over y, x_lo), ax: 16 (over z, core), circ: 2 (over x_hi).
Axes of the slice: x: 4 (x_hi: 2, x_lo: 2; x = x_hi * 2 + x_lo), y: 4, z: 8, core: 2. Of those that a mesh axis runs over, the one named last changes fastest.
Arguments:
- flow_state: float32 [8, 7, 128, 128, 128], P('inst', None, 'ax', 'circ'), may hold values from -2 to 40, as said below
- thinc_flags: int32 [8, 128, 128], P('inst', 'ax', 'circ'), may hold values 0 or 1
Outputs:
- new_state: float32 [8, 7, 128, 128, 128], P('inst', None, 'ax', 'circ')
The draws below stay inside these ranges and needn't reach their ends.
Inputs may be any that keep to these rules, and one draw needn't show every extreme that they name: `flow_state`: every cell holds a two-phase state with positive partial densities and positive pressure, whose seventh field, the volume fraction, lies between 0.02 and 0.98.
All inputs are finite; a program needn't handle non-finite values. No bound on the sum of `thinc_flags` on one device may be relied on, other than what follows from the above.
Results may differ from the reference program's by a relative error of at most 0.0003.
Values sent between devices are 32-bit elements; how exact they have to be, the bound alone decides.
No kernel may reach another device: no remote copies, remote signals or barrier semaphores. Data moves between devices by JAX's collectives and lax.ppermute only.
A program may use at most 64 MiB of HBM per device.

```python
import jax
import jax.numpy as jnp
from jax import lax

RADIAL = 128
INSTANCES = 8
AXIAL = 128
CIRCUM = 128


G_LIQ = 4.4


P_LIQ = 6.0


G_GAS = 1.4


def draw_flow_state(key, part):
    streams = jax.random.split(jax.random.fold_in(key, 17), 8)
    grid_shape = (INSTANCES, AXIAL, CIRCUM, RADIAL)
    fraction = jax.random.uniform(streams[0], grid_shape, jnp.float32, 0.02, 0.98)
    dens_liq = jax.random.uniform(streams[1], grid_shape, jnp.float32, 0.8, 1.2)
    dens_gas = jax.random.uniform(streams[2], grid_shape, jnp.float32, 0.1, 0.3)
    pressure = jax.random.uniform(streams[3], grid_shape, jnp.float32, 0.5, 2.0)
    vel_ax = 1.0 + 0.4 * jax.random.truncated_normal(streams[4], -2.0, 2.0, grid_shape, jnp.float32)
    vel_circ = 0.4 * jax.random.truncated_normal(streams[5], -2.0, 2.0, grid_shape, jnp.float32)
    vel_rad = 0.25 * jax.random.truncated_normal(streams[6], -2.0, 2.0, grid_shape, jnp.float32)
    part_liq = fraction * dens_liq
    part_gas = (1.0 - fraction) * dens_gas
    density = part_liq + part_gas
    gamma_term = fraction / (G_LIQ - 1.0) + (1.0 - fraction) / (G_GAS - 1.0)
    stiff_term = fraction * (G_LIQ * P_LIQ / (G_LIQ - 1.0))
    kinetic = 0.5 * density * (vel_ax * vel_ax + vel_circ * vel_circ + vel_rad * vel_rad)
    energy = gamma_term * pressure + stiff_term + kinetic
    return jnp.stack([part_liq, part_gas, density * vel_ax, density * vel_circ, density * vel_rad, energy, fraction], axis=1)


def touch_ends(array, rng, smallest, high):
    index_at = [jax.random.randint(jax.random.fold_in(rng, axis), (), 0, length) for axis, length in enumerate(array.shape)]
    longest = array.shape.index(max(array.shape))
    beside = index_at[:longest] + [(index_at[longest] + 1) % array.shape[longest]] + index_at[longest + 1:]
    return array.at[tuple(index_at)].set(smallest).at[tuple(beside)].set(high)


def setup_inputs(seed: int = 0) -> dict:
    keys = jax.random.split(jax.random.key(seed), 3)
    return {
        "flow_state": draw_flow_state(jax.random.fold_in(keys[2], 71), 0),
        "thinc_flags": touch_ends((jax.random.randint(keys[1], (INSTANCES, AXIAL, CIRCUM), 0, 2) < 1).astype(jnp.int32), jax.random.fold_in(keys[1], 1), 0, 1),
    }


G_LIQ = 4.4
P_LIQ = 6.0
G_GAS = 1.4
BETA = 1.6
EPSA = 0.1
ALPHA = 4.0
DIAG0 = 0.016
OMEGA = 1.0
NU_T = 0.25

def spectral_table(period_count):
    harmonic = jnp.arange(period_count, dtype=jnp.int32)
    phase_angle = jnp.pi / period_count * harmonic.astype(jnp.float32)
    sine_safe = jnp.where(harmonic == 0, 1.0, jnp.sin(phase_angle))
    parity = jnp.where(harmonic % 2 == 0, 1.0, -1.0)
    first_der = jnp.where(harmonic == 0, 0.0, 0.5 * parity * jnp.cos(phase_angle) / sine_safe)
    second = jnp.where(harmonic == 0, -(period_count * period_count + 2) / 12.0, -parity / (2.0 * sine_safe * sine_safe))
    return OMEGA * first_der - NU_T * OMEGA * OMEGA * second

def primitives(cells):
    density = cells[0] + cells[1]
    vel_ax = cells[2] / density
    vel_circ = cells[3] / density
    vel_rad = cells[4] / density
    fraction = cells[6]
    gamma_term = fraction / (G_LIQ - 1.0) + (1.0 - fraction) / (G_GAS - 1.0)
    stiff_term = fraction * (G_LIQ * P_LIQ / (G_LIQ - 1.0))
    kinetic = 0.5 * density * (vel_ax * vel_ax + vel_circ * vel_circ + vel_rad * vel_rad)
    pressure = (cells[5] - kinetic - stiff_term) / gamma_term
    sound_speed = jnp.sqrt(((1.0 + 1.0 / gamma_term) * pressure + stiff_term / gamma_term) / density)
    return (density, vel_ax, vel_circ, pressure, sound_speed)

def sharpen(lower_val, centre, upper_val, offset):
    average = 0.5 * (lower_val + upper_val)
    difference = upper_val - lower_val
    steepness = 2.0 * (centre - average) / (jnp.abs(difference) + EPSA)
    return average + 0.5 * difference * jnp.tanh(BETA * (steepness + offset))

def physical(cells, fraction, circ_vel, pressure):
    return [cells[0] * circ_vel, cells[1] * circ_vel, cells[2] * circ_vel, cells[3] * circ_vel + pressure, cells[4] * circ_vel, (cells[5] + pressure) * circ_vel, fraction * circ_vel]

def face_flux(left_state, right_state, frac_left, frac_right):
    _, _, circ_left, press_left, sound_left = primitives(left_state)
    _, _, circ_right, press_right, sound_right = primitives(right_state)
    speed = jnp.maximum(jnp.abs(circ_left) + sound_left, jnp.abs(circ_right) + sound_right)
    flux_left = physical(left_state, frac_left, circ_left, press_left)
    flux_right = physical(right_state, frac_right, circ_right, press_right)
    jumps = [right_state[component] - left_state[component] for component in range(6)]
    jumps.append(frac_right - frac_left)
    return jnp.stack([0.5 * (flux_left[component] + flux_right[component]) - 0.5 * speed * jumps[component] for component in range(7)])

def circ_residual(cells, flag_block):
    fraction = cells[6]
    frac_back2 = jnp.roll(fraction, 2, axis=1)
    frac_back1 = jnp.roll(fraction, 1, axis=1)
    frac_next = jnp.roll(fraction, -1, axis=1)
    flagged = (flag_block > 0)[:, :, None]
    frac_left = jnp.where(flagged, sharpen(frac_back2, frac_back1, fraction, 1.0), frac_back1)
    frac_right = jnp.where(flagged, sharpen(frac_back1, fraction, frac_next, -1.0), fraction)
    fluxes = face_flux(jnp.roll(cells, 1, axis=2), cells, frac_left, frac_right)
    return jnp.roll(fluxes, -1, axis=2) - fluxes

def advance(operands):
    cells, spectral, flag_block = operands
    residual = circ_residual(cells, flag_block) + spectral
    _, vel_ax, _, _, sound_speed = primitives(cells)
    radius = jnp.abs(vel_ax) + sound_speed
    coupling = jnp.moveaxis(-ALPHA * radius, 0, -1)
    diagonal = jnp.moveaxis(DIAG0 + 2.0 * ALPHA * radius, 0, -1)
    lower_coef = coupling.at[..., 0].set(0.0)
    upper_coef = coupling.at[..., -1].set(0.0)
    full_shape = (cells.shape[0],) + coupling.shape
    right_side = jnp.moveaxis(-residual, 1, -1)[..., None]
    delta = lax.linalg.tridiagonal_solve(jnp.broadcast_to(lower_coef, full_shape), jnp.broadcast_to(diagonal, full_shape), jnp.broadcast_to(upper_coef, full_shape), right_side)[..., 0]
    return cells + jnp.moveaxis(delta, -1, 1)

def reference(flow_state, thinc_flags):
    period_count = flow_state.shape[0]
    table_values = spectral_table(period_count)
    positions = jnp.arange(period_count, dtype=jnp.int32)
    lag_index = (positions[:, None] - positions[None, :]) % period_count
    weight_matrix = table_values[lag_index]
    spectral = jnp.einsum('nm,mfacr->nfacr', weight_matrix, flow_state, precision=lax.Precision.HIGHEST)
    return lax.map(advance, (flow_state, spectral, thinc_flags))
```

```python
import functools
import math

import jax
import jax.numpy as jnp
from jax import lax
from jax.experimental import pallas as pl
from jax.experimental.pallas import tpu as pltpu
from jax.sharding import PartitionSpec as P

G_LIQ = 4.4
P_LIQ = 6.0
G_GAS = 1.4
BETA = 1.6
EPSA = 0.1
ALPHA = 4.0
DIAG0 = 0.016
OMEGA = 1.0
NU_T = 0.25

FIELDS = 7
TILE = 8
CHUNKS = ((0, 7),)


VMEM = pl.BlockSpec(memory_space=pltpu.VMEM)


def spectral_weights(count):
    table = []
    for k in range(count):
        if k == 0:
            first, second = 0.0, -(count * count + 2) / 12.0
        else:
            sign = 1.0 if k % 2 == 0 else -1.0
            angle = math.pi * k / count
            first = 0.5 * sign * math.cos(angle) / math.sin(angle)
            second = -sign / (2.0 * math.sin(angle) ** 2)
        table.append(OMEGA * first - NU_T * OMEGA * OMEGA * second)
    return table


def call(kernel, outs, *operands, flops=0):
    outs = [jax.ShapeDtypeStruct(shape, jnp.float32) for shape in outs]
    total = sum(x.size * 4 for x in operands) + sum(x.size * 4 for x in outs)
    return pl.pallas_call(
        kernel,
        out_shape=outs,
        in_specs=[VMEM] * len(operands),
        out_specs=[VMEM] * len(outs),
        cost_estimate=pl.CostEstimate(flops=flops, bytes_accessed=total, transcendentals=0),
    )(*operands)


def spectral_kernel(weights, state_ref, out_ref):
    count, fields, rows, _ = state_ref.shape
    half = count // 2
    even = [0.5 * (weights[k] + weights[k + half]) for k in range(half)]
    odd = [0.5 * (weights[k] - weights[k + half]) for k in range(half)]

    def step(index, _):
        field = index // (rows // TILE)
        span = pl.ds(pl.multiple_of((index % (rows // TILE)) * TILE, TILE), TILE)
        cells = [state_ref[m, field, span] for m in range(count)]
        sums = [cells[m] + cells[m + half] for m in range(half)]
        diffs = [cells[m] - cells[m + half] for m in range(half)]
        for n in range(half):
            total = sum(even[(n - m) % half] * sums[m] for m in range(half))
            alternate = sum(
                (odd[n - m] if n >= m else -odd[n - m + half]) * diffs[m] for m in range(half)
            )
            out_ref[n, field, span] = total + alternate
            out_ref[n + half, field, span] = total - alternate
        return 0

    lax.fori_loop(0, fields * (rows // TILE), step, 0)


def primitives(cells):
    density = cells[0] + cells[1]
    inverse = 1.0 / density
    vel_ax = cells[2] * inverse
    vel_circ = cells[3] * inverse
    vel_rad = cells[4] * inverse
    fraction = cells[6]
    gamma_term = fraction / (G_LIQ - 1.0) + (1.0 - fraction) / (G_GAS - 1.0)
    stiff_term = fraction * (G_LIQ * P_LIQ / (G_LIQ - 1.0))
    kinetic = 0.5 * density * (vel_ax * vel_ax + vel_circ * vel_circ + vel_rad * vel_rad)
    gamma_inv = 1.0 / gamma_term
    pressure = (cells[5] - kinetic - stiff_term) * gamma_inv
    sound_speed = jnp.sqrt(((1.0 + gamma_inv) * pressure + stiff_term * gamma_inv) * inverse)
    return vel_ax, vel_circ, pressure, sound_speed


def sharpen(lower_val, centre, upper_val, offset):
    average = 0.5 * (lower_val + upper_val)
    difference = upper_val - lower_val
    steepness = 2.0 * (centre - average) / (jnp.abs(difference) + EPSA)
    return average + 0.5 * difference * jnp.tanh(BETA * (steepness + offset))


def flux_kernel(state_ref, halo_ref, flag_ref, res_ref, coup_ref, inv_ref, v_ref, w_ref, red_ref):
    planes = state_ref.shape[2]
    rows = state_ref.shape[3]
    last = planes - 1

    def plane(i, _):
        cells = []
        for f in range(FIELDS):
            edge = halo_ref[f, i]
            cells.append(
                jnp.concatenate(
                    [state_ref[0, f, i], edge[0:2], edge[0:2], edge[2:4], edge[2:4]], axis=0
                )
            )
        edge = halo_ref[FIELDS, i]
        flags = jnp.concatenate([flag_ref[i], edge, edge], axis=0)
        total = rows + TILE

        def below(x, by=1):
            return pltpu.roll(x, by, 0)

        def above(x):
            return pltpu.roll(x, total - 1, 0)

        vel_ax, vel_circ, pressure, sound = primitives(cells)
        coup_ref[i] = -ALPHA * (jnp.abs(vel_ax) + sound)[:rows]
        wave = jnp.abs(vel_circ) + sound
        half_speed = 0.5 * jnp.maximum(below(wave), wave)
        fraction = cells[6]
        back1 = below(fraction)
        sharp_left = sharpen(below(fraction, 2), back1, fraction, 1.0)
        sharp_right = sharpen(back1, fraction, above(fraction), -1.0)
        flagged = flags > 0.5
        frac_left = jnp.where(flagged, sharp_left, back1)
        frac_right = jnp.where(flagged, sharp_right, fraction)
        for f in range(FIELDS):
            if f < 6:
                flux = cells[f] * vel_circ
                if f == 3:
                    flux = flux + pressure
                elif f == 5:
                    flux = flux + pressure * vel_circ
                mean = 0.5 * (below(flux) + flux)
                jump = cells[f] - below(cells[f])
            else:
                mean = 0.5 * (frac_left * below(vel_circ) + frac_right * vel_circ)
                jump = frac_right - frac_left
            face = mean - half_speed * jump
            res_ref[i, f] = (above(face) - face)[:rows]
        return 0

    lax.fori_loop(0, planes, plane, 0)

    def factor(t, _):
        span = pl.ds(pl.multiple_of(t * TILE, TILE), TILE)
        coup = [coup_ref[i, span] for i in range(planes)]
        inv, ratio, v = [], [], []
        for i in range(last):
            pivot = DIAG0 - 2.0 * coup[i]
            if i:
                pivot = pivot - coup[i] * ratio[-1]
            inv.append(1.0 / pivot)
            ratio.append(coup[i] * inv[-1])
            v.append(inv[-1] if i == 0 else -(ratio[-1] * v[-1]))
            inv_ref[i, span] = inv[-1]
        v_next, w_next = v[-1], inv[-1]
        v_last, w_last = v_next * coup[0], w_next * coup[last - 1]
        for i in range(last - 1, -1, -1):
            if i < last - 1:
                v_next = v[i] - ratio[i] * v_next
                w_next = -(ratio[i] * w_next)
            v_first, w_first = v_next * coup[0], w_next * coup[last - 1]
            v_ref[i, span] = v_first
            w_ref[i, span] = w_first
        sep = coup[last]
        rows_out = (
            -(sep * v_last),
            DIAG0 - 2.0 * sep - sep * w_last,
            sep,
            v_first,
            w_first,
        )
        for k, value in enumerate(rows_out):
            red_ref[2 * t, k] = value[0:4]
            red_ref[2 * t + 1, k] = value[4:8]
        return 0

    lax.fori_loop(0, rows // TILE, factor, 0)


def sweep_kernel(first, res_ref, spec_ref, coup_ref, inv_ref, y_ref, red_ref):
    planes, fields, rows, _ = spec_ref.shape
    last = planes - 1

    def step(t, _):
        span = pl.ds(pl.multiple_of(t * TILE, TILE), TILE)
        coup = [coup_ref[i, span] for i in range(planes)]
        inv = [inv_ref[i, span] for i in range(last)]
        ratio = [coup[i] * inv[i] for i in range(last)]
        for f in range(fields):
            value = []
            for i in range(last):
                right = -(res_ref[i, first + f, span] + spec_ref[i, f, span])
                if i:
                    right = right - coup[i] * value[-1]
                value.append(right * inv[i])
            y = value[-1]
            y_last = y
            y_ref[last - 1, f, span] = y
            for i in range(last - 2, -1, -1):
                y = value[i] - ratio[i] * y
                y_ref[i, f, span] = y
            right = -(res_ref[last, first + f, span] + spec_ref[last, f, span])
            own = right - coup[last] * y_last
            for k, x in ((f, y), (fields + f, own)):
                red_ref[2 * t, k] = x[0:4]
                red_ref[2 * t + 1, k] = x[4:8]
        return 0

    lax.fori_loop(0, rows // TILE, step, 0)


def reduced_kernel(coef_ref, rhs_ref, out_ref):
    count = coef_ref.shape[0]
    fields = rhs_ref.shape[1] // 2
    ratio = []
    values = []
    for p in range(count):
        lower, diag, sep = coef_ref[p, 0], coef_ref[p, 1], coef_ref[p, 2]
        more = p + 1 < count
        if more:
            diag = diag - sep * coef_ref[p + 1, 3]
        if p:
            diag = diag - lower * ratio[-1]
        inv = 1.0 / diag
        if more:
            ratio.append(-(sep * coef_ref[p + 1, 4]) * inv)
        row = []
        for f in range(fields):
            right = rhs_ref[p, fields + f]
            if more:
                right = right - sep * rhs_ref[p + 1, f]
            if p:
                right = right - lower * values[-1][f]
            row.append(right * inv)
        values.append(row)
    solved = values[-1]
    for p in range(count - 1, -1, -1):
        if p < count - 1:
            solved = [values[p][f] - ratio[p] * solved[f] for f in range(fields)]
        for f in range(fields):
            out_ref[p, f] = solved[f]
            if p < count - 1:
                out_ref[p + 1, fields + f] = solved[f]
    for f in range(fields):
        out_ref[0, fields + f] = jnp.zeros_like(solved[f])


def finish_kernel(chunks, state_ref, v_ref, w_ref, *refs):
    out_ref = refs[-1]
    y_refs, sep_refs = refs[: len(chunks)], refs[len(chunks) : 2 * len(chunks)]
    planes, rows = state_ref.shape[2], state_ref.shape[3]
    last = planes - 1

    def step(t, _):
        span = pl.ds(pl.multiple_of(t * TILE, TILE), TILE)
        v = [v_ref[i, span] for i in range(last)]
        w = [w_ref[i, span] for i in range(last)]
        for (first, stop), y_ref, sep_ref in zip(chunks, y_refs, sep_refs):
            fields = stop - first
            for f in range(fields):
                own = jnp.concatenate([sep_ref[2 * t, f], sep_ref[2 * t + 1, f]], axis=0)
                prev = jnp.concatenate(
                    [sep_ref[2 * t, fields + f], sep_ref[2 * t + 1, fields + f]], axis=0
                )
                for i in range(last):
                    delta = y_ref[i, f, span] - v[i] * prev - w[i] * own
                    out_ref[0, first + f, i, span] = state_ref[0, first + f, i, span] + delta
                out_ref[0, first + f, last, span] = state_ref[0, first + f, last, span] + own
        return 0

    lax.fori_loop(0, rows // TILE, step, 0)


def exchange(x, axis):
    return lax.all_to_all(x, axis, 0, 0, tiled=True)


def local(flow_state, thinc_flags):
    own = flow_state[0]
    planes, rows, lanes = own.shape[1:]
    instances = lax.axis_size("inst")
    ax_count = lax.axis_size("ax")
    piece = rows // ax_count
    weights = spectral_weights(instances)

    flags = (thinc_flags[0] > 0).astype(jnp.float32)
    edge_flags = jnp.broadcast_to(flags[None, :, 0:1, None], (1, planes, 4, lanes))
    edges = jnp.concatenate([own[:, :, 0:2], own[:, :, rows - 2 : rows]], axis=2)
    circ_count = lax.axis_size("circ")
    halo = lax.ppermute(
        jnp.concatenate([edges, edge_flags], axis=0),
        "circ",
        [(i, (i + 1) % circ_count) for i in range(circ_count)],
    )
    flag_cells = jnp.broadcast_to(flags[:, :, None], (planes, rows, lanes))

    gathered = [
        exchange(jnp.swapaxes(own[first:stop], 0, 1), "inst") for first, stop in CHUNKS
    ]
    grid = (rows, lanes)
    res, coup, inv, v, w, coefs = call(
        flux_kernel,
        [
            (planes, FIELDS) + grid,
            (planes,) + grid,
            (planes - 1,) + grid,
            (planes - 1,) + grid,
            (planes - 1,) + grid,
            (ax_count, 5, piece, lanes),
        ],
        flow_state,
        halo,
        flag_cells,
        flops=own.size * 60,
    )
    coefs = exchange(coefs, "ax")
    y_parts, sep_parts = [], []
    for (first, stop), block in zip(CHUNKS, gathered):
        fields = stop - first
        (spec,) = call(
            functools.partial(spectral_kernel, weights), [block.shape], block, flops=block.size * 9
        )
        spec = exchange(spec, "inst")
        y, rhs = call(
            functools.partial(sweep_kernel, first),
            [(planes - 1, fields) + grid, (ax_count, 2 * fields, piece, lanes)],
            res,
            spec,
            coup,
            inv,
            flops=spec.size * 8,
        )
        rhs = exchange(rhs, "ax")
        (seps,) = call(reduced_kernel, [rhs.shape], coefs, rhs, flops=rhs.size * 8)
        sep_parts.append(exchange(seps, "ax"))
        y_parts.append(y)
    (out,) = call(
        functools.partial(finish_kernel, CHUNKS),
        [flow_state.shape],
        flow_state,
        v,
        w,
        *y_parts,
        *sep_parts,
        flops=own.size * 5,
    )
    return out


def solution(mesh):
    return jax.shard_map(
        local,
        mesh=mesh,
        in_specs=(P("inst", None, "ax", "circ", None), P("inst", "ax", "circ")),
        out_specs=P("inst", None, "ax", "circ", None),
        check_vma=False,
    )
```

```python
import functools
import math

import jax
import jax.numpy as jnp
from jax import lax
from jax.experimental import pallas as pl
from jax.experimental.pallas import tpu as pltpu
from jax.sharding import PartitionSpec as P


G_LIQ = 4.4
P_LIQ = 6.0
G_GAS = 1.4
BETA = 1.6
EPSA = 0.1
ALPHA = 4.0
DIAG0 = 0.016
OMEGA = 1.0
NU_T = 0.25

FIELDS = 7
COEFS = 5
TILE = 8
CHUNKS = ((0, 7),)


VMEM = pl.BlockSpec(memory_space=pltpu.VMEM)


def spectral_weights(count):
    table = []
    for k in range(count):
        if k == 0:
            first, second = 0.0, -(count * count + 2) / 12.0
        else:
            sign = 1.0 if k % 2 == 0 else -1.0
            angle = math.pi * k / count
            first = 0.5 * sign * math.cos(angle) / math.sin(angle)
            second = -sign / (2.0 * math.sin(angle) ** 2)
        table.append(OMEGA * first - NU_T * OMEGA * OMEGA * second)
    return table


def call(kernel, outs, *operands, flops=0):
    outs = [jax.ShapeDtypeStruct(shape, jnp.float32) for shape in outs]
    total = sum(x.size * 4 for x in operands) + sum(x.size * 4 for x in outs)
    return pl.pallas_call(
        kernel,
        out_shape=outs,
        in_specs=[VMEM] * len(operands),
        out_specs=[VMEM] * len(outs),
        compiler_params=pltpu.CompilerParams(vmem_limit_bytes=20 << 20),
        cost_estimate=pl.CostEstimate(flops=flops, bytes_accessed=total, transcendentals=0),
    )(*operands)


def spectral_kernel(weights, state_ref, out_ref):
    count, fields, rows, _ = state_ref.shape
    half = count // 2
    even = [0.5 * (weights[k] + weights[k + half]) for k in range(half)]
    odd = [0.5 * (weights[k] - weights[k + half]) for k in range(half)]

    def step(index, _):
        field = index // (rows // TILE)
        span = pl.ds(pl.multiple_of((index % (rows // TILE)) * TILE, TILE), TILE)
        cells = [state_ref[m, field, span] for m in range(count)]
        sums = [cells[m] + cells[m + half] for m in range(half)]
        diffs = [cells[m] - cells[m + half] for m in range(half)]
        for n in range(half):
            total = sum(even[(n - m) % half] * sums[m] for m in range(half))
            alternate = sum(
                (odd[n - m] if n >= m else -odd[n - m + half]) * diffs[m] for m in range(half)
            )
            out_ref[n, field, span] = total + alternate
            out_ref[n + half, field, span] = total - alternate
        return 0

    lax.fori_loop(0, fields * (rows // TILE), step, 0)


def primitives(cells):
    density = cells[0] + cells[1]
    inverse = 1.0 / density
    vel_ax = cells[2] * inverse
    vel_circ = cells[3] * inverse
    vel_rad = cells[4] * inverse
    fraction = cells[6]
    gamma_term = fraction / (G_LIQ - 1.0) + (1.0 - fraction) / (G_GAS - 1.0)
    stiff_term = fraction * (G_LIQ * P_LIQ / (G_LIQ - 1.0))
    kinetic = 0.5 * density * (vel_ax * vel_ax + vel_circ * vel_circ + vel_rad * vel_rad)
    gamma_inv = 1.0 / gamma_term
    pressure = (cells[5] - kinetic - stiff_term) * gamma_inv
    sound_speed = jnp.sqrt(((1.0 + gamma_inv) * pressure + stiff_term * gamma_inv) * inverse)
    return vel_ax, vel_circ, pressure, sound_speed


def sharpen(lower_val, centre, upper_val, offset):
    average = 0.5 * (lower_val + upper_val)
    difference = upper_val - lower_val
    steepness = 2.0 * (centre - average) / (jnp.abs(difference) + EPSA)
    return average + 0.5 * difference * jnp.tanh(BETA * (steepness + offset))


def flux_kernel(state_ref, halo_ref, flag_ref, res_ref, coup_ref, inv_ref, v_ref, w_ref, red_ref):
    planes = state_ref.shape[2]
    rows = state_ref.shape[3]
    last = planes - 1

    def plane(i, _):
        cells = []
        for f in range(FIELDS):
            edge = halo_ref[f, i]
            cells.append(
                jnp.concatenate(
                    [state_ref[0, f, i], edge[0:2], edge[0:2], edge[2:4], edge[2:4]], axis=0
                )
            )
        edge = halo_ref[FIELDS, i]
        flags = jnp.concatenate([flag_ref[i], edge, edge], axis=0)
        total = rows + TILE

        def below(x, by=1):
            return pltpu.roll(x, by, 0)

        def above(x):
            return pltpu.roll(x, total - 1, 0)

        vel_ax, vel_circ, pressure, sound = primitives(cells)
        coup_ref[i] = -ALPHA * (jnp.abs(vel_ax) + sound)[:rows]
        wave = jnp.abs(vel_circ) + sound
        half_speed = 0.5 * jnp.maximum(below(wave), wave)
        fraction = cells[6]
        back1 = below(fraction)
        sharp_left = sharpen(below(fraction, 2), back1, fraction, 1.0)
        sharp_right = sharpen(back1, fraction, above(fraction), -1.0)
        flagged = flags > 0.5
        frac_left = jnp.where(flagged, sharp_left, back1)
        frac_right = jnp.where(flagged, sharp_right, fraction)
        for f in range(FIELDS):
            if f < 6:
                flux = cells[f] * vel_circ
                if f == 3:
                    flux = flux + pressure
                elif f == 5:
                    flux = flux + pressure * vel_circ
                mean = 0.5 * (below(flux) + flux)
                jump = cells[f] - below(cells[f])
            else:
                mean = 0.5 * (frac_left * below(vel_circ) + frac_right * vel_circ)
                jump = frac_right - frac_left
            face = mean - half_speed * jump
            res_ref[i, f] = (above(face) - face)[:rows]
        return 0

    lax.fori_loop(0, planes, plane, 0)

    def factor(t, _):
        span = pl.ds(pl.multiple_of(t * TILE, TILE), TILE)
        coup = [coup_ref[i, span] for i in range(planes)]
        inv, ratio, v = [], [], []
        for i in range(last):
            pivot = DIAG0 - 2.0 * coup[i]
            if i:
                pivot = pivot - coup[i] * ratio[-1]
            inv.append(1.0 / pivot)
            ratio.append(coup[i] * inv[-1])
            v.append(inv[-1] if i == 0 else -(ratio[-1] * v[-1]))
            inv_ref[i, span] = inv[-1]
        v_next, w_next = v[-1], inv[-1]
        v_last, w_last = v_next * coup[0], w_next * coup[last - 1]
        for i in range(last - 1, -1, -1):
            if i < last - 1:
                v_next = v[i] - ratio[i] * v_next
                w_next = -(ratio[i] * w_next)
            v_first, w_first = v_next * coup[0], w_next * coup[last - 1]
            v_ref[i, span] = v_first
            w_ref[i, span] = w_first
        sep = coup[last]
        rows_out = (
            -(sep * v_last),
            DIAG0 - 2.0 * sep - sep * w_last,
            sep,
            v_first,
            w_first,
        )
        for k, value in enumerate(rows_out):
            red_ref[k, span] = value
        return 0

    lax.fori_loop(0, rows // TILE, factor, 0)


def sweep_kernel(first, res_ref, spec_ref, coup_ref, inv_ref, coef_ref, y_ref, red_ref):
    planes, fields, rows, _ = spec_ref.shape
    last = planes - 1

    def step(t, _):
        span = pl.ds(pl.multiple_of(t * TILE, TILE), TILE)
        coup = [coup_ref[i, span] for i in range(planes)]
        inv = [inv_ref[i, span] for i in range(last)]
        ratio = [coup[i] * inv[i] for i in range(last)]
        for f in range(fields):
            value = []
            for i in range(last):
                right = -(res_ref[i, first + f, span] + spec_ref[i, f, span])
                if i:
                    right = right - coup[i] * value[-1]
                value.append(right * inv[i])
            y = value[-1]
            y_last = y
            y_ref[last - 1, f, span] = y
            for i in range(last - 2, -1, -1):
                y = value[i] - ratio[i] * y
                y_ref[i, f, span] = y
            right = -(res_ref[last, first + f, span] + spec_ref[last, f, span])
            own = right - coup[last] * y_last
            for k, x in ((f, y), (fields + f, own)):
                red_ref[2 * t, k] = x[0:4]
                red_ref[2 * t + 1, k] = x[4:8]
        for k in range(COEFS):
            x = coef_ref[k, span]
            red_ref[2 * t, 2 * fields + k] = x[0:4]
            red_ref[2 * t + 1, 2 * fields + k] = x[4:8]
        return 0

    lax.fori_loop(0, rows // TILE, step, 0)


def reduced_kernel(rhs_ref, out_ref):
    count = rhs_ref.shape[0]
    fields = out_ref.shape[1] // 2
    base = 2 * fields
    ratio = []
    values = []
    for p in range(count):
        lower, diag, sep = rhs_ref[p, base], rhs_ref[p, base + 1], rhs_ref[p, base + 2]
        more = p + 1 < count
        if more:
            diag = diag - sep * rhs_ref[p + 1, base + 3]
        if p:
            diag = diag - lower * ratio[-1]
        inv = 1.0 / diag
        if more:
            ratio.append(-(sep * rhs_ref[p + 1, base + 4]) * inv)
        row = []
        for f in range(fields):
            right = rhs_ref[p, fields + f]
            if more:
                right = right - sep * rhs_ref[p + 1, f]
            if p:
                right = right - lower * values[-1][f]
            row.append(right * inv)
        values.append(row)
    solved = values[-1]
    for p in range(count - 1, -1, -1):
        if p < count - 1:
            solved = [values[p][f] - ratio[p] * solved[f] for f in range(fields)]
        for f in range(fields):
            out_ref[p, f] = solved[f]
            if p < count - 1:
                out_ref[p + 1, fields + f] = solved[f]
    for f in range(fields):
        out_ref[0, fields + f] = jnp.zeros_like(solved[f])


def finish_kernel(chunks, state_ref, v_ref, w_ref, *refs):
    out_ref = refs[-1]
    y_refs, sep_refs = refs[: len(chunks)], refs[len(chunks) : 2 * len(chunks)]
    planes, rows = state_ref.shape[2], state_ref.shape[3]
    last = planes - 1

    def step(t, _):
        span = pl.ds(pl.multiple_of(t * TILE, TILE), TILE)
        v = [v_ref[i, span] for i in range(last)]
        w = [w_ref[i, span] for i in range(last)]
        for (first, stop), y_ref, sep_ref in zip(chunks, y_refs, sep_refs):
            fields = stop - first
            for f in range(fields):
                own = jnp.concatenate([sep_ref[2 * t, f], sep_ref[2 * t + 1, f]], axis=0)
                prev = jnp.concatenate(
                    [sep_ref[2 * t, fields + f], sep_ref[2 * t + 1, fields + f]], axis=0
                )
                for i in range(last):
                    delta = y_ref[i, f, span] - v[i] * prev - w[i] * own
                    out_ref[0, first + f, i, span] = state_ref[0, first + f, i, span] + delta
                out_ref[0, first + f, last, span] = state_ref[0, first + f, last, span] + own
        return 0

    lax.fori_loop(0, rows // TILE, step, 0)


def exchange(x, axis):
    return lax.all_to_all(x, axis, 0, 0, tiled=True)


def body(flow_state, thinc_flags):
    own = flow_state[0]
    planes, rows, lanes = own.shape[1:]
    instances = lax.axis_size("inst")
    ax_count = lax.axis_size("ax")
    circ_count = lax.axis_size("circ")
    piece = rows // ax_count
    grid = (rows, lanes)
    weights = spectral_weights(instances)

    flags = (thinc_flags[0] > 0).astype(jnp.float32)
    edge_flags = jnp.broadcast_to(flags[None, :, 0:1, None], (1, planes, 4, lanes))
    edges = jnp.concatenate([own[:, :, 0:2], own[:, :, rows - 2 : rows]], axis=2)
    edges = jnp.concatenate([edges, edge_flags], axis=0)
    halo = lax.ppermute(
        edges, "circ", [(i, (i + 1) % circ_count) for i in range(circ_count)]
    )
    flag_cells = jnp.broadcast_to(flags[:, :, None], (planes, rows, lanes))

    gathered = [
        exchange(jnp.swapaxes(own[first:stop], 0, 1), "inst") for first, stop in CHUNKS
    ]
    res, coup, inv, v, w, coefs = call(
        flux_kernel,
        [
            (planes, FIELDS) + grid,
            (planes,) + grid,
            (planes - 1,) + grid,
            (planes - 1,) + grid,
            (planes - 1,) + grid,
            (COEFS,) + grid,
        ],
        flow_state,
        halo,
        flag_cells,
        flops=own.size * 60,
    )
    gathered, res = lax.optimization_barrier((gathered, res))
    y_parts, sep_parts = [], []
    for (first, stop), block in zip(CHUNKS, gathered):
        fields = stop - first
        (spec,) = call(
            functools.partial(spectral_kernel, weights), [block.shape], block, flops=block.size * 9
        )
        spec = exchange(spec, "inst")
        y, rhs = call(
            functools.partial(sweep_kernel, first),
            [(planes - 1, fields) + grid, (ax_count, 2 * fields + COEFS, piece, lanes)],
            res,
            spec,
            coup,
            inv,
            coefs,
            flops=spec.size * 8,
        )
        rhs = exchange(rhs, "ax")
        (seps,) = call(
            reduced_kernel, [(ax_count, 2 * fields, piece, lanes)], rhs, flops=rhs.size * 8
        )
        sep_parts.append(exchange(seps, "ax"))
        y_parts.append(y)
    (out,) = call(
        functools.partial(finish_kernel, CHUNKS),
        [flow_state.shape],
        flow_state,
        v,
        w,
        *y_parts,
        *sep_parts,
        flops=own.size * 5,
    )
    return out


def solution(mesh):
    return jax.shard_map(
        body,
        mesh=mesh,
        in_specs=(P("inst", None, "ax", "circ", None), P("inst", "ax", "circ")),
        out_specs=P("inst", None, "ax", "circ", None),
        check_vma=False,
    )
```

```python
import functools
import math

import jax
import jax.numpy as jnp
from jax import lax
from jax.experimental import pallas as pl
from jax.experimental.pallas import tpu as pltpu
from jax.sharding import PartitionSpec as P


G_LIQ = 4.4
P_LIQ = 6.0
G_GAS = 1.4
BETA = 1.6
EPSA = 0.1
ALPHA = 4.0
DIAG0 = 0.016
OMEGA = 1.0
NU_T = 0.25

FIELDS = 7
COEFS = 5
TILE = 8


VMEM = pl.BlockSpec(memory_space=pltpu.VMEM)
SMEM = pl.BlockSpec(memory_space=pltpu.SMEM)


def spectral_weights(count):
    table = []
    for k in range(count):
        if k == 0:
            first, second = 0.0, -(count * count + 2) / 12.0
        else:
            sign = 1.0 if k % 2 == 0 else -1.0
            angle = math.pi * k / count
            first = 0.5 * sign * math.cos(angle) / math.sin(angle)
            second = -sign / (2.0 * math.sin(angle) ** 2)
        table.append(OMEGA * first - NU_T * OMEGA * OMEGA * second)
    return table


def call(kernel, outs, *operands, flops=0):
    outs = [jax.ShapeDtypeStruct(shape, jnp.float32) for shape in outs]
    total = sum(x.size * 4 for x in operands) + sum(x.size * 4 for x in outs)
    return pl.pallas_call(
        kernel,
        out_shape=outs,
        in_specs=[SMEM if x.dtype == jnp.int32 else VMEM for x in operands],
        out_specs=[VMEM] * len(outs),
        compiler_params=pltpu.CompilerParams(vmem_limit_bytes=20 << 20),
        cost_estimate=pl.CostEstimate(flops=flops, bytes_accessed=total, transcendentals=0),
    )(*operands)


def spectral_kernel(weights, state_ref, out_ref):
    count, fields, rows, _ = state_ref.shape
    half = count // 2
    even = [0.5 * (weights[k] + weights[k + half]) for k in range(half)]
    odd = [0.5 * (weights[k] - weights[k + half]) for k in range(half)]

    def step(index, _):
        field = index // (rows // TILE)
        span = pl.ds(pl.multiple_of((index % (rows // TILE)) * TILE, TILE), TILE)
        cells = [state_ref[m, field, span] for m in range(count)]
        sums = [cells[m] + cells[m + half] for m in range(half)]
        diffs = [cells[m] - cells[m + half] for m in range(half)]
        for n in range(half):
            total = sum(even[(n - m) % half] * sums[m] for m in range(half))
            alternate = sum(
                (odd[n - m] if n >= m else -odd[n - m + half]) * diffs[m] for m in range(half)
            )
            out_ref[n, field, span] = total + alternate
            out_ref[n + half, field, span] = total - alternate
        return 0

    lax.fori_loop(0, fields * (rows // TILE), step, 0)


def primitives(cells):
    density = cells[0] + cells[1]
    inverse = 1.0 / density
    vel_ax = cells[2] * inverse
    vel_circ = cells[3] * inverse
    vel_rad = cells[4] * inverse
    fraction = cells[6]
    gamma_term = fraction / (G_LIQ - 1.0) + (1.0 - fraction) / (G_GAS - 1.0)
    stiff_term = fraction * (G_LIQ * P_LIQ / (G_LIQ - 1.0))
    kinetic = 0.5 * density * (vel_ax * vel_ax + vel_circ * vel_circ + vel_rad * vel_rad)
    gamma_inv = 1.0 / gamma_term
    pressure = (cells[5] - kinetic - stiff_term) * gamma_inv
    sound_speed = jnp.sqrt(((1.0 + gamma_inv) * pressure + stiff_term * gamma_inv) * inverse)
    return vel_ax, vel_circ, pressure, sound_speed


def sharpen(lower_val, centre, upper_val, offset):
    average = 0.5 * (lower_val + upper_val)
    difference = upper_val - lower_val
    steepness = 2.0 * (centre - average) / (jnp.abs(difference) + EPSA)
    return average + 0.5 * difference * jnp.tanh(BETA * (steepness + offset))


def flux_kernel(state_ref, halo_ref, flag_ref, res_ref, coup_ref, inv_ref, v_ref, w_ref, red_ref):
    planes = state_ref.shape[2]
    rows = state_ref.shape[3]
    last = planes - 1

    def plane(i, _):
        cells = []
        for f in range(FIELDS):
            edge = halo_ref[f, i]
            cells.append(
                jnp.concatenate(
                    [state_ref[0, f, i], edge[0:2], edge[0:2], edge[2:4], edge[2:4]], axis=0
                )
            )
        edge = halo_ref[FIELDS, i]
        flags = jnp.concatenate([flag_ref[i], edge, edge], axis=0)
        total = rows + TILE

        def below(x, by=1):
            return pltpu.roll(x, by, 0)

        def above(x):
            return pltpu.roll(x, total - 1, 0)

        vel_ax, vel_circ, pressure, sound = primitives(cells)
        coup_ref[i] = -ALPHA * (jnp.abs(vel_ax) + sound)[:rows]
        wave = jnp.abs(vel_circ) + sound
        half_speed = 0.5 * jnp.maximum(below(wave), wave)
        fraction = cells[6]
        back1 = below(fraction)
        sharp_left = sharpen(below(fraction, 2), back1, fraction, 1.0)
        sharp_right = sharpen(back1, fraction, above(fraction), -1.0)
        flagged = flags > 0.5
        frac_left = jnp.where(flagged, sharp_left, back1)
        frac_right = jnp.where(flagged, sharp_right, fraction)
        for f in range(FIELDS):
            if f < 6:
                flux = cells[f] * vel_circ
                if f == 3:
                    flux = flux + pressure
                elif f == 5:
                    flux = flux + pressure * vel_circ
                mean = 0.5 * (below(flux) + flux)
                jump = cells[f] - below(cells[f])
            else:
                mean = 0.5 * (frac_left * below(vel_circ) + frac_right * vel_circ)
                jump = frac_right - frac_left
            face = mean - half_speed * jump
            res_ref[i, f] = (above(face) - face)[:rows]
        return 0

    lax.fori_loop(0, planes, plane, 0)

    def factor(t, _):
        span = pl.ds(pl.multiple_of(t * TILE, TILE), TILE)
        coup = [coup_ref[i, span] for i in range(planes)]
        inv, ratio, v = [], [], []
        for i in range(last):
            pivot = DIAG0 - 2.0 * coup[i]
            if i:
                pivot = pivot - coup[i] * ratio[-1]
            inv.append(1.0 / pivot)
            ratio.append(coup[i] * inv[-1])
            v.append(inv[-1] if i == 0 else -(ratio[-1] * v[-1]))
            inv_ref[i, span] = inv[-1]
        v_next, w_next = v[-1], inv[-1]
        v_last, w_last = v_next * coup[0], w_next * coup[last - 1]
        for i in range(last - 1, -1, -1):
            if i < last - 1:
                v_next = v[i] - ratio[i] * v_next
                w_next = -(ratio[i] * w_next)
            v_first, w_first = v_next * coup[0], w_next * coup[last - 1]
            v_ref[i, span] = v_first
            w_ref[i, span] = w_first
        sep = coup[last]
        rows_out = (
            -(sep * v_last),
            DIAG0 - 2.0 * sep - sep * w_last,
            sep,
            v_first,
            w_first,
        )
        for k, value in enumerate(rows_out):
            red_ref[k, span] = value
        return 0

    lax.fori_loop(0, rows // TILE, factor, 0)


def sweep_kernel(core_ref, res_ref, spec_ref, coup_ref, inv_ref, y_ref, keep_ref, send_ref):
    planes, fields, rows, _ = spec_ref.shape
    last = planes - 1
    tiles = rows // TILE // 2
    core = core_ref[0]

    for target_ref, side in ((keep_ref, core), (send_ref, 1 - core)):

        def step(t, _, target_ref=target_ref, side=side):
            span = pl.ds(pl.multiple_of((side * tiles + t) * TILE, TILE), TILE)
            place = pl.ds(pl.multiple_of(t * TILE, TILE), TILE)
            coup = [coup_ref[i, span] for i in range(planes)]
            inv = [inv_ref[i, span] for i in range(last)]
            ratio = [coup[i] * inv[i] for i in range(last)]
            for f in range(fields):
                value = []
                for i in range(last):
                    right = -(res_ref[i, f, span] + spec_ref[i, f, span])
                    if i:
                        right = right - coup[i] * value[-1]
                    value.append(right * inv[i])
                y = value[-1]
                y_last = y
                y_ref[last - 1, f, span] = y
                for i in range(last - 2, -1, -1):
                    y = value[i] - ratio[i] * y
                    y_ref[i, f, span] = y
                right = -(res_ref[last, f, span] + spec_ref[last, f, span])
                target_ref[f, place] = y
                target_ref[fields + f, place] = right - coup[last] * y_last
            return 0

        lax.fori_loop(0, tiles, step, 0)


def merge_kernel(core_ref, keep_ref, got_ref, pair_ref, link_ref, edge_ref, inner_ref, out_ref):
    fields = inner_ref.shape[0]
    rows = inner_ref.shape[1]
    lower_core = core_ref[0] == 0

    def step(t, _):
        span = pl.ds(pl.multiple_of(t * TILE, TILE), TILE)
        inv, sep_a, first_a, lower_b = (pair_ref[k, span] for k in range(4))
        scale, lower, upper = (link_ref[k, span] for k in range(3))
        edge = edge_ref[0, span]
        for f in range(fields):
            keep_y, got_y = keep_ref[f, span], got_ref[f, span]
            keep_own, got_own = keep_ref[fields + f, span], got_ref[fields + f, span]
            y_a = jnp.where(lower_core, keep_y, got_y)
            y_b = jnp.where(lower_core, got_y, keep_y)
            own_a = jnp.where(lower_core, keep_own, got_own)
            own_b = jnp.where(lower_core, got_own, keep_own)
            inner = inv * (own_a - sep_a * y_b)
            inner_ref[f, span] = inner
            for k, x in (
                (f, scale * (own_b - lower_b * inner)),
                (fields + f, edge * (y_a - first_a * inner)),
            ):
                out_ref[2 * t, k] = x[0:4]
                out_ref[2 * t + 1, k] = x[4:8]
        for k, x in ((2 * fields, lower), (2 * fields + 1, upper)):
            out_ref[2 * t, k] = x[0:4]
            out_ref[2 * t + 1, k] = x[4:8]
        return 0

    lax.fori_loop(0, rows // TILE, step, 0)


def reduced_kernel(rhs_ref, out_ref):
    count = rhs_ref.shape[0]
    fields = out_ref.shape[1] // 2
    ratio = []
    values = []
    for p in range(count):
        lower, upper = rhs_ref[p, 2 * fields], rhs_ref[p, 2 * fields + 1]
        more = p + 1 < count
        inv = 1.0 / (1.0 - lower * ratio[-1]) if p else jnp.ones_like(lower)
        ratio.append(upper * inv)
        row = []
        for f in range(fields):
            right = rhs_ref[p, f]
            if more:
                right = right - rhs_ref[p + 1, fields + f]
            if p:
                right = right - lower * values[-1][f]
            row.append(right * inv)
        values.append(row)
    solved = values[-1]
    for p in range(count - 1, -1, -1):
        if p < count - 1:
            solved = [values[p][f] - ratio[p] * solved[f] for f in range(fields)]
        for f in range(fields):
            out_ref[p, fields + f] = solved[f]
            if p < count - 1:
                out_ref[p + 1, f] = solved[f]
    for f in range(fields):
        out_ref[0, f] = jnp.zeros_like(solved[f])


def expand_kernel(core_ref, solved_ref, inner_ref, pair_ref, keep_ref, send_ref):
    fields, rows, _ = inner_ref.shape
    lower_core = core_ref[0] == 0

    def step(t, _):
        span = pl.ds(pl.multiple_of(t * TILE, TILE), TILE)
        v, w = pair_ref[4, span], pair_ref[5, span]
        for f in range(fields):
            prev = jnp.concatenate([solved_ref[2 * t, f], solved_ref[2 * t + 1, f]], axis=0)
            own = jnp.concatenate(
                [solved_ref[2 * t, fields + f], solved_ref[2 * t + 1, fields + f]], axis=0
            )
            inner = inner_ref[f, span] - v * prev - w * own
            keep_ref[f, span] = jnp.where(lower_core, prev, inner)
            keep_ref[fields + f, span] = jnp.where(lower_core, inner, own)
            send_ref[f, span] = jnp.where(lower_core, inner, prev)
            send_ref[fields + f, span] = jnp.where(lower_core, own, inner)
        return 0

    lax.fori_loop(0, rows // TILE, step, 0)


def finish_kernel(core_ref, state_ref, v_ref, w_ref, y_ref, keep_ref, got_ref, out_ref):
    fields, planes, rows = state_ref.shape[1:4]
    last = planes - 1
    tiles = rows // TILE // 2
    core = core_ref[0]

    for source_ref, side in ((keep_ref, core), (got_ref, 1 - core)):

        def step(t, _, source_ref=source_ref, side=side):
            span = pl.ds(pl.multiple_of((side * tiles + t) * TILE, TILE), TILE)
            place = pl.ds(pl.multiple_of(t * TILE, TILE), TILE)
            v = [v_ref[i, span] for i in range(last)]
            w = [w_ref[i, span] for i in range(last)]
            for f in range(fields):
                prev, own = source_ref[f, place], source_ref[fields + f, place]
                for i in range(last):
                    delta = y_ref[i, f, span] - v[i] * prev - w[i] * own
                    out_ref[0, f, i, span] = state_ref[0, f, i, span] + delta
                out_ref[0, f, last, span] = state_ref[0, f, last, span] + own
            return 0

        lax.fori_loop(0, tiles, step, 0)


def exchange(x, axis, groups=None):
    return lax.all_to_all(x, axis, 0, 0, tiled=True, axis_index_groups=groups)


def body(flow_state, thinc_flags):
    own = flow_state[0]
    planes, rows, lanes = own.shape[1:]
    instances = lax.axis_size("inst")
    ax_count = lax.axis_size("ax")
    circ_count = lax.axis_size("circ")
    chips = ax_count // 2
    half = rows // 2
    piece = half // chips
    grid = (rows, lanes)
    weights = spectral_weights(instances)

    core = lax.axis_index("ax") % 2
    core_op = jnp.reshape(core, (1,)).astype(jnp.int32)
    swap = [(i, i ^ 1) for i in range(ax_count)]
    groups = [list(range(c, ax_count, 2)) for c in range(2)]

    def partner(x):
        return lax.ppermute(x, "ax", swap)

    def neighbour(x, by):
        moves = [(i, i + 2 * by) for i in range(ax_count) if 0 <= i + 2 * by < ax_count]
        return lax.ppermute(x, "ax", moves)

    flags = (thinc_flags[0] > 0).astype(jnp.float32)
    edge_flags = jnp.broadcast_to(flags[None, :, 0:1, None], (1, planes, 4, lanes))
    edges = jnp.concatenate([own[:, :, 0:2], own[:, :, rows - 2 : rows]], axis=2)
    edges = jnp.concatenate([edges, edge_flags], axis=0)
    halo = lax.ppermute(
        edges, "circ", [(i, (i + 1) % circ_count) for i in range(circ_count)]
    )
    flag_cells = jnp.broadcast_to(flags[:, :, None], (planes, rows, lanes))

    block = exchange(jnp.swapaxes(own, 0, 1), "inst")
    block, halo = lax.optimization_barrier((block, halo))
    (spec,) = call(
        functools.partial(spectral_kernel, weights), [block.shape], block, flops=block.size * 9
    )
    spec = exchange(spec, "inst")

    res, coup, inv, v, w, coefs = call(
        flux_kernel,
        [
            (planes, FIELDS) + grid,
            (planes,) + grid,
            (planes - 1,) + grid,
            (planes - 1,) + grid,
            (planes - 1,) + grid,
            (COEFS,) + grid,
        ],
        flow_state,
        halo,
        flag_cells,
        flops=own.size * 60,
    )
    mine = lax.dynamic_slice_in_dim(coefs, core * half, half, axis=1)
    other = partner(lax.dynamic_slice_in_dim(coefs, (1 - core) * half, half, axis=1))
    lower_a, diag_a, sep_a, v_a, w_a = jnp.where(core == 0, mine, other)
    lower_b, diag_b, sep_b, v_b, w_b = jnp.where(core == 0, other, mine)
    pair_inv = 1.0 / (diag_a - sep_a * v_b)
    pair_v = pair_inv * lower_a
    pair_w = -(pair_inv * sep_a * w_b)
    pair = jnp.stack([pair_inv, sep_a, w_a, lower_b, pair_v, pair_w])
    ends = neighbour(jnp.stack([v_a - w_a * pair_v, -(w_a * pair_w)]), -1)
    scale = 1.0 / (diag_b - lower_b * pair_w - sep_b * ends[0])
    link = jnp.stack([scale, -(lower_b * pair_v) * scale, -(sep_b * ends[1]) * scale])
    edge = neighbour((sep_b * scale)[None], 1)

    y, keep, send = call(
        sweep_kernel,
        [(planes - 1, FIELDS) + grid, (2 * FIELDS, half, lanes), (2 * FIELDS, half, lanes)],
        core_op,
        res,
        spec,
        coup,
        inv,
        flops=spec.size * 8,
    )
    inner, rhs = call(
        merge_kernel,
        [(FIELDS, half, lanes), (chips, 2 * FIELDS + 2, piece, lanes)],
        core_op,
        keep,
        partner(send),
        pair,
        link,
        edge,
        flops=send.size * 4,
    )
    rhs = exchange(rhs, "ax", groups)
    (solved,) = call(
        reduced_kernel, [(chips, 2 * FIELDS, piece, lanes)], rhs, flops=rhs.size * 8
    )
    solved = exchange(solved, "ax", groups)
    keep, send = call(
        expand_kernel,
        [(2 * FIELDS, half, lanes)] * 2,
        core_op,
        solved,
        inner,
        pair,
        flops=send.size * 4,
    )
    (out,) = call(
        finish_kernel,
        [flow_state.shape],
        core_op,
        flow_state,
        v,
        w,
        y,
        keep,
        partner(send),
        flops=own.size * 5,
    )
    return out


def solution(mesh):
    return jax.shard_map(
        body,
        mesh=mesh,
        in_specs=(P("inst", None, "ax", "circ", None), P("inst", "ax", "circ")),
        out_specs=P("inst", None, "ax", "circ", None),
        check_vma=False,
    )
```

```python
import functools
import math

import jax
import jax.numpy as jnp
from jax import lax
from jax.experimental import pallas as pl
from jax.experimental.pallas import tpu as pltpu
from jax.sharding import PartitionSpec as P


G_LIQ = 4.4
P_LIQ = 6.0
G_GAS = 1.4
BETA = 1.6
EPSA = 0.1
ALPHA = 4.0
DIAG0 = 0.016
OMEGA = 1.0
NU_T = 0.25

FIELDS = 7
COEFS = 5
TILE = 8


VMEM = pl.BlockSpec(memory_space=pltpu.VMEM)


def spectral_weights(count):
    table = []
    for k in range(count):
        if k == 0:
            first, second = 0.0, -(count * count + 2) / 12.0
        else:
            sign = 1.0 if k % 2 == 0 else -1.0
            angle = math.pi * k / count
            first = 0.5 * sign * math.cos(angle) / math.sin(angle)
            second = -sign / (2.0 * math.sin(angle) ** 2)
        table.append(OMEGA * first - NU_T * OMEGA * OMEGA * second)
    return table


def core_index():
    return lax.rem(lax.axis_index("ax"), 2)


def call(kernel, outs, *operands, flops=0, scratch=()):
    outs = [jax.ShapeDtypeStruct(shape, jnp.float32) for shape in outs]
    total = sum(x.size * 4 for x in operands) + sum(x.size * 4 for x in outs)
    run = pl.pallas_call(
        kernel,
        out_shape=outs,
        in_specs=[VMEM] * len(operands),
        out_specs=[VMEM] * len(outs),
        scratch_shapes=[pltpu.VMEM(x, jnp.float32) for x in scratch],
        compiler_params=pltpu.CompilerParams(
            vmem_limit_bytes=total + sum(math.prod(x) * 4 for x in scratch) + (2 << 20)
        ),
        cost_estimate=pl.CostEstimate(flops=flops, bytes_accessed=total, transcendentals=0),
    )
    return list(run(*operands))


def slots(count):
    steps = [(dy, dx) for dy in range(count // 2) for dx in range(2)]
    return steps


def route(dy, dx, count):
    ring = count // 2
    return [(i, 2 * ((i // 2 + dy) % ring) + ((i % 2) ^ dx)) for i in range(count)]


def pick_kernel(count, state_ref, flag_ref, *refs):
    outs, edge_ref, sems = refs[:count], refs[count], refs[count + 1]
    fields, planes, rows = state_ref.shape[1:4]
    index = lax.axis_index("inst")
    ring = count // 2
    places = [
        2 * lax.rem(index // 2 + dy, ring) + lax.rem(lax.rem(index, 2) + dx, 2)
        for dy, dx in slots(count)
    ]
    copies = [
        pltpu.make_async_copy(state_ref.at[0, :, place], out, sems.at[k])
        for k, (place, out) in enumerate(zip(places, outs))
    ]
    for copy in copies:
        copy.start()
    flags = (flag_ref[0] > 0).astype(jnp.float32)
    for i in range(planes):
        edge_ref[i, fields] = jnp.broadcast_to(flags[i : i + 1, 0:1], edge_ref.shape[2:])
    for copy, place, out in zip(copies, places, outs):
        copy.wait()
        for f in range(fields):
            edge_ref[place, f] = jnp.concatenate(
                [out[f, 0:2], out[f, rows - 2 : rows]], axis=0
            )


def pick(state, flags, count):
    _, fields, planes, rows, lanes = state.shape
    shapes = [(fields, rows, lanes)] * count + [(planes, fields + 1, 4, lanes)]
    return pl.pallas_call(
        functools.partial(pick_kernel, count),
        out_shape=[jax.ShapeDtypeStruct(x, jnp.float32) for x in shapes],
        in_specs=[pl.BlockSpec(memory_space=pltpu.HBM), VMEM],
        out_specs=[VMEM] * len(shapes),
        scratch_shapes=[pltpu.SemaphoreType.DMA((count,))],
        compiler_params=pltpu.CompilerParams(vmem_limit_bytes=state.size * 4 + (3 << 20)),
        cost_estimate=pl.CostEstimate(flops=0, bytes_accessed=state.size * 8, transcendentals=0),
    )(state, flags)


def mixing(count, parity):
    weights = spectral_weights(count)
    table = []
    for shift in (0, 1 - 2 * parity, 2 * parity - 1):
        g = [weights[(2 * a + shift) % count] for a in range(4)]
        table += [0.5 * (g[0] + g[2]), 0.5 * (g[1] + g[3])]
        table += [0.5 * (g[0] - g[2]), 0.5 * (g[1] - g[3])]
    return table


def spectral_kernel(*refs):
    count = len(refs) // 2
    ins, outs = refs[:count], refs[count:]
    fields, rows, _ = ins[0].shape
    tiles = rows // TILE
    first = lax.rem(lax.axis_index("inst"), 2) == 0
    mix = [
        jnp.where(first, jnp.float32(a), jnp.float32(b))
        for a, b in zip(mixing(count, 0), mixing(count, 1))
    ]

    def step(index, _):
        f = index // tiles
        span = pl.ds(pl.multiple_of((index % tiles) * TILE, TILE), TILE)
        parts = []
        for dx in range(2):
            u = [ins[2 * dy + dx][f, span] for dy in range(4)]
            parts.append((u[0] + u[2], u[1] + u[3], u[0] - u[2], u[1] - u[3]))
        for ex in range(2):
            even, odd, even_next, odd_next = 0.0, 0.0, 0.0, 0.0
            for dx in range(2):
                kind = 0 if ex == dx else (1 if ex else 2)
                e0, e1, o0, o1 = mix[4 * kind : 4 * kind + 4]
                s0, s1, d0, d1 = parts[dx]
                even = even + (e0 * s0 + e1 * s1)
                odd = odd + (o0 * d0 + o1 * d1)
                even_next = even_next + (e1 * s0 + e0 * s1)
                odd_next = odd_next + (o1 * d0 - o0 * d1)
            outs[ex][f, span] = even + odd
            outs[4 + ex][f, span] = even - odd
            outs[2 + ex][f, span] = even_next + odd_next
            outs[6 + ex][f, span] = even_next - odd_next
        return 0

    lax.fori_loop(0, fields * tiles, step, 0)


def primitives(cells):
    density = cells[0] + cells[1]
    inverse = 1.0 / density
    vel_ax = cells[2] * inverse
    vel_circ = cells[3] * inverse
    vel_rad = cells[4] * inverse
    fraction = cells[6]
    gamma_term = fraction / (G_LIQ - 1.0) + (1.0 - fraction) / (G_GAS - 1.0)
    stiff_term = fraction * (G_LIQ * P_LIQ / (G_LIQ - 1.0))
    kinetic = 0.5 * density * (vel_ax * vel_ax + vel_circ * vel_circ + vel_rad * vel_rad)
    gamma_inv = 1.0 / gamma_term
    pressure = (cells[5] - kinetic - stiff_term) * gamma_inv
    sound_speed = jnp.sqrt(((1.0 + gamma_inv) * pressure + stiff_term * gamma_inv) * inverse)
    return vel_ax, vel_circ, pressure, sound_speed


def sharpen(lower_val, centre, upper_val, offset):
    average = 0.5 * (lower_val + upper_val)
    difference = upper_val - lower_val
    steepness = 2.0 * (centre - average) / (jnp.abs(difference) + EPSA)
    return average + 0.5 * difference * jnp.tanh(BETA * (steepness + offset))


def flux_kernel(
    state_ref, halo_ref, flag_ref, res_ref, coup_ref, inv_ref, v_ref, w_ref, keep_ref, send_ref
):
    planes = state_ref.shape[2]
    rows = state_ref.shape[3]
    last = planes - 1

    def plane(i, _):
        cells = []
        for f in range(FIELDS):
            edge = halo_ref[i, f]
            cells.append(
                jnp.concatenate(
                    [state_ref[0, f, i], edge[0:2], edge[0:2], edge[2:4], edge[2:4]], axis=0
                )
            )
        edge = halo_ref[i, FIELDS]
        flags = jnp.concatenate([flag_ref[i], edge, edge], axis=0)
        total = rows + TILE

        def below(x, by=1):
            return pltpu.roll(x, by, 0)

        def above(x):
            return pltpu.roll(x, total - 1, 0)

        vel_ax, vel_circ, pressure, sound = primitives(cells)
        coup_ref[i] = -ALPHA * (jnp.abs(vel_ax) + sound)[:rows]
        wave = jnp.abs(vel_circ) + sound
        half_speed = 0.5 * jnp.maximum(below(wave), wave)
        fraction = cells[6]
        back1 = below(fraction)
        sharp_left = sharpen(below(fraction, 2), back1, fraction, 1.0)
        sharp_right = sharpen(back1, fraction, above(fraction), -1.0)
        flagged = flags > 0.5
        frac_left = jnp.where(flagged, sharp_left, back1)
        frac_right = jnp.where(flagged, sharp_right, fraction)
        for f in range(FIELDS):
            if f < 6:
                flux = cells[f] * vel_circ
                if f == 3:
                    flux = flux + pressure
                elif f == 5:
                    flux = flux + pressure * vel_circ
                mean = 0.5 * (below(flux) + flux)
                jump = cells[f] - below(cells[f])
            else:
                mean = 0.5 * (frac_left * below(vel_circ) + frac_right * vel_circ)
                jump = frac_right - frac_left
            face = mean - half_speed * jump
            res_ref[i, f] = (above(face) - face)[:rows]
        return 0

    lax.fori_loop(0, planes, plane, 0)

    core = core_index()
    tiles = rows // TILE // 2
    for target_ref, side in ((keep_ref, core), (send_ref, 1 - core)):

        def factor(t, _, target_ref=target_ref, side=side):
            span = pl.ds(pl.multiple_of((side * tiles + t) * TILE, TILE), TILE)
            place = pl.ds(pl.multiple_of(t * TILE, TILE), TILE)
            coup = [coup_ref[i, span] for i in range(planes)]
            inv, ratio, v = [], [], []
            for i in range(last):
                pivot = DIAG0 - 2.0 * coup[i]
                if i:
                    pivot = pivot - coup[i] * ratio[-1]
                inv.append(1.0 / pivot)
                ratio.append(coup[i] * inv[-1])
                v.append(inv[-1] if i == 0 else -(ratio[-1] * v[-1]))
                inv_ref[i, span] = inv[-1]
            v_next, w_next = v[-1], inv[-1]
            v_last, w_last = v_next * coup[0], w_next * coup[last - 1]
            for i in range(last - 1, -1, -1):
                if i < last - 1:
                    v_next = v[i] - ratio[i] * v_next
                    w_next = -(ratio[i] * w_next)
                v_first, w_first = v_next * coup[0], w_next * coup[last - 1]
                v_ref[i, span] = v_first
                w_ref[i, span] = w_first
            sep = coup[last]
            target_ref[0, place] = -(sep * v_last)
            target_ref[1, place] = DIAG0 - 2.0 * sep - sep * w_last
            target_ref[2, place] = sep
            target_ref[3, place] = v_first
            target_ref[4, place] = w_first
            return 0

        lax.fori_loop(0, tiles, factor, 0)


def pair_kernel(keep_ref, got_ref, pair_ref, raw_ref, ends_ref):
    lower_core = core_index() == 0
    lower_a, diag_a, sep_a, v_a, w_a = (
        jnp.where(lower_core, keep_ref[k], got_ref[k]) for k in range(COEFS)
    )
    lower_b, diag_b, sep_b, v_b, w_b = (
        jnp.where(lower_core, got_ref[k], keep_ref[k]) for k in range(COEFS)
    )
    inv = 1.0 / (diag_a - sep_a * v_b)
    v = inv * lower_a
    w = -(inv * sep_a * w_b)
    for k, x in enumerate((inv, sep_a, w_a, lower_b, v, w)):
        pair_ref[k] = x
    raw_ref[0] = diag_b - lower_b * w
    raw_ref[1] = -(lower_b * v)
    raw_ref[2] = sep_b
    ends_ref[0] = v_a - w_a * v
    ends_ref[1] = -(w_a * w)


def link_kernel(raw_ref, ends_ref, link_ref, edge_ref):
    sep = raw_ref[2]
    scale = 1.0 / (raw_ref[0] - sep * ends_ref[0])
    link_ref[0] = scale
    link_ref[1] = raw_ref[1] * scale
    link_ref[2] = -(sep * ends_ref[1]) * scale
    edge_ref[0] = sep * scale


def sweep_kernel(res_ref, coup_ref, inv_ref, *refs):
    count = len(refs) - 4
    specs = refs[:count]
    y_ref, keep_ref, send_ref, right_ref = refs[count:]
    planes, fields, rows, _ = res_ref.shape
    last = planes - 1
    tiles = rows // TILE // 2
    core = core_index()
    index = lax.axis_index("inst")
    ring = count // 2
    places = [
        2 * lax.rem(index // 2 + ring - dy, ring) + lax.rem(lax.rem(index, 2) + dx, 2)
        for dy, dx in slots(count)
    ]

    for target_ref, side in ((keep_ref, core), (send_ref, 1 - core)):

        def step(t, _, target_ref=target_ref, side=side):
            span = pl.ds(pl.multiple_of((side * tiles + t) * TILE, TILE), TILE)
            place = pl.ds(pl.multiple_of(t * TILE, TILE), TILE)
            for f in range(fields):
                for i, spec_ref in zip(places, specs):
                    right_ref[f, i] = -(res_ref[i, f, span] + spec_ref[f, span])
            coup = [coup_ref[i, span] for i in range(planes)]
            inv = [inv_ref[i, span] for i in range(last)]
            ratio = [coup[i] * inv[i] for i in range(last)]
            for f in range(fields):
                value = []
                for i in range(last):
                    right = right_ref[f, i]
                    if i:
                        right = right - coup[i] * value[-1]
                    value.append(right * inv[i])
                y = value[-1]
                y_last = y
                y_ref[last - 1, f, span] = y
                for i in range(last - 2, -1, -1):
                    y = value[i] - ratio[i] * y
                    y_ref[i, f, span] = y
                target_ref[f, place] = y
                target_ref[fields + f, place] = right_ref[f, last] - coup[last] * y_last
            return 0

        lax.fori_loop(0, tiles, step, 0)


def merge_kernel(keep_ref, got_ref, pair_ref, link_ref, edge_ref, inner_ref, out_ref):
    fields = inner_ref.shape[0]
    rows = inner_ref.shape[1]
    lower_core = core_index() == 0

    def step(t, _):
        span = pl.ds(pl.multiple_of(t * TILE, TILE), TILE)
        inv, sep_a, first_a, lower_b = (pair_ref[k, span] for k in range(4))
        scale, lower, upper = (link_ref[k, span] for k in range(3))
        edge = edge_ref[0, span]
        for f in range(fields):
            keep_y, got_y = keep_ref[f, span], got_ref[f, span]
            keep_own, got_own = keep_ref[fields + f, span], got_ref[fields + f, span]
            y_a = jnp.where(lower_core, keep_y, got_y)
            y_b = jnp.where(lower_core, got_y, keep_y)
            own_a = jnp.where(lower_core, keep_own, got_own)
            own_b = jnp.where(lower_core, got_own, keep_own)
            inner = inv * (own_a - sep_a * y_b)
            inner_ref[f, span] = inner
            for k, x in (
                (f, scale * (own_b - lower_b * inner)),
                (fields + f, edge * (y_a - first_a * inner)),
            ):
                out_ref[2 * t, k] = x[0:4]
                out_ref[2 * t + 1, k] = x[4:8]
        for k, x in ((2 * fields, lower), (2 * fields + 1, upper)):
            out_ref[2 * t, k] = x[0:4]
            out_ref[2 * t + 1, k] = x[4:8]
        return 0

    lax.fori_loop(0, rows // TILE, step, 0)


def reduced_kernel(rhs_ref, out_ref):
    count = rhs_ref.shape[0]
    fields = out_ref.shape[1] // 2
    ratio = []
    values = []
    for p in range(count):
        lower, upper = rhs_ref[p, 2 * fields], rhs_ref[p, 2 * fields + 1]
        more = p + 1 < count
        inv = 1.0 / (1.0 - lower * ratio[-1]) if p else jnp.ones_like(lower)
        ratio.append(upper * inv)
        row = []
        for f in range(fields):
            right = rhs_ref[p, f]
            if more:
                right = right - rhs_ref[p + 1, fields + f]
            if p:
                right = right - lower * values[-1][f]
            row.append(right * inv)
        values.append(row)
    solved = values[-1]
    for p in range(count - 1, -1, -1):
        if p < count - 1:
            solved = [values[p][f] - ratio[p] * solved[f] for f in range(fields)]
        for f in range(fields):
            out_ref[p, fields + f] = solved[f]
            if p < count - 1:
                out_ref[p + 1, f] = solved[f]
    for f in range(fields):
        out_ref[0, f] = jnp.zeros_like(solved[f])


def expand_kernel(solved_ref, inner_ref, pair_ref, keep_ref, send_ref):
    fields, rows, _ = inner_ref.shape
    lower_core = core_index() == 0

    def step(t, _):
        span = pl.ds(pl.multiple_of(t * TILE, TILE), TILE)
        v, w = pair_ref[4, span], pair_ref[5, span]
        for f in range(fields):
            prev = jnp.concatenate([solved_ref[2 * t, f], solved_ref[2 * t + 1, f]], axis=0)
            own = jnp.concatenate(
                [solved_ref[2 * t, fields + f], solved_ref[2 * t + 1, fields + f]], axis=0
            )
            inner = inner_ref[f, span] - v * prev - w * own
            keep_ref[f, span] = jnp.where(lower_core, prev, inner)
            keep_ref[fields + f, span] = jnp.where(lower_core, inner, own)
            send_ref[f, span] = jnp.where(lower_core, inner, prev)
            send_ref[fields + f, span] = jnp.where(lower_core, own, inner)
        return 0

    lax.fori_loop(0, rows // TILE, step, 0)


def finish_kernel(state_ref, v_ref, w_ref, y_ref, keep_ref, got_ref, out_ref):
    fields, planes, rows = state_ref.shape[1:4]
    last = planes - 1
    tiles = rows // TILE // 2
    core = core_index()

    for source_ref, side in ((keep_ref, core), (got_ref, 1 - core)):

        def step(t, _, source_ref=source_ref, side=side):
            span = pl.ds(pl.multiple_of((side * tiles + t) * TILE, TILE), TILE)
            place = pl.ds(pl.multiple_of(t * TILE, TILE), TILE)
            v = [v_ref[i, span] for i in range(last)]
            w = [w_ref[i, span] for i in range(last)]
            for f in range(fields):
                prev, own = source_ref[f, place], source_ref[fields + f, place]
                for i in range(last):
                    delta = y_ref[i, f, span] - v[i] * prev - w[i] * own
                    out_ref[0, f, i, span] = state_ref[0, f, i, span] + delta
                out_ref[0, f, last, span] = state_ref[0, f, last, span] + own
            return 0

        lax.fori_loop(0, tiles, step, 0)


def flux_parts(state, halo, flag_cells):
    fields, planes, rows, lanes = state.shape[1:]
    grid = (rows, lanes)
    return call(
        flux_kernel,
        [
            (planes, fields) + grid,
            (planes,) + grid,
            (planes - 1,) + grid,
            (planes - 1,) + grid,
            (planes - 1,) + grid,
            (COEFS, rows // 2, lanes),
            (COEFS, rows // 2, lanes),
        ],
        state,
        halo,
        flag_cells,
        flops=state.size * 60,
    )


def exchange(x, axis, groups=None):
    return lax.all_to_all(x, axis, 0, 0, tiled=True, axis_index_groups=groups)


def body(flow_state, thinc_flags):
    own = flow_state[0]
    planes, rows, lanes = own.shape[1:]
    instances = lax.axis_size("inst")
    ax_count = lax.axis_size("ax")
    circ_count = lax.axis_size("circ")
    chips = ax_count // 2
    half = rows // 2
    piece = half // chips
    grid = (rows, lanes)

    swap = [(i, i ^ 1) for i in range(ax_count)]
    groups = [list(range(c, ax_count, 2)) for c in range(2)]

    def partner(x):
        return lax.ppermute(x, "ax", swap)

    def neighbour(x, by):
        moves = [(i, i + 2 * by) for i in range(ax_count) if 0 <= i + 2 * by < ax_count]
        return lax.ppermute(x, "ax", moves)

    steps = slots(instances)
    blocks = list(pick(flow_state, thinc_flags, instances))
    edges = blocks.pop()
    halo = lax.ppermute(
        edges, "circ", [(i, (i + 1) % circ_count) for i in range(circ_count)]
    )
    order = sorted(range(1, instances), key=lambda k: -min(steps[k][0], 4 - steps[k][0]))
    for k in order:
        blocks[k] = lax.ppermute(blocks[k], "inst", route(*steps[k], instances))
    flags = (thinc_flags[0] > 0).astype(jnp.float32)
    flag_cells = jnp.broadcast_to(flags[:, :, None], (planes, rows, lanes))

    res, coup, inv, v, w, keep, send = flux_parts(flow_state, halo, flag_cells)

    thin = (half, lanes)
    pair, raw, ends = call(
        pair_kernel, [(6,) + thin, (3,) + thin, (2,) + thin], keep, partner(send)
    )
    link, edge = call(link_kernel, [(3,) + thin, (1,) + thin], raw, neighbour(ends, -1))
    edge = neighbour(edge, 1)
    blocks, res, link, edge = lax.optimization_barrier((blocks, res, link, edge))
    specs = call(spectral_kernel, [blocks[0].shape] * instances, *blocks, flops=own.size * 9)
    for k in order:
        specs[k] = lax.ppermute(specs[k], "inst", route(*steps[k], instances))
    y, keep, send = call(
        sweep_kernel,
        [(planes - 1, FIELDS) + grid, (2 * FIELDS, half, lanes), (2 * FIELDS, half, lanes)],
        res,
        coup,
        inv,
        *specs,
        flops=own.size * 8,
        scratch=[(FIELDS, planes, TILE, lanes)],
    )
    inner, rhs = call(
        merge_kernel,
        [(FIELDS, half, lanes), (chips, 2 * FIELDS + 2, piece, lanes)],
        keep,
        partner(send),
        pair,
        link,
        edge,
        flops=send.size * 4,
    )
    rhs = exchange(rhs, "ax", groups)
    (solved,) = call(
        reduced_kernel, [(chips, 2 * FIELDS, piece, lanes)], rhs, flops=rhs.size * 8
    )
    solved = exchange(solved, "ax", groups)
    keep, send = call(
        expand_kernel,
        [(2 * FIELDS, half, lanes)] * 2,
        solved,
        inner,
        pair,
        flops=send.size * 4,
    )
    (out,) = call(
        finish_kernel,
        [flow_state.shape],
        flow_state,
        v,
        w,
        y,
        keep,
        partner(send),
        flops=own.size * 5,
    )
    return out


def solution(mesh):
    return jax.shard_map(
        body,
        mesh=mesh,
        in_specs=(P("inst", None, "ax", "circ", None), P("inst", "ax", "circ")),
        out_specs=P("inst", None, "ax", "circ", None),
        check_vma=False,
    )
```

```python
import functools
import math

import jax
import jax.numpy as jnp
from jax import lax
from jax.experimental import pallas as pl
from jax.experimental.pallas import tpu as pltpu
from jax.sharding import PartitionSpec as P


G_LIQ = 4.4
P_LIQ = 6.0
G_GAS = 1.4
BETA = 1.6
EPSA = 0.1
ALPHA = 4.0
DIAG0 = 0.016
OMEGA = 1.0
NU_T = 0.25

FIELDS = 7
ORDER = (5, 4, 3, 7, 2, 6, 1)
COEFS = 5
TILE = 8


VMEM = pl.BlockSpec(memory_space=pltpu.VMEM)


def spectral_weights(count):
    table = []
    for k in range(count):
        if k == 0:
            first, second = 0.0, -(count * count + 2) / 12.0
        else:
            sign = 1.0 if k % 2 == 0 else -1.0
            angle = math.pi * k / count
            first = 0.5 * sign * math.cos(angle) / math.sin(angle)
            second = -sign / (2.0 * math.sin(angle) ** 2)
        table.append(OMEGA * first - NU_T * OMEGA * OMEGA * second)
    return table


def core_index():
    return lax.rem(lax.axis_index("ax"), 2)


def call(kernel, outs, *operands, flops=0, scratch=()):
    outs = [jax.ShapeDtypeStruct(shape, jnp.float32) for shape in outs]
    total = sum(x.size * 4 for x in operands) + sum(x.size * 4 for x in outs)
    run = pl.pallas_call(
        kernel,
        out_shape=outs,
        in_specs=[VMEM] * len(operands),
        out_specs=[VMEM] * len(outs),
        scratch_shapes=[pltpu.VMEM(x, jnp.float32) for x in scratch],
        compiler_params=pltpu.CompilerParams(
            vmem_limit_bytes=total + sum(math.prod(x) * 4 for x in scratch) + (2 << 20)
        ),
        cost_estimate=pl.CostEstimate(flops=flops, bytes_accessed=total, transcendentals=0),
    )
    return list(run(*operands))


def slots(count):
    steps = [(dy, dx) for dy in range(count // 2) for dx in range(2)]
    return steps


def route(dy, dx, count):
    ring = count // 2
    return [(i, 2 * ((i // 2 + dy) % ring) + ((i % 2) ^ dx)) for i in range(count)]


def pick_kernel(count, state_ref, flag_ref, *refs):
    outs = refs[:count]
    edge_ref, held_ref, sems = refs[count:]
    fields, planes, rows = state_ref.shape[1:4]
    index = lax.axis_index("inst")
    ring = count // 2
    places = [
        2 * lax.rem(index // 2 + dy, ring) + lax.rem(lax.rem(index, 2) + dx, 2)
        for dy, dx in slots(count)
    ]
    copies = [
        pltpu.make_async_copy(state_ref.at[0, :, place], out, sems.at[k])
        for k, (place, out) in enumerate(zip(places, outs))
    ]
    for copy in copies:
        copy.start()
    flag_copy = pltpu.make_async_copy(flag_ref, held_ref, sems.at[count])
    flag_copy.start()
    flag_copy.wait()
    flags = (held_ref[0] > 0).astype(jnp.float32)
    for i in range(planes):
        edge_ref[i, fields] = jnp.broadcast_to(flags[i : i + 1, 0:1], edge_ref.shape[2:])
    for copy, place, out in zip(copies, places, outs):
        copy.wait()
        for f in range(fields):
            edge_ref[place, f] = jnp.concatenate(
                [out[f, 0:2], out[f, rows - 2 : rows]], axis=0
            )


def pick(state, flags, count):
    _, fields, planes, rows, lanes = state.shape
    shapes = [(fields, rows, lanes)] * count + [(planes, fields + 1, 4, lanes)]
    return pl.pallas_call(
        functools.partial(pick_kernel, count),
        out_shape=[jax.ShapeDtypeStruct(x, jnp.float32) for x in shapes],
        in_specs=[pl.BlockSpec(memory_space=pltpu.HBM)] * 2,
        out_specs=[VMEM] * len(shapes),
        scratch_shapes=[
            pltpu.VMEM(flags.shape, flags.dtype),
            pltpu.SemaphoreType.DMA((count + 1,)),
        ],
        compiler_params=pltpu.CompilerParams(vmem_limit_bytes=state.size * 4 + (3 << 20)),
        cost_estimate=pl.CostEstimate(flops=0, bytes_accessed=state.size * 8, transcendentals=0),
    )(*(pltpu.with_memory_space_constraint(x, pltpu.HBM) for x in (state, flags)))


def mixing(count, parity):
    weights = spectral_weights(count)
    table = []
    for shift in (0, 1 - 2 * parity, 2 * parity - 1):
        g = [weights[(2 * a + shift) % count] for a in range(4)]
        table += [0.5 * (g[0] + g[2]), 0.5 * (g[1] + g[3])]
        table += [0.5 * (g[0] - g[2]), 0.5 * (g[1] - g[3])]
    return table


def spectral_kernel(*refs):
    count = len(refs) // 2
    ins, outs = refs[:count], refs[count:]
    fields, rows, _ = ins[0].shape
    tiles = rows // TILE
    first = lax.rem(lax.axis_index("inst"), 2) == 0
    mix = [
        jnp.where(first, jnp.float32(a), jnp.float32(b))
        for a, b in zip(mixing(count, 0), mixing(count, 1))
    ]

    def step(index, _):
        f = index // tiles
        span = pl.ds(pl.multiple_of((index % tiles) * TILE, TILE), TILE)
        parts = []
        for dx in range(2):
            u = [ins[2 * dy + dx][f, span] for dy in range(4)]
            parts.append((u[0] + u[2], u[1] + u[3], u[0] - u[2], u[1] - u[3]))
        for ex in range(2):
            even, odd, even_next, odd_next = 0.0, 0.0, 0.0, 0.0
            for dx in range(2):
                kind = 0 if ex == dx else (1 if ex else 2)
                e0, e1, o0, o1 = mix[4 * kind : 4 * kind + 4]
                s0, s1, d0, d1 = parts[dx]
                even = even + (e0 * s0 + e1 * s1)
                odd = odd + (o0 * d0 + o1 * d1)
                even_next = even_next + (e1 * s0 + e0 * s1)
                odd_next = odd_next + (o1 * d0 - o0 * d1)
            outs[ex][f, span] = even + odd
            outs[4 + ex][f, span] = even - odd
            outs[2 + ex][f, span] = even_next + odd_next
            outs[6 + ex][f, span] = even_next - odd_next
        return 0

    lax.fori_loop(0, fields * tiles, step, 0)


def primitives(cells):
    density = cells[0] + cells[1]
    inverse = 1.0 / density
    vel_ax = cells[2] * inverse
    vel_circ = cells[3] * inverse
    vel_rad = cells[4] * inverse
    fraction = cells[6]
    gamma_term = fraction / (G_LIQ - 1.0) + (1.0 - fraction) / (G_GAS - 1.0)
    stiff_term = fraction * (G_LIQ * P_LIQ / (G_LIQ - 1.0))
    kinetic = 0.5 * density * (vel_ax * vel_ax + vel_circ * vel_circ + vel_rad * vel_rad)
    gamma_inv = 1.0 / gamma_term
    pressure = (cells[5] - kinetic - stiff_term) * gamma_inv
    sound_speed = jnp.sqrt(((1.0 + gamma_inv) * pressure + stiff_term * gamma_inv) * inverse)
    return vel_ax, vel_circ, pressure, sound_speed


def sharpen(lower_val, centre, upper_val, offset):
    average = 0.5 * (lower_val + upper_val)
    difference = upper_val - lower_val
    steepness = 2.0 * (centre - average) / (jnp.abs(difference) + EPSA)
    return average + 0.5 * difference * jnp.tanh(BETA * (steepness + offset))


def flux_kernel(
    state_ref, halo_ref, flag_ref, res_ref, coup_ref, inv_ref, v_ref, w_ref, keep_ref, send_ref
):
    planes = state_ref.shape[2]
    rows = state_ref.shape[3]
    last = planes - 1

    def plane(i, _):
        cells = []
        for f in range(FIELDS):
            edge = halo_ref[i, f]
            cells.append(
                jnp.concatenate(
                    [state_ref[0, f, i], edge[0:2], edge[0:2], edge[2:4], edge[2:4]], axis=0
                )
            )
        edge = halo_ref[i, FIELDS]
        flags = jnp.concatenate([flag_ref[i], edge, edge], axis=0)
        total = rows + TILE

        def below(x, by=1):
            return pltpu.roll(x, by, 0)

        def above(x):
            return pltpu.roll(x, total - 1, 0)

        vel_ax, vel_circ, pressure, sound = primitives(cells)
        coup_ref[i] = -ALPHA * (jnp.abs(vel_ax) + sound)[:rows]
        wave = jnp.abs(vel_circ) + sound
        half_speed = 0.5 * jnp.maximum(below(wave), wave)
        fraction = cells[6]
        back1 = below(fraction)
        sharp_left = sharpen(below(fraction, 2), back1, fraction, 1.0)
        sharp_right = sharpen(back1, fraction, above(fraction), -1.0)
        flagged = flags > 0.5
        frac_left = jnp.where(flagged, sharp_left, back1)
        frac_right = jnp.where(flagged, sharp_right, fraction)
        for f in range(FIELDS):
            if f < 6:
                flux = cells[f] * vel_circ
                if f == 3:
                    flux = flux + pressure
                elif f == 5:
                    flux = flux + pressure * vel_circ
                mean = 0.5 * (below(flux) + flux)
                jump = cells[f] - below(cells[f])
            else:
                mean = 0.5 * (frac_left * below(vel_circ) + frac_right * vel_circ)
                jump = frac_right - frac_left
            face = mean - half_speed * jump
            res_ref[i, f] = (above(face) - face)[:rows]
        return 0

    lax.fori_loop(0, planes, plane, 0)

    core = core_index()
    tiles = rows // TILE // 2
    for target_ref, side in ((keep_ref, core), (send_ref, 1 - core)):

        def factor(t, _, target_ref=target_ref, side=side):
            span = pl.ds(pl.multiple_of((side * tiles + t) * TILE, TILE), TILE)
            place = pl.ds(pl.multiple_of(t * TILE, TILE), TILE)
            coup = [coup_ref[i, span] for i in range(planes)]
            inv, ratio, v = [], [], []
            for i in range(last):
                pivot = DIAG0 - 2.0 * coup[i]
                if i:
                    pivot = pivot - coup[i] * ratio[-1]
                inv.append(1.0 / pivot)
                ratio.append(coup[i] * inv[-1])
                v.append(inv[-1] if i == 0 else -(ratio[-1] * v[-1]))
                inv_ref[i, span] = inv[-1]
            v_next, w_next = v[-1], inv[-1]
            v_last, w_last = v_next * coup[0], w_next * coup[last - 1]
            for i in range(last - 1, -1, -1):
                if i < last - 1:
                    v_next = v[i] - ratio[i] * v_next
                    w_next = -(ratio[i] * w_next)
                v_first, w_first = v_next * coup[0], w_next * coup[last - 1]
                v_ref[i, span] = v_first
                w_ref[i, span] = w_first
            sep = coup[last]
            target_ref[0, place] = -(sep * v_last)
            target_ref[1, place] = DIAG0 - 2.0 * sep - sep * w_last
            target_ref[2, place] = sep
            target_ref[3, place] = v_first
            target_ref[4, place] = w_first
            return 0

        lax.fori_loop(0, tiles, factor, 0)


def pair_kernel(keep_ref, got_ref, pair_ref, raw_ref, ends_ref):
    lower_core = core_index() == 0
    lower_a, diag_a, sep_a, v_a, w_a = (
        jnp.where(lower_core, keep_ref[k], got_ref[k]) for k in range(COEFS)
    )
    lower_b, diag_b, sep_b, v_b, w_b = (
        jnp.where(lower_core, got_ref[k], keep_ref[k]) for k in range(COEFS)
    )
    inv = 1.0 / (diag_a - sep_a * v_b)
    v = inv * lower_a
    w = -(inv * sep_a * w_b)
    for k, x in enumerate((inv, sep_a, w_a, lower_b, v, w)):
        pair_ref[k] = x
    raw_ref[0] = diag_b - lower_b * w
    raw_ref[1] = -(lower_b * v)
    raw_ref[2] = sep_b
    ends_ref[0] = v_a - w_a * v
    ends_ref[1] = -(w_a * w)


def link_kernel(raw_ref, ends_ref, link_ref, edge_ref):
    sep = raw_ref[2]
    scale = 1.0 / (raw_ref[0] - sep * ends_ref[0])
    link_ref[0] = scale
    link_ref[1] = raw_ref[1] * scale
    link_ref[2] = -(sep * ends_ref[1]) * scale
    edge_ref[0] = sep * scale


def half_of(mine):
    core = core_index()
    return core if mine else 1 - core


def sweep_kernel(mine, res_ref, coup_ref, inv_ref, *refs):
    count = len(refs) - 3
    specs = refs[:count]
    y_ref, target_ref, right_ref = refs[count:]
    planes, fields, rows, _ = res_ref.shape
    last = planes - 1
    tiles = rows // TILE // 2
    side = half_of(mine)
    index = lax.axis_index("inst")
    ring = count // 2
    places = [
        2 * lax.rem(index // 2 + ring - dy, ring) + lax.rem(lax.rem(index, 2) + dx, 2)
        for dy, dx in slots(count)
    ]

    def step(t, _):
        span = pl.ds(pl.multiple_of((side * tiles + t) * TILE, TILE), TILE)
        place = pl.ds(pl.multiple_of(t * TILE, TILE), TILE)
        for f in range(fields):
            for i, spec_ref in zip(places, specs):
                right_ref[f, i] = -(res_ref[i, f, span] + spec_ref[f, span])
        coup = [coup_ref[i, span] for i in range(planes)]
        inv = [inv_ref[i, span] for i in range(last)]
        ratio = [coup[i] * inv[i] for i in range(last)]
        for f in range(fields):
            value = []
            for i in range(last):
                right = right_ref[f, i]
                if i:
                    right = right - coup[i] * value[-1]
                value.append(right * inv[i])
            y = value[-1]
            y_last = y
            y_ref[last - 1, f, place] = y
            for i in range(last - 2, -1, -1):
                y = value[i] - ratio[i] * y
                y_ref[i, f, place] = y
            target_ref[f, place] = y
            target_ref[fields + f, place] = right_ref[f, last] - coup[last] * y_last
        return 0

    lax.fori_loop(0, tiles, step, 0)


def merge_kernel(keep_ref, got_ref, pair_ref, link_ref, edge_ref, inner_ref, out_ref):
    fields = inner_ref.shape[0]
    rows = inner_ref.shape[1]
    lower_core = core_index() == 0

    def step(t, _):
        span = pl.ds(pl.multiple_of(t * TILE, TILE), TILE)
        inv, sep_a, first_a, lower_b = (pair_ref[k, span] for k in range(4))
        scale, lower, upper = (link_ref[k, span] for k in range(3))
        edge = edge_ref[0, span]
        for f in range(fields):
            keep_y, got_y = keep_ref[f, span], got_ref[f, span]
            keep_own, got_own = keep_ref[fields + f, span], got_ref[fields + f, span]
            y_a = jnp.where(lower_core, keep_y, got_y)
            y_b = jnp.where(lower_core, got_y, keep_y)
            own_a = jnp.where(lower_core, keep_own, got_own)
            own_b = jnp.where(lower_core, got_own, keep_own)
            inner = inv * (own_a - sep_a * y_b)
            inner_ref[f, span] = inner
            for k, x in (
                (f, scale * (own_b - lower_b * inner)),
                (fields + f, edge * (y_a - first_a * inner)),
            ):
                out_ref[2 * t, k] = x[0:4]
                out_ref[2 * t + 1, k] = x[4:8]
        for k, x in ((2 * fields, lower), (2 * fields + 1, upper)):
            out_ref[2 * t, k] = x[0:4]
            out_ref[2 * t + 1, k] = x[4:8]
        return 0

    lax.fori_loop(0, rows // TILE, step, 0)


def reduced_kernel(rhs_ref, out_ref):
    count = rhs_ref.shape[0]
    fields = out_ref.shape[1] // 2
    ratio = []
    values = []
    for p in range(count):
        lower, upper = rhs_ref[p, 2 * fields], rhs_ref[p, 2 * fields + 1]
        more = p + 1 < count
        inv = 1.0 / (1.0 - lower * ratio[-1]) if p else jnp.ones_like(lower)
        ratio.append(upper * inv)
        row = []
        for f in range(fields):
            right = rhs_ref[p, f]
            if more:
                right = right - rhs_ref[p + 1, fields + f]
            if p:
                right = right - lower * values[-1][f]
            row.append(right * inv)
        values.append(row)
    solved = values[-1]
    for p in range(count - 1, -1, -1):
        if p < count - 1:
            solved = [values[p][f] - ratio[p] * solved[f] for f in range(fields)]
        for f in range(fields):
            out_ref[p, fields + f] = solved[f]
            if p < count - 1:
                out_ref[p + 1, f] = solved[f]
    for f in range(fields):
        out_ref[0, f] = jnp.zeros_like(solved[f])


def expand_kernel(solved_ref, inner_ref, pair_ref, keep_ref, send_ref):
    fields, rows, _ = inner_ref.shape
    lower_core = core_index() == 0

    def step(t, _):
        span = pl.ds(pl.multiple_of(t * TILE, TILE), TILE)
        v, w = pair_ref[4, span], pair_ref[5, span]
        for f in range(fields):
            prev = jnp.concatenate([solved_ref[2 * t, f], solved_ref[2 * t + 1, f]], axis=0)
            own = jnp.concatenate(
                [solved_ref[2 * t, fields + f], solved_ref[2 * t + 1, fields + f]], axis=0
            )
            inner = inner_ref[f, span] - v * prev - w * own
            keep_ref[f, span] = jnp.where(lower_core, prev, inner)
            keep_ref[fields + f, span] = jnp.where(lower_core, inner, own)
            send_ref[f, span] = jnp.where(lower_core, inner, prev)
            send_ref[fields + f, span] = jnp.where(lower_core, own, inner)
        return 0

    lax.fori_loop(0, rows // TILE, step, 0)


def finish_kernel(mine, state_ref, v_ref, w_ref, y_ref, ends_ref, *refs):
    out_ref, block_ref, sems = refs[-3:]
    fields, planes, rows = state_ref.shape[1:4]
    last = planes - 1
    tiles = rows // TILE // 2
    side = half_of(mine)
    copies = []
    for t in range(tiles):
        span = pl.ds(pl.multiple_of((side * tiles + t) * TILE, TILE), TILE)
        place = pl.ds(t * TILE, TILE)

        def field(f, _, span=span, place=place, t=t):
            prev, own = ends_ref[f, place], ends_ref[fields + f, place]
            for i in range(last):
                delta = y_ref[i, f, place] - v_ref[i, span] * prev - w_ref[i, span] * own
                block_ref[t, f, i] = state_ref[0, f, i, span] + delta
            block_ref[t, f, last] = state_ref[0, f, last, span] + own
            return 0

        lax.fori_loop(0, fields, field, 0)
        copy = pltpu.make_async_copy(
            block_ref.at[t], out_ref.at[0, :, :, span], sems.at[t]
        )
        copy.start()
        copies.append(copy)
    for copy in copies:
        copy.wait()


def finish(mine, state, v, w, y, ends, partial=None):
    fields, planes, rows, lanes = state.shape[1:]
    tiles = rows // TILE // 2
    hbm = pl.BlockSpec(memory_space=pltpu.HBM)
    operands = [state, v, w, y, ends]
    specs = [VMEM] * len(operands)
    aliases = {}
    if partial is not None:
        aliases = {len(operands): 0}
        operands.append(partial)
        specs.append(hbm)
    return pl.pallas_call(
        functools.partial(finish_kernel, mine),
        out_shape=jax.ShapeDtypeStruct(state.shape, jnp.float32),
        in_specs=specs,
        out_specs=hbm,
        scratch_shapes=[
            pltpu.VMEM((tiles, fields, planes, TILE, lanes), jnp.float32),
            pltpu.SemaphoreType.DMA((tiles,)),
        ],
        input_output_aliases=aliases,
        compiler_params=pltpu.CompilerParams(vmem_limit_bytes=state.size * 12),
        cost_estimate=pl.CostEstimate(
            flops=state.size * 2, bytes_accessed=state.size * 6, transcendentals=0
        ),
    )(*operands)


def flux_parts(state, halo, flag_cells):
    fields, planes, rows, lanes = state.shape[1:]
    grid = (rows, lanes)
    return call(
        flux_kernel,
        [
            (planes, fields) + grid,
            (planes,) + grid,
            (planes - 1,) + grid,
            (planes - 1,) + grid,
            (planes - 1,) + grid,
            (COEFS, rows // 2, lanes),
            (COEFS, rows // 2, lanes),
        ],
        state,
        halo,
        flag_cells,
        flops=state.size * 60,
    )


def exchange(x, axis, groups=None):
    return lax.all_to_all(x, axis, 0, 0, tiled=True, axis_index_groups=groups)


def body(flow_state, thinc_flags):
    own = flow_state[0]
    planes, rows, lanes = own.shape[1:]
    instances = lax.axis_size("inst")
    ax_count = lax.axis_size("ax")
    circ_count = lax.axis_size("circ")
    chips = ax_count // 2
    half = rows // 2
    piece = half // chips

    swap = [(i, i ^ 1) for i in range(ax_count)]
    groups = [list(range(c, ax_count, 2)) for c in range(2)]

    def partner(x):
        return lax.ppermute(x, "ax", swap)

    def neighbour(x, by):
        moves = [(i, i + 2 * by) for i in range(ax_count) if 0 <= i + 2 * by < ax_count]
        return lax.ppermute(x, "ax", moves)

    steps = slots(instances)
    blocks = list(pick(flow_state, thinc_flags, instances))
    edges = blocks.pop()
    halo = lax.ppermute(
        edges, "circ", [(i, (i + 1) % circ_count) for i in range(circ_count)]
    )
    order = ORDER
    for k in order:
        blocks[k] = lax.ppermute(blocks[k], "inst", route(*steps[k], instances))
    flags = (thinc_flags[0] > 0).astype(jnp.float32)
    flag_cells = jnp.broadcast_to(flags[:, :, None], (planes, rows, lanes))

    res, coup, inv, v, w, keep, send = flux_parts(flow_state, halo, flag_cells)

    thin = (half, lanes)
    pair, raw, ends = call(
        pair_kernel, [(6,) + thin, (3,) + thin, (2,) + thin], keep, partner(send)
    )
    blocks, res, ends = lax.optimization_barrier((blocks, res, ends))
    specs = call(spectral_kernel, [blocks[0].shape] * instances, *blocks, flops=own.size * 9)
    for k in order:
        specs[k] = lax.ppermute(specs[k], "inst", route(*steps[k], instances))
    ends = neighbour(ends, -1)
    link, edge = call(link_kernel, [(3,) + thin, (1,) + thin], raw, ends)
    edge = neighbour(edge, 1)
    shapes = [(planes - 1, FIELDS, half, lanes), (2 * FIELDS, half, lanes)]
    parts = []
    for mine in (False, True):
        parts.append(
            call(
                functools.partial(sweep_kernel, mine),
                shapes,
                res,
                coup,
                inv,
                *specs,
                flops=own.size * 4,
                scratch=[(FIELDS, planes, TILE, lanes)],
            )
        )
    (y_other, send), (y_mine, keep) = parts
    inner, rhs = call(
        merge_kernel,
        [(FIELDS, half, lanes), (chips, 2 * FIELDS + 2, piece, lanes)],
        keep,
        partner(send),
        pair,
        link,
        edge,
        flops=send.size * 4,
    )
    rhs = exchange(rhs, "ax", groups)
    (solved,) = call(
        reduced_kernel, [(chips, 2 * FIELDS, piece, lanes)], rhs, flops=rhs.size * 8
    )
    solved = exchange(solved, "ax", groups)
    keep, send = call(
        expand_kernel,
        [(2 * FIELDS, half, lanes)] * 2,
        solved,
        inner,
        pair,
        flops=send.size * 4,
    )
    got = partner(send)
    out = finish(True, flow_state, v, w, y_mine, keep)
    return finish(False, flow_state, v, w, y_other, got, out)


def solution(mesh):
    return jax.shard_map(
        body,
        mesh=mesh,
        in_specs=(P("inst", None, "ax", "circ", None), P("inst", "ax", "circ")),
        out_specs=P("inst", None, "ax", "circ", None),
        check_vma=False,
    )
```

```python
import functools
import math

import jax
import jax.numpy as jnp
from jax import lax
from jax.experimental import pallas as pl
from jax.experimental.pallas import tpu as pltpu
from jax.sharding import PartitionSpec as P


G_LIQ = 4.4
P_LIQ = 6.0
G_GAS = 1.4
BETA = 1.6
EPSA = 0.1
ALPHA = 4.0
DIAG0 = 0.016
OMEGA = 1.0
NU_T = 0.25

FIELDS = 7
ORDER = (5, 4, 3, 7, 2, 6, 1)
EDGES = 2 * FIELDS + 3
COEFS = 5
TILE = 8


VMEM = pl.BlockSpec(memory_space=pltpu.VMEM)


def spectral_weights(count):
    table = []
    for k in range(count):
        if k == 0:
            first, second = 0.0, -(count * count + 2) / 12.0
        else:
            sign = 1.0 if k % 2 == 0 else -1.0
            angle = math.pi * k / count
            first = 0.5 * sign * math.cos(angle) / math.sin(angle)
            second = -sign / (2.0 * math.sin(angle) ** 2)
        table.append(OMEGA * first - NU_T * OMEGA * OMEGA * second)
    return table


def core_index():
    return lax.rem(lax.axis_index("ax"), 2)


def call(kernel, outs, *operands, flops=0, scratch=()):
    outs = [jax.ShapeDtypeStruct(shape, jnp.float32) for shape in outs]
    total = sum(x.size * 4 for x in operands) + sum(x.size * 4 for x in outs)
    run = pl.pallas_call(
        kernel,
        out_shape=outs,
        in_specs=[VMEM] * len(operands),
        out_specs=[VMEM] * len(outs),
        scratch_shapes=[pltpu.VMEM(x, jnp.float32) for x in scratch],
        compiler_params=pltpu.CompilerParams(
            vmem_limit_bytes=total + sum(math.prod(x) * 4 for x in scratch) + (2 << 20)
        ),
        cost_estimate=pl.CostEstimate(flops=flops, bytes_accessed=total, transcendentals=0),
    )
    return list(run(*operands))


def slots(count):
    steps = [(dy, dx) for dy in range(count // 2) for dx in range(2)]
    return steps


def route(dy, dx, count):
    ring = count // 2
    return [(i, 2 * ((i // 2 + dy) % ring) + ((i % 2) ^ dx)) for i in range(count)]


def pick_kernel(count, state_ref, flag_ref, *refs):
    outs = refs[:count]
    edge_ref, held_ref, sems = refs[count:]
    fields, _, rows = state_ref.shape[1:4]
    index = lax.axis_index("inst")
    ring = count // 2
    places = [
        2 * lax.rem(index // 2 + dy, ring) + lax.rem(lax.rem(index, 2) + dx, 2)
        for dy, dx in slots(count)
    ]
    copies = [
        pltpu.make_async_copy(state_ref.at[0, :, place], out, sems.at[k])
        for k, (place, out) in enumerate(zip(places, outs))
    ]
    for copy in copies:
        copy.start()
    flag_copy = pltpu.make_async_copy(flag_ref, held_ref, sems.at[count])
    flag_copy.start()
    flag_copy.wait()
    flags = (held_ref[0] > 0).astype(jnp.float32)
    edge_ref[EDGES - 1] = jnp.broadcast_to(flags[:, 0:1], edge_ref.shape[1:])
    for copy, place, out in zip(copies, places, outs):
        copy.wait()
        row = pl.ds(place, 1)
        for f in range(fields):
            edge_ref[f, row] = out[f, 0:1]
            edge_ref[fields + f, row] = out[f, rows - 1 : rows]
        edge_ref[2 * fields, row] = out[fields - 1, 1:2]
        edge_ref[2 * fields + 1, row] = out[fields - 1, rows - 2 : rows - 1]


def pick(state, flags, count):
    _, fields, planes, rows, lanes = state.shape
    shapes = [(fields, rows, lanes)] * count + [(EDGES, planes, lanes)]
    return pl.pallas_call(
        functools.partial(pick_kernel, count),
        out_shape=[jax.ShapeDtypeStruct(x, jnp.float32) for x in shapes],
        in_specs=[pl.BlockSpec(memory_space=pltpu.HBM)] * 2,
        out_specs=[VMEM] * len(shapes),
        scratch_shapes=[
            pltpu.VMEM(flags.shape, flags.dtype),
            pltpu.SemaphoreType.DMA((count + 1,)),
        ],
        compiler_params=pltpu.CompilerParams(vmem_limit_bytes=state.size * 4 + (3 << 20)),
        cost_estimate=pl.CostEstimate(flops=0, bytes_accessed=state.size * 8, transcendentals=0),
    )(*(pltpu.with_memory_space_constraint(x, pltpu.HBM) for x in (state, flags)))


def mixing(count, parity):
    weights = spectral_weights(count)
    table = []
    for shift in (0, 1 - 2 * parity, 2 * parity - 1):
        g = [weights[(2 * a + shift) % count] for a in range(4)]
        table += [0.5 * (g[0] + g[2]), 0.5 * (g[1] + g[3])]
        table += [0.5 * (g[0] - g[2]), 0.5 * (g[1] - g[3])]
    return table


def spectral_kernel(*refs):
    count = len(refs) // 2
    ins, outs = refs[:count], refs[count:]
    fields, rows, _ = ins[0].shape
    tiles = rows // TILE
    first = lax.rem(lax.axis_index("inst"), 2) == 0
    mix = [
        jnp.where(first, jnp.float32(a), jnp.float32(b))
        for a, b in zip(mixing(count, 0), mixing(count, 1))
    ]

    def step(index, _):
        f = index // tiles
        span = pl.ds(pl.multiple_of((index % tiles) * TILE, TILE), TILE)
        parts = []
        for dx in range(2):
            u = [ins[2 * dy + dx][f, span] for dy in range(4)]
            parts.append((u[0] + u[2], u[1] + u[3], u[0] - u[2], u[1] - u[3]))
        for ex in range(2):
            even, odd, even_next, odd_next = 0.0, 0.0, 0.0, 0.0
            for dx in range(2):
                kind = 0 if ex == dx else (1 if ex else 2)
                e0, e1, o0, o1 = mix[4 * kind : 4 * kind + 4]
                s0, s1, d0, d1 = parts[dx]
                even = even + (e0 * s0 + e1 * s1)
                odd = odd + (o0 * d0 + o1 * d1)
                even_next = even_next + (e1 * s0 + e0 * s1)
                odd_next = odd_next + (o1 * d0 - o0 * d1)
            outs[ex][f, span] = even + odd
            outs[4 + ex][f, span] = even - odd
            outs[2 + ex][f, span] = even_next + odd_next
            outs[6 + ex][f, span] = even_next - odd_next
        return 0

    lax.fori_loop(0, fields * tiles, step, 0)


def primitives(cells):
    density = cells[0] + cells[1]
    inverse = 1.0 / density
    vel_ax = cells[2] * inverse
    vel_circ = cells[3] * inverse
    vel_rad = cells[4] * inverse
    fraction = cells[6]
    gamma_term = fraction / (G_LIQ - 1.0) + (1.0 - fraction) / (G_GAS - 1.0)
    stiff_term = fraction * (G_LIQ * P_LIQ / (G_LIQ - 1.0))
    kinetic = 0.5 * density * (vel_ax * vel_ax + vel_circ * vel_circ + vel_rad * vel_rad)
    gamma_inv = 1.0 / gamma_term
    pressure = (cells[5] - kinetic - stiff_term) * gamma_inv
    sound_speed = jnp.sqrt(((1.0 + gamma_inv) * pressure + stiff_term * gamma_inv) * inverse)
    return vel_ax, vel_circ, pressure, sound_speed


def sharpen(lower_val, centre, upper_val, offset):
    average = 0.5 * (lower_val + upper_val)
    difference = upper_val - lower_val
    steepness = 2.0 * (centre - average) / (jnp.abs(difference) + EPSA)
    return average + 0.5 * difference * jnp.tanh(BETA * (steepness + offset))


def flux_kernel(
    state_ref, halo_ref, flag_ref, res_ref, coup_ref, inv_ref, v_ref, w_ref, keep_ref, send_ref
):
    planes = state_ref.shape[2]
    rows = state_ref.shape[3]
    last = planes - 1

    def plane(i, _):
        row = pl.ds(i, 1)
        quad = (TILE // 2, state_ref.shape[4])
        cells = []
        for f in range(FIELDS):
            upper, lower = halo_ref[f, row], halo_ref[FIELDS + f, row]
            if f < FIELDS - 1:
                edge = [jnp.broadcast_to(upper, quad), jnp.broadcast_to(lower, quad)]
            else:
                next_upper = halo_ref[2 * FIELDS, row]
                next_lower = halo_ref[2 * FIELDS + 1, row]
                edge = [upper] + [next_upper] * 3 + [next_lower] * 3 + [lower]
            cells.append(jnp.concatenate([state_ref[0, f, i]] + edge, axis=0))
        edge = jnp.broadcast_to(halo_ref[EDGES - 1, row], (TILE, state_ref.shape[4]))
        flags = jnp.concatenate([flag_ref[i], edge], axis=0)
        total = rows + TILE

        def below(x, by=1):
            return pltpu.roll(x, by, 0)

        def above(x):
            return pltpu.roll(x, total - 1, 0)

        vel_ax, vel_circ, pressure, sound = primitives(cells)
        coup_ref[i] = -ALPHA * (jnp.abs(vel_ax) + sound)[:rows]
        wave = jnp.abs(vel_circ) + sound
        half_speed = 0.5 * jnp.maximum(below(wave), wave)
        fraction = cells[6]
        back1 = below(fraction)
        sharp_left = sharpen(below(fraction, 2), back1, fraction, 1.0)
        sharp_right = sharpen(back1, fraction, above(fraction), -1.0)
        flagged = flags > 0.5
        frac_left = jnp.where(flagged, sharp_left, back1)
        frac_right = jnp.where(flagged, sharp_right, fraction)
        for f in range(FIELDS):
            if f < 6:
                flux = cells[f] * vel_circ
                if f == 3:
                    flux = flux + pressure
                elif f == 5:
                    flux = flux + pressure * vel_circ
                mean = 0.5 * (below(flux) + flux)
                jump = cells[f] - below(cells[f])
            else:
                mean = 0.5 * (frac_left * below(vel_circ) + frac_right * vel_circ)
                jump = frac_right - frac_left
            face = mean - half_speed * jump
            res_ref[i, f] = (above(face) - face)[:rows]
        return 0

    lax.fori_loop(0, planes, plane, 0)

    core = core_index()
    tiles = rows // TILE // 2
    for target_ref, side in ((keep_ref, core), (send_ref, 1 - core)):

        def factor(t, _, target_ref=target_ref, side=side):
            span = pl.ds(pl.multiple_of((side * tiles + t) * TILE, TILE), TILE)
            place = pl.ds(pl.multiple_of(t * TILE, TILE), TILE)
            coup = [coup_ref[i, span] for i in range(planes)]
            inv, ratio, v = [], [], []
            for i in range(last):
                pivot = DIAG0 - 2.0 * coup[i]
                if i:
                    pivot = pivot - coup[i] * ratio[-1]
                inv.append(1.0 / pivot)
                ratio.append(coup[i] * inv[-1])
                v.append(inv[-1] if i == 0 else -(ratio[-1] * v[-1]))
                inv_ref[i, span] = inv[-1]
            v_next, w_next = v[-1], inv[-1]
            v_last, w_last = v_next * coup[0], w_next * coup[last - 1]
            for i in range(last - 1, -1, -1):
                if i < last - 1:
                    v_next = v[i] - ratio[i] * v_next
                    w_next = -(ratio[i] * w_next)
                v_first, w_first = v_next * coup[0], w_next * coup[last - 1]
                v_ref[i, span] = v_first
                w_ref[i, span] = w_first
            sep = coup[last]
            target_ref[0, place] = -(sep * v_last)
            target_ref[1, place] = DIAG0 - 2.0 * sep - sep * w_last
            target_ref[2, place] = sep
            target_ref[3, place] = v_first
            target_ref[4, place] = w_first
            return 0

        lax.fori_loop(0, tiles, factor, 0)


def pair_kernel(keep_ref, got_ref, pair_ref, raw_ref, ends_ref):
    lower_core = core_index() == 0
    lower_a, diag_a, sep_a, v_a, w_a = (
        jnp.where(lower_core, keep_ref[k], got_ref[k]) for k in range(COEFS)
    )
    lower_b, diag_b, sep_b, v_b, w_b = (
        jnp.where(lower_core, got_ref[k], keep_ref[k]) for k in range(COEFS)
    )
    inv = 1.0 / (diag_a - sep_a * v_b)
    v = inv * lower_a
    w = -(inv * sep_a * w_b)
    for k, x in enumerate((inv, sep_a, w_a, lower_b, v, w)):
        pair_ref[k] = x
    raw_ref[0] = diag_b - lower_b * w
    raw_ref[1] = -(lower_b * v)
    raw_ref[2] = sep_b
    ends_ref[0] = v_a - w_a * v
    ends_ref[1] = -(w_a * w)


def link_kernel(raw_ref, ends_ref, link_ref, edge_ref):
    sep = raw_ref[2]
    scale = 1.0 / (raw_ref[0] - sep * ends_ref[0])
    link_ref[0] = scale
    link_ref[1] = raw_ref[1] * scale
    link_ref[2] = -(sep * ends_ref[1]) * scale
    edge_ref[0] = sep * scale


def join_kernel(link_ref, edge_ref, out_ref):
    for k in range(3):
        out_ref[k] = link_ref[k]
    out_ref[3] = edge_ref[0]


def half_of(mine):
    core = core_index()
    return core if mine else 1 - core


def sweep_kernel(mine, res_ref, coup_ref, inv_ref, *refs):
    count = len(refs) - 3
    specs = refs[:count]
    y_ref, target_ref, right_ref = refs[count:]
    planes, fields, rows, _ = res_ref.shape
    last = planes - 1
    tiles = rows // TILE // 2
    side = half_of(mine)
    index = lax.axis_index("inst")
    ring = count // 2
    places = [
        2 * lax.rem(index // 2 + ring - dy, ring) + lax.rem(lax.rem(index, 2) + dx, 2)
        for dy, dx in slots(count)
    ]

    def step(t, _):
        span = pl.ds(pl.multiple_of((side * tiles + t) * TILE, TILE), TILE)
        place = pl.ds(pl.multiple_of(t * TILE, TILE), TILE)
        for f in range(fields):
            for i, spec_ref in zip(places, specs):
                right_ref[f, i] = -(res_ref[i, f, span] + spec_ref[f, span])
        coup = [coup_ref[i, span] for i in range(planes)]
        inv = [inv_ref[i, span] for i in range(last)]
        ratio = [coup[i] * inv[i] for i in range(last)]
        for f in range(fields):
            value = []
            for i in range(last):
                right = right_ref[f, i]
                if i:
                    right = right - coup[i] * value[-1]
                value.append(right * inv[i])
            y = value[-1]
            y_last = y
            y_ref[last - 1, f, place] = y
            for i in range(last - 2, -1, -1):
                y = value[i] - ratio[i] * y
                y_ref[i, f, place] = y
            target_ref[f, place] = y
            target_ref[fields + f, place] = right_ref[f, last] - coup[last] * y_last
        return 0

    lax.fori_loop(0, tiles, step, 0)


def merge_kernel(keep_ref, got_ref, pair_ref, link_ref, inner_ref, out_ref):
    fields = inner_ref.shape[0]
    rows = inner_ref.shape[1]
    lower_core = core_index() == 0

    def step(t, _):
        span = pl.ds(pl.multiple_of(t * TILE, TILE), TILE)
        inv, sep_a, first_a, lower_b = (pair_ref[k, span] for k in range(4))
        scale, lower, upper, edge = (link_ref[k, span] for k in range(4))
        for f in range(fields):
            keep_y, got_y = keep_ref[f, span], got_ref[f, span]
            keep_own, got_own = keep_ref[fields + f, span], got_ref[fields + f, span]
            y_a = jnp.where(lower_core, keep_y, got_y)
            y_b = jnp.where(lower_core, got_y, keep_y)
            own_a = jnp.where(lower_core, keep_own, got_own)
            own_b = jnp.where(lower_core, got_own, keep_own)
            inner = inv * (own_a - sep_a * y_b)
            inner_ref[f, span] = inner
            for k, x in (
                (f, scale * (own_b - lower_b * inner)),
                (fields + f, edge * (y_a - first_a * inner)),
            ):
                out_ref[2 * t, k] = x[0:4]
                out_ref[2 * t + 1, k] = x[4:8]
        for k, x in ((2 * fields, lower), (2 * fields + 1, upper)):
            out_ref[2 * t, k] = x[0:4]
            out_ref[2 * t + 1, k] = x[4:8]
        return 0

    lax.fori_loop(0, rows // TILE, step, 0)


def reduced_kernel(rhs_ref, out_ref):
    count = rhs_ref.shape[0]
    fields = out_ref.shape[1] // 2
    ratio = []
    values = []
    for p in range(count):
        lower, upper = rhs_ref[p, 2 * fields], rhs_ref[p, 2 * fields + 1]
        more = p + 1 < count
        inv = 1.0 / (1.0 - lower * ratio[-1]) if p else jnp.ones_like(lower)
        ratio.append(upper * inv)
        row = []
        for f in range(fields):
            right = rhs_ref[p, f]
            if more:
                right = right - rhs_ref[p + 1, fields + f]
            if p:
                right = right - lower * values[-1][f]
            row.append(right * inv)
        values.append(row)
    solved = values[-1]
    for p in range(count - 1, -1, -1):
        if p < count - 1:
            solved = [values[p][f] - ratio[p] * solved[f] for f in range(fields)]
        for f in range(fields):
            out_ref[p, fields + f] = solved[f]
            if p < count - 1:
                out_ref[p + 1, f] = solved[f]
    for f in range(fields):
        out_ref[0, f] = jnp.zeros_like(solved[f])


def expand_kernel(solved_ref, inner_ref, pair_ref, keep_ref, send_ref):
    fields, rows, _ = inner_ref.shape
    lower_core = core_index() == 0

    def step(t, _):
        span = pl.ds(pl.multiple_of(t * TILE, TILE), TILE)
        v, w = pair_ref[4, span], pair_ref[5, span]
        for f in range(fields):
            prev = jnp.concatenate([solved_ref[2 * t, f], solved_ref[2 * t + 1, f]], axis=0)
            own = jnp.concatenate(
                [solved_ref[2 * t, fields + f], solved_ref[2 * t + 1, fields + f]], axis=0
            )
            inner = inner_ref[f, span] - v * prev - w * own
            keep_ref[f, span] = jnp.where(lower_core, prev, inner)
            keep_ref[fields + f, span] = jnp.where(lower_core, inner, own)
            send_ref[f, span] = jnp.where(lower_core, inner, prev)
            send_ref[fields + f, span] = jnp.where(lower_core, own, inner)
        return 0

    lax.fori_loop(0, rows // TILE, step, 0)


def finish_kernel(mine, state_ref, v_ref, w_ref, y_ref, ends_ref, *refs):
    out_ref, block_ref, sems = refs[-3:]
    fields, planes, rows = state_ref.shape[1:4]
    last = planes - 1
    tiles = rows // TILE // 2
    side = half_of(mine)
    copies = []
    for t in range(tiles):
        span = pl.ds(pl.multiple_of((side * tiles + t) * TILE, TILE), TILE)
        place = pl.ds(t * TILE, TILE)

        def field(f, _, span=span, place=place, t=t):
            prev, own = ends_ref[f, place], ends_ref[fields + f, place]
            for i in range(last):
                delta = y_ref[i, f, place] - v_ref[i, span] * prev - w_ref[i, span] * own
                block_ref[t, f, i] = state_ref[0, f, i, span] + delta
            block_ref[t, f, last] = state_ref[0, f, last, span] + own
            return 0

        lax.fori_loop(0, fields, field, 0)
        copy = pltpu.make_async_copy(
            block_ref.at[t], out_ref.at[0, :, :, span], sems.at[t]
        )
        copy.start()
        copies.append(copy)
    for copy in copies:
        copy.wait()


def finish(mine, state, v, w, y, ends, partial=None):
    fields, planes, rows, lanes = state.shape[1:]
    tiles = rows // TILE // 2
    hbm = pl.BlockSpec(memory_space=pltpu.HBM)
    operands = [state, v, w, y, ends]
    specs = [VMEM] * len(operands)
    aliases = {}
    if partial is not None:
        aliases = {len(operands): 0}
        operands.append(partial)
        specs.append(hbm)
    return pl.pallas_call(
        functools.partial(finish_kernel, mine),
        out_shape=jax.ShapeDtypeStruct(state.shape, jnp.float32),
        in_specs=specs,
        out_specs=hbm,
        scratch_shapes=[
            pltpu.VMEM((tiles, fields, planes, TILE, lanes), jnp.float32),
            pltpu.SemaphoreType.DMA((tiles,)),
        ],
        input_output_aliases=aliases,
        compiler_params=pltpu.CompilerParams(vmem_limit_bytes=state.size * 12),
        cost_estimate=pl.CostEstimate(
            flops=state.size * 2, bytes_accessed=state.size * 6, transcendentals=0
        ),
    )(*operands)


def flux_parts(state, halo, flag_cells):
    fields, planes, rows, lanes = state.shape[1:]
    grid = (rows, lanes)
    return call(
        flux_kernel,
        [
            (planes, fields) + grid,
            (planes,) + grid,
            (planes - 1,) + grid,
            (planes - 1,) + grid,
            (planes - 1,) + grid,
            (COEFS, rows // 2, lanes),
            (COEFS, rows // 2, lanes),
        ],
        state,
        halo,
        flag_cells,
        flops=state.size * 60,
    )


def exchange(x, axis, groups=None):
    return lax.all_to_all(x, axis, 0, 0, tiled=True, axis_index_groups=groups)


def body(flow_state, thinc_flags):
    own = flow_state[0]
    planes, rows, lanes = own.shape[1:]
    instances = lax.axis_size("inst")
    ax_count = lax.axis_size("ax")
    circ_count = lax.axis_size("circ")
    chips = ax_count // 2
    half = rows // 2
    piece = half // chips

    swap = [(i, i ^ 1) for i in range(ax_count)]
    groups = [list(range(c, ax_count, 2)) for c in range(2)]

    def partner(x):
        return lax.ppermute(x, "ax", swap)

    def neighbour(x, by):
        moves = [(i, i + 2 * by) for i in range(ax_count) if 0 <= i + 2 * by < ax_count]
        return lax.ppermute(x, "ax", moves)

    steps = slots(instances)
    blocks = list(pick(flow_state, thinc_flags, instances))
    edges = blocks.pop()
    halo = lax.ppermute(
        edges, "circ", [(i, (i + 1) % circ_count) for i in range(circ_count)]
    )
    order = ORDER
    for k in order:
        blocks[k] = lax.ppermute(blocks[k], "inst", route(*steps[k], instances))
    flags = (thinc_flags[0] > 0).astype(jnp.float32)
    flag_cells = jnp.broadcast_to(flags[:, :, None], (planes, rows, lanes))

    res, coup, inv, v, w, keep, send = flux_parts(flow_state, halo, flag_cells)

    thin = (half, lanes)
    pair, raw, ends = call(
        pair_kernel, [(6,) + thin, (3,) + thin, (2,) + thin], keep, partner(send)
    )
    blocks, res, ends = lax.optimization_barrier((blocks, res, ends))
    specs = call(spectral_kernel, [blocks[0].shape] * instances, *blocks, flops=own.size * 9)
    for k in order:
        specs[k] = lax.ppermute(specs[k], "inst", route(*steps[k], instances))
    ends = neighbour(ends, -1)
    link, edge = call(link_kernel, [(3,) + thin, (1,) + thin], raw, ends)
    edge = neighbour(edge, 1)
    (link,) = call(join_kernel, [(4,) + thin], link, edge)
    shapes = [(planes - 1, FIELDS, half, lanes), (2 * FIELDS, half, lanes)]
    parts = []
    for mine in (False, True):
        parts.append(
            call(
                functools.partial(sweep_kernel, mine),
                shapes,
                res,
                coup,
                inv,
                *specs,
                flops=own.size * 4,
                scratch=[(FIELDS, planes, TILE, lanes)],
            )
        )
    (y_other, send), (y_mine, keep) = parts
    inner, rhs = call(
        merge_kernel,
        [(FIELDS, half, lanes), (chips, 2 * FIELDS + 2, piece, lanes)],
        keep,
        partner(send),
        pair,
        link,
        flops=send.size * 4,
    )
    rhs = exchange(rhs, "ax", groups)
    (solved,) = call(
        reduced_kernel, [(chips, 2 * FIELDS, piece, lanes)], rhs, flops=rhs.size * 8
    )
    solved = exchange(solved, "ax", groups)
    keep, send = call(
        expand_kernel,
        [(2 * FIELDS, half, lanes)] * 2,
        solved,
        inner,
        pair,
        flops=send.size * 4,
    )
    got = partner(send)
    out = finish(True, flow_state, v, w, y_mine, keep)
    return finish(False, flow_state, v, w, y_other, got, out)


def solution(mesh):
    return jax.shard_map(
        body,
        mesh=mesh,
        in_specs=(P("inst", None, "ax", "circ", None), P("inst", "ax", "circ")),
        out_specs=P("inst", None, "ax", "circ", None),
        check_vma=False,
    )
```

```python
import functools
import math

import jax
import jax.numpy as jnp
from jax import lax
from jax.experimental import pallas as pl
from jax.experimental.pallas import tpu as pltpu
from jax.sharding import PartitionSpec as P


G_LIQ = 4.4
P_LIQ = 6.0
G_GAS = 1.4
BETA = 1.6
EPSA = 0.1
ALPHA = 4.0
DIAG0 = 0.016
OMEGA = 1.0
NU_T = 0.25

FIELDS = 7
ORDER = (4, 5, 3, 7, 1, 2, 6)
EDGES = 2 * FIELDS + 3
COEFS = 5
TILE = 8


VMEM = pl.BlockSpec(memory_space=pltpu.VMEM)


def spectral_weights(count):
    table = []
    for k in range(count):
        if k == 0:
            first, second = 0.0, -(count * count + 2) / 12.0
        else:
            sign = 1.0 if k % 2 == 0 else -1.0
            angle = math.pi * k / count
            first = 0.5 * sign * math.cos(angle) / math.sin(angle)
            second = -sign / (2.0 * math.sin(angle) ** 2)
        table.append(OMEGA * first - NU_T * OMEGA * OMEGA * second)
    return table


def core_index():
    return lax.rem(lax.axis_index("ax"), 2)


def call(kernel, outs, *operands, flops=0, scratch=()):
    outs = [jax.ShapeDtypeStruct(shape, jnp.float32) for shape in outs]
    total = sum(x.size * 4 for x in operands) + sum(x.size * 4 for x in outs)
    run = pl.pallas_call(
        kernel,
        out_shape=outs,
        in_specs=[VMEM] * len(operands),
        out_specs=[VMEM] * len(outs),
        scratch_shapes=[pltpu.VMEM(x, jnp.float32) for x in scratch],
        compiler_params=pltpu.CompilerParams(
            vmem_limit_bytes=total + sum(math.prod(x) * 4 for x in scratch) + (2 << 20)
        ),
        cost_estimate=pl.CostEstimate(flops=flops, bytes_accessed=total, transcendentals=0),
    )
    return list(run(*operands))


def slots(count):
    steps = [(dy, dx) for dy in range(count // 2) for dx in range(2)]
    return steps


def route(dy, dx, count):
    ring = count // 2
    return [(i, 2 * ((i // 2 + dy) % ring) + ((i % 2) ^ dx)) for i in range(count)]


def pick_kernel(count, state_ref, flag_ref, *refs):
    outs = refs[:count]
    edge_ref, held_ref, sems = refs[count:]
    fields, _, rows = state_ref.shape[1:4]
    index = lax.axis_index("inst")
    ring = count // 2
    places = [
        2 * lax.rem(index // 2 + dy, ring) + lax.rem(lax.rem(index, 2) + dx, 2)
        for dy, dx in slots(count)
    ]
    copies = [
        pltpu.make_async_copy(state_ref.at[0, :, place], out, sems.at[k])
        for k, (place, out) in enumerate(zip(places, outs))
    ]
    for copy in copies:
        copy.start()
    flag_copy = pltpu.make_async_copy(flag_ref, held_ref, sems.at[count])
    flag_copy.start()
    flag_copy.wait()
    flags = (held_ref[0] > 0).astype(jnp.float32)
    edge_ref[EDGES - 1] = jnp.broadcast_to(flags[:, 0:1], edge_ref.shape[1:])
    for copy, place, out in zip(copies, places, outs):
        copy.wait()
        row = pl.ds(place, 1)
        for f in range(fields):
            edge_ref[f, row] = out[f, 0:1]
            edge_ref[fields + f, row] = out[f, rows - 1 : rows]
        edge_ref[2 * fields, row] = out[fields - 1, 1:2]
        edge_ref[2 * fields + 1, row] = out[fields - 1, rows - 2 : rows - 1]


def pick(state, flags, count):
    _, fields, planes, rows, lanes = state.shape
    shapes = [(fields, rows, lanes)] * count + [(EDGES, planes, lanes)]
    return pl.pallas_call(
        functools.partial(pick_kernel, count),
        out_shape=[jax.ShapeDtypeStruct(x, jnp.float32) for x in shapes],
        in_specs=[pl.BlockSpec(memory_space=pltpu.HBM)] * 2,
        out_specs=[VMEM] * len(shapes),
        scratch_shapes=[
            pltpu.VMEM(flags.shape, flags.dtype),
            pltpu.SemaphoreType.DMA((count + 1,)),
        ],
        compiler_params=pltpu.CompilerParams(vmem_limit_bytes=state.size * 4 + (3 << 20)),
        cost_estimate=pl.CostEstimate(flops=0, bytes_accessed=state.size * 8, transcendentals=0),
    )(*(pltpu.with_memory_space_constraint(x, pltpu.HBM) for x in (state, flags)))


def mixing(count, parity):
    weights = spectral_weights(count)
    table = []
    for shift in (0, 1 - 2 * parity, 2 * parity - 1):
        g = [weights[(2 * a + shift) % count] for a in range(4)]
        table += [0.5 * (g[0] + g[2]), 0.5 * (g[1] + g[3])]
        table += [0.5 * (g[0] - g[2]), 0.5 * (g[1] - g[3])]
    return table


def spectral_kernel(*refs):
    count = len(refs) // 2
    ins, outs = refs[:count], refs[count:]
    fields, rows, _ = ins[0].shape
    tiles = rows // TILE
    first = lax.rem(lax.axis_index("inst"), 2) == 0
    mix = [
        jnp.where(first, jnp.float32(a), jnp.float32(b))
        for a, b in zip(mixing(count, 0), mixing(count, 1))
    ]

    def step(index, _):
        f = index // tiles
        span = pl.ds(pl.multiple_of((index % tiles) * TILE, TILE), TILE)
        parts = []
        for dx in range(2):
            u = [ins[2 * dy + dx][f, span] for dy in range(4)]
            parts.append((u[0] + u[2], u[1] + u[3], u[0] - u[2], u[1] - u[3]))
        for ex in range(2):
            even, odd, even_next, odd_next = 0.0, 0.0, 0.0, 0.0
            for dx in range(2):
                kind = 0 if ex == dx else (1 if ex else 2)
                e0, e1, o0, o1 = mix[4 * kind : 4 * kind + 4]
                s0, s1, d0, d1 = parts[dx]
                even = even + (e0 * s0 + e1 * s1)
                odd = odd + (o0 * d0 + o1 * d1)
                even_next = even_next + (e1 * s0 + e0 * s1)
                odd_next = odd_next + (o1 * d0 - o0 * d1)
            outs[ex][f, span] = even + odd
            outs[4 + ex][f, span] = even - odd
            outs[2 + ex][f, span] = even_next + odd_next
            outs[6 + ex][f, span] = even_next - odd_next
        return 0

    lax.fori_loop(0, fields * tiles, step, 0, unroll=4)


def primitives(cells):
    density = cells[0] + cells[1]
    inverse = 1.0 / density
    vel_ax = cells[2] * inverse
    vel_circ = cells[3] * inverse
    vel_rad = cells[4] * inverse
    fraction = cells[6]
    gamma_term = fraction / (G_LIQ - 1.0) + (1.0 - fraction) / (G_GAS - 1.0)
    stiff_term = fraction * (G_LIQ * P_LIQ / (G_LIQ - 1.0))
    kinetic = 0.5 * density * (vel_ax * vel_ax + vel_circ * vel_circ + vel_rad * vel_rad)
    gamma_inv = 1.0 / gamma_term
    pressure = (cells[5] - kinetic - stiff_term) * gamma_inv
    sound_speed = jnp.sqrt(((1.0 + gamma_inv) * pressure + stiff_term * gamma_inv) * inverse)
    return vel_ax, vel_circ, pressure, sound_speed


def sharpen(lower_val, centre, upper_val, offset):
    average = 0.5 * (lower_val + upper_val)
    difference = upper_val - lower_val
    steepness = 2.0 * (centre - average) / (jnp.abs(difference) + EPSA)
    return average + 0.5 * difference * jnp.tanh(BETA * (steepness + offset))


def flux_kernel(
    state_ref, halo_ref, flag_ref, res_ref, coup_ref, inv_ref, v_ref, w_ref, keep_ref, send_ref
):
    planes = state_ref.shape[2]
    rows = state_ref.shape[3]
    last = planes - 1

    def plane(i, _):
        row = pl.ds(i, 1)
        quad = (TILE // 2, state_ref.shape[4])
        cells = []
        for f in range(FIELDS):
            upper, lower = halo_ref[f, row], halo_ref[FIELDS + f, row]
            if f < FIELDS - 1:
                edge = [jnp.broadcast_to(upper, quad), jnp.broadcast_to(lower, quad)]
            else:
                next_upper = halo_ref[2 * FIELDS, row]
                next_lower = halo_ref[2 * FIELDS + 1, row]
                edge = [upper] + [next_upper] * 3 + [next_lower] * 3 + [lower]
            cells.append(jnp.concatenate([state_ref[0, f, i]] + edge, axis=0))
        edge = jnp.broadcast_to(halo_ref[EDGES - 1, row], (TILE, state_ref.shape[4]))
        flags = jnp.concatenate([flag_ref[i], edge], axis=0)
        total = rows + TILE

        def below(x, by=1):
            return pltpu.roll(x, by, 0)

        def above(x):
            return pltpu.roll(x, total - 1, 0)

        vel_ax, vel_circ, pressure, sound = primitives(cells)
        coup_ref[i] = -ALPHA * (jnp.abs(vel_ax) + sound)[:rows]
        wave = jnp.abs(vel_circ) + sound
        half_speed = 0.5 * jnp.maximum(below(wave), wave)
        fraction = cells[6]
        back1 = below(fraction)
        sharp_left = sharpen(below(fraction, 2), back1, fraction, 1.0)
        sharp_right = sharpen(back1, fraction, above(fraction), -1.0)
        flagged = flags > 0.5
        frac_left = jnp.where(flagged, sharp_left, back1)
        frac_right = jnp.where(flagged, sharp_right, fraction)
        for f in range(FIELDS):
            if f < 6:
                flux = cells[f] * vel_circ
                if f == 3:
                    flux = flux + pressure
                elif f == 5:
                    flux = flux + pressure * vel_circ
                mean = 0.5 * (below(flux) + flux)
                jump = cells[f] - below(cells[f])
            else:
                mean = 0.5 * (frac_left * below(vel_circ) + frac_right * vel_circ)
                jump = frac_right - frac_left
            face = mean - half_speed * jump
            res_ref[i, f] = (above(face) - face)[:rows]
        return 0

    lax.fori_loop(0, planes, plane, 0)

    core = core_index()
    tiles = rows // TILE // 2
    for target_ref, side in ((keep_ref, core), (send_ref, 1 - core)):

        def factor(t, _, target_ref=target_ref, side=side):
            span = pl.ds(pl.multiple_of((side * tiles + t) * TILE, TILE), TILE)
            place = pl.ds(pl.multiple_of(t * TILE, TILE), TILE)
            coup = [coup_ref[i, span] for i in range(planes)]
            inv, ratio, v = [], [], []
            for i in range(last):
                pivot = DIAG0 - 2.0 * coup[i]
                if i:
                    pivot = pivot - coup[i] * ratio[-1]
                inv.append(1.0 / pivot)
                ratio.append(coup[i] * inv[-1])
                v.append(inv[-1] if i == 0 else -(ratio[-1] * v[-1]))
                inv_ref[i, span] = inv[-1]
            v_next, w_next = v[-1], inv[-1]
            v_last, w_last = v_next * coup[0], w_next * coup[last - 1]
            for i in range(last - 1, -1, -1):
                if i < last - 1:
                    v_next = v[i] - ratio[i] * v_next
                    w_next = -(ratio[i] * w_next)
                v_first, w_first = v_next * coup[0], w_next * coup[last - 1]
                v_ref[i, span] = v_first
                w_ref[i, span] = w_first
            sep = coup[last]
            target_ref[0, place] = -(sep * v_last)
            target_ref[1, place] = DIAG0 - 2.0 * sep - sep * w_last
            target_ref[2, place] = sep
            target_ref[3, place] = v_first
            target_ref[4, place] = w_first
            return 0

        lax.fori_loop(0, tiles, factor, 0)


def pair_kernel(keep_ref, got_ref, pair_ref, raw_ref, ends_ref):
    lower_core = core_index() == 0
    lower_a, diag_a, sep_a, v_a, w_a = (
        jnp.where(lower_core, keep_ref[k], got_ref[k]) for k in range(COEFS)
    )
    lower_b, diag_b, sep_b, v_b, w_b = (
        jnp.where(lower_core, got_ref[k], keep_ref[k]) for k in range(COEFS)
    )
    inv = 1.0 / (diag_a - sep_a * v_b)
    v = inv * lower_a
    w = -(inv * sep_a * w_b)
    for k, x in enumerate((inv, sep_a, w_a, lower_b, v, w)):
        pair_ref[k] = x
    raw_ref[0] = diag_b - lower_b * w
    raw_ref[1] = -(lower_b * v)
    raw_ref[2] = sep_b
    ends_ref[0] = v_a - w_a * v
    ends_ref[1] = -(w_a * w)


def link_kernel(raw_ref, ends_ref, link_ref, edge_ref):
    sep = raw_ref[2]
    scale = 1.0 / (raw_ref[0] - sep * ends_ref[0])
    link_ref[0] = scale
    link_ref[1] = raw_ref[1] * scale
    link_ref[2] = -(sep * ends_ref[1]) * scale
    edge_ref[0] = sep * scale


def join_kernel(link_ref, edge_ref, out_ref):
    for k in range(3):
        out_ref[k] = link_ref[k]
    out_ref[3] = edge_ref[0]


def half_of(mine):
    core = core_index()
    return core if mine else 1 - core


def sweep_kernel(mine, res_ref, coup_ref, inv_ref, *refs):
    count = len(refs) - 3
    specs = refs[:count]
    y_ref, target_ref, right_ref = refs[count:]
    planes, fields, rows, _ = res_ref.shape
    last = planes - 1
    tiles = rows // TILE // 2
    side = half_of(mine)
    index = lax.axis_index("inst")
    ring = count // 2
    places = [
        2 * lax.rem(index // 2 + ring - dy, ring) + lax.rem(lax.rem(index, 2) + dx, 2)
        for dy, dx in slots(count)
    ]

    def step(t, _):
        span = pl.ds(pl.multiple_of((side * tiles + t) * TILE, TILE), TILE)
        place = pl.ds(pl.multiple_of(t * TILE, TILE), TILE)
        for f in range(fields):
            for i, spec_ref in zip(places, specs):
                right_ref[f, i] = -(res_ref[i, f, span] + spec_ref[f, span])
        coup = [coup_ref[i, span] for i in range(planes)]
        inv = [inv_ref[i, span] for i in range(last)]
        ratio = [coup[i] * inv[i] for i in range(last)]
        for f in range(fields):
            value = []
            for i in range(last):
                right = right_ref[f, i]
                if i:
                    right = right - coup[i] * value[-1]
                value.append(right * inv[i])
            y = value[-1]
            y_last = y
            y_ref[last - 1, f, place] = y
            for i in range(last - 2, -1, -1):
                y = value[i] - ratio[i] * y
                y_ref[i, f, place] = y
            target_ref[f, place] = y
            target_ref[fields + f, place] = right_ref[f, last] - coup[last] * y_last
        return 0

    lax.fori_loop(0, tiles, step, 0)


def merge_kernel(keep_ref, got_ref, pair_ref, link_ref, inner_ref, out_ref):
    fields = inner_ref.shape[0]
    rows = inner_ref.shape[1]
    lower_core = core_index() == 0

    def step(t, _):
        span = pl.ds(pl.multiple_of(t * TILE, TILE), TILE)
        inv, sep_a, first_a, lower_b = (pair_ref[k, span] for k in range(4))
        scale, lower, upper, edge = (link_ref[k, span] for k in range(4))
        for f in range(fields):
            keep_y, got_y = keep_ref[f, span], got_ref[f, span]
            keep_own, got_own = keep_ref[fields + f, span], got_ref[fields + f, span]
            y_a = jnp.where(lower_core, keep_y, got_y)
            y_b = jnp.where(lower_core, got_y, keep_y)
            own_a = jnp.where(lower_core, keep_own, got_own)
            own_b = jnp.where(lower_core, got_own, keep_own)
            inner = inv * (own_a - sep_a * y_b)
            inner_ref[f, span] = inner
            for k, x in (
                (f, scale * (own_b - lower_b * inner)),
                (fields + f, edge * (y_a - first_a * inner)),
            ):
                out_ref[2 * t, k] = x[0:4]
                out_ref[2 * t + 1, k] = x[4:8]
        for k, x in ((2 * fields, lower), (2 * fields + 1, upper)):
            out_ref[2 * t, k] = x[0:4]
            out_ref[2 * t + 1, k] = x[4:8]
        return 0

    lax.fori_loop(0, rows // TILE, step, 0)


def reduced_kernel(rhs_ref, out_ref):
    count = rhs_ref.shape[0]
    fields = out_ref.shape[1] // 2
    ratio = []
    values = []
    for p in range(count):
        lower, upper = rhs_ref[p, 2 * fields], rhs_ref[p, 2 * fields + 1]
        more = p + 1 < count
        inv = 1.0 / (1.0 - lower * ratio[-1]) if p else jnp.ones_like(lower)
        ratio.append(upper * inv)
        row = []
        for f in range(fields):
            right = rhs_ref[p, f]
            if more:
                right = right - rhs_ref[p + 1, fields + f]
            if p:
                right = right - lower * values[-1][f]
            row.append(right * inv)
        values.append(row)
    solved = values[-1]
    for p in range(count - 1, -1, -1):
        if p < count - 1:
            solved = [values[p][f] - ratio[p] * solved[f] for f in range(fields)]
        for f in range(fields):
            out_ref[p, fields + f] = solved[f]
            if p < count - 1:
                out_ref[p + 1, f] = solved[f]
    for f in range(fields):
        out_ref[0, f] = jnp.zeros_like(solved[f])


def expand_kernel(solved_ref, inner_ref, pair_ref, keep_ref, send_ref):
    fields, rows, _ = inner_ref.shape
    lower_core = core_index() == 0

    def step(t, _):
        span = pl.ds(pl.multiple_of(t * TILE, TILE), TILE)
        v, w = pair_ref[4, span], pair_ref[5, span]
        for f in range(fields):
            prev = jnp.concatenate([solved_ref[2 * t, f], solved_ref[2 * t + 1, f]], axis=0)
            own = jnp.concatenate(
                [solved_ref[2 * t, fields + f], solved_ref[2 * t + 1, fields + f]], axis=0
            )
            inner = inner_ref[f, span] - v * prev - w * own
            keep_ref[f, span] = jnp.where(lower_core, prev, inner)
            keep_ref[fields + f, span] = jnp.where(lower_core, inner, own)
            send_ref[f, span] = jnp.where(lower_core, inner, prev)
            send_ref[fields + f, span] = jnp.where(lower_core, own, inner)
        return 0

    lax.fori_loop(0, rows // TILE, step, 0)


def finish_kernel(mine, state_ref, v_ref, w_ref, y_ref, ends_ref, *refs):
    out_ref, block_ref, sems = refs[-3:]
    fields, planes, rows = state_ref.shape[1:4]
    last = planes - 1
    tiles = rows // TILE // 2
    side = half_of(mine)
    lines = pl.ds(pl.multiple_of(side * (rows // 2), rows // 2), rows // 2)
    copies = []
    for f in range(fields):

        def tile(t, _, f=f):
            span = pl.ds(pl.multiple_of((side * tiles + t) * TILE, TILE), TILE)
            place = pl.ds(pl.multiple_of(t * TILE, TILE), TILE)
            prev, own = ends_ref[f, place], ends_ref[fields + f, place]
            for i in range(last):
                delta = y_ref[i, f, place] - v_ref[i, span] * prev - w_ref[i, span] * own
                block_ref[f, i, place] = state_ref[0, f, i, span] + delta
            block_ref[f, last, place] = state_ref[0, f, last, span] + own
            return 0

        lax.fori_loop(0, tiles, tile, 0)
        copy = pltpu.make_async_copy(block_ref.at[f], out_ref.at[0, f, :, lines], sems.at[f])
        copy.start()
        copies.append(copy)
    for copy in copies:
        copy.wait()


def finish(mine, state, v, w, y, ends, partial=None):
    fields, planes, rows, lanes = state.shape[1:]
    hbm = pl.BlockSpec(memory_space=pltpu.HBM)
    operands = [state, v, w, y, ends]
    specs = [VMEM] * len(operands)
    aliases = {}
    if partial is not None:
        aliases = {len(operands): 0}
        operands.append(partial)
        specs.append(hbm)
    return pl.pallas_call(
        functools.partial(finish_kernel, mine),
        out_shape=jax.ShapeDtypeStruct(state.shape, jnp.float32),
        in_specs=specs,
        out_specs=hbm,
        scratch_shapes=[
            pltpu.VMEM((fields, planes, rows // 2, lanes), jnp.float32),
            pltpu.SemaphoreType.DMA((fields,)),
        ],
        input_output_aliases=aliases,
        compiler_params=pltpu.CompilerParams(vmem_limit_bytes=state.size * 12),
        cost_estimate=pl.CostEstimate(
            flops=state.size * 2, bytes_accessed=state.size * 6, transcendentals=0
        ),
    )(*operands)


def flux_parts(state, halo, flag_cells):
    fields, planes, rows, lanes = state.shape[1:]
    grid = (rows, lanes)
    return call(
        flux_kernel,
        [
            (planes, fields) + grid,
            (planes,) + grid,
            (planes - 1,) + grid,
            (planes - 1,) + grid,
            (planes - 1,) + grid,
            (COEFS, rows // 2, lanes),
            (COEFS, rows // 2, lanes),
        ],
        state,
        halo,
        flag_cells,
        flops=state.size * 60,
    )


def exchange(x, axis, groups=None):
    return lax.all_to_all(x, axis, 0, 0, tiled=True, axis_index_groups=groups)


def body(flow_state, thinc_flags):
    own = flow_state[0]
    planes, rows, lanes = own.shape[1:]
    instances = lax.axis_size("inst")
    ax_count = lax.axis_size("ax")
    circ_count = lax.axis_size("circ")
    chips = ax_count // 2
    half = rows // 2
    piece = half // chips

    swap = [(i, i ^ 1) for i in range(ax_count)]
    groups = [list(range(c, ax_count, 2)) for c in range(2)]

    def partner(x):
        return lax.ppermute(x, "ax", swap)

    def neighbour(x, by):
        moves = [(i, i + 2 * by) for i in range(ax_count) if 0 <= i + 2 * by < ax_count]
        return lax.ppermute(x, "ax", moves)

    steps = slots(instances)
    blocks = list(pick(flow_state, thinc_flags, instances))
    edges = blocks.pop()
    halo = lax.ppermute(
        edges, "circ", [(i, (i + 1) % circ_count) for i in range(circ_count)]
    )
    order = ORDER
    for k in order:
        blocks[k] = lax.ppermute(blocks[k], "inst", route(*steps[k], instances))
    flags = (thinc_flags[0] > 0).astype(jnp.float32)
    flag_cells = jnp.broadcast_to(flags[:, :, None], (planes, rows, lanes))

    res, coup, inv, v, w, keep, send = flux_parts(flow_state, halo, flag_cells)

    thin = (half, lanes)
    pair, raw, ends = call(
        pair_kernel, [(6,) + thin, (3,) + thin, (2,) + thin], keep, partner(send)
    )
    blocks, res, ends = lax.optimization_barrier((blocks, res, ends))
    specs = call(spectral_kernel, [blocks[0].shape] * instances, *blocks, flops=own.size * 9)
    for k in order:
        specs[k] = lax.ppermute(specs[k], "inst", route(*steps[k], instances))
    ends = neighbour(ends, -1)
    link, edge = call(link_kernel, [(3,) + thin, (1,) + thin], raw, ends)
    edge = neighbour(edge, 1)
    (link,) = call(join_kernel, [(4,) + thin], link, edge)
    shapes = [(planes - 1, FIELDS, half, lanes), (2 * FIELDS, half, lanes)]
    parts = []
    for mine in (False, True):
        parts.append(
            call(
                functools.partial(sweep_kernel, mine),
                shapes,
                res,
                coup,
                inv,
                *specs,
                flops=own.size * 4,
                scratch=[(FIELDS, planes, TILE, lanes)],
            )
        )
    (y_other, send), (y_mine, keep) = parts
    inner, rhs = call(
        merge_kernel,
        [(FIELDS, half, lanes), (chips, 2 * FIELDS + 2, piece, lanes)],
        keep,
        partner(send),
        pair,
        link,
        flops=send.size * 4,
    )
    rhs = exchange(rhs, "ax", groups)
    (solved,) = call(
        reduced_kernel, [(chips, 2 * FIELDS, piece, lanes)], rhs, flops=rhs.size * 8
    )
    solved = exchange(solved, "ax", groups)
    keep, send = call(
        expand_kernel,
        [(2 * FIELDS, half, lanes)] * 2,
        solved,
        inner,
        pair,
        flops=send.size * 4,
    )
    got = partner(send)
    out = finish(True, flow_state, v, w, y_mine, keep)
    return finish(False, flow_state, v, w, y_other, got, out)


def solution(mesh):
    return jax.shard_map(
        body,
        mesh=mesh,
        in_specs=(P("inst", None, "ax", "circ", None), P("inst", "ax", "circ")),
        out_specs=P("inst", None, "ax", "circ", None),
        check_vma=False,
    )
```

```python
import functools
import math

import jax
import jax.numpy as jnp
from jax import lax
from jax.experimental import pallas as pl
from jax.experimental.pallas import tpu as pltpu
from jax.sharding import PartitionSpec as P


G_LIQ = 4.4
P_LIQ = 6.0
G_GAS = 1.4
BETA = 1.6
EPSA = 0.1
ALPHA = 4.0
DIAG0 = 0.016
OMEGA = 1.0
NU_T = 0.25

FIELDS = 7
ORDER = (3, 4, 5, 7, 1, 2, 6)
EDGES = 2 * FIELDS + 3
COEFS = 5
TILE = 8


VMEM = pl.BlockSpec(memory_space=pltpu.VMEM)


def spectral_weights(count):
    table = []
    for k in range(count):
        if k == 0:
            first, second = 0.0, -(count * count + 2) / 12.0
        else:
            sign = 1.0 if k % 2 == 0 else -1.0
            angle = math.pi * k / count
            first = 0.5 * sign * math.cos(angle) / math.sin(angle)
            second = -sign / (2.0 * math.sin(angle) ** 2)
        table.append(OMEGA * first - NU_T * OMEGA * OMEGA * second)
    return table


def core_index():
    return lax.rem(lax.axis_index("ax"), 2)


def call(kernel, outs, *operands, flops=0, scratch=()):
    outs = [jax.ShapeDtypeStruct(shape, jnp.float32) for shape in outs]
    total = sum(x.size * 4 for x in operands) + sum(x.size * 4 for x in outs)
    run = pl.pallas_call(
        kernel,
        out_shape=outs,
        in_specs=[VMEM] * len(operands),
        out_specs=[VMEM] * len(outs),
        scratch_shapes=[pltpu.VMEM(x, jnp.float32) for x in scratch],
        compiler_params=pltpu.CompilerParams(
            vmem_limit_bytes=total + sum(math.prod(x) * 4 for x in scratch) + (2 << 20)
        ),
        cost_estimate=pl.CostEstimate(flops=flops, bytes_accessed=total, transcendentals=0),
    )
    return list(run(*operands))


def slots(count):
    steps = [(dy, dx) for dy in range(count // 2) for dx in range(2)]
    return steps


def route(dy, dx, count):
    ring = count // 2
    return [(i, 2 * ((i // 2 + dy) % ring) + ((i % 2) ^ dx)) for i in range(count)]


def places_of(count, chosen):
    index = lax.axis_index("inst")
    ring = count // 2
    steps = slots(count)
    return [
        2 * lax.rem(index // 2 + steps[k][0], ring) + lax.rem(lax.rem(index, 2) + steps[k][1], 2)
        for k in chosen
    ]


def first_kernel(count, chosen, state_ref, out_ref, sem):
    (place,) = places_of(count, (chosen,))
    copy = pltpu.make_async_copy(state_ref.at[0, :, place], out_ref, sem)
    copy.start()
    copy.wait()


def rest_kernel(count, chosen, state_ref, flag_ref, early_ref, *refs):
    outs = refs[: len(chosen)]
    edge_ref, held_ref, sems = refs[len(chosen) :]
    fields, rows = state_ref.shape[1], state_ref.shape[3]
    early = next(k for k in range(count) if k not in chosen)
    (early_place,), places = places_of(count, (early,)), places_of(count, chosen)
    copies = [
        pltpu.make_async_copy(state_ref.at[0, :, place], out, sems.at[k])
        for k, (place, out) in enumerate(zip(places, outs))
    ]
    for copy in copies:
        copy.start()
    flag_copy = pltpu.make_async_copy(flag_ref, held_ref, sems.at[len(chosen)])
    flag_copy.start()

    def edges(place, block):
        row = pl.ds(place, 1)
        for f in range(fields):
            edge_ref[f, row] = block[f, 0:1]
            edge_ref[fields + f, row] = block[f, rows - 1 : rows]
        edge_ref[2 * fields, row] = block[fields - 1, 1:2]
        edge_ref[2 * fields + 1, row] = block[fields - 1, rows - 2 : rows - 1]

    edges(early_place, early_ref)
    flag_copy.wait()
    flags = (held_ref[0] > 0).astype(jnp.float32)
    edge_ref[EDGES - 1] = jnp.broadcast_to(flags[:, 0:1], edge_ref.shape[1:])
    for copy, place, out in zip(copies, places, outs):
        copy.wait()
        edges(place, out)


def pick_first(state, count, chosen):
    _, fields, _, rows, lanes = state.shape
    return pl.pallas_call(
        functools.partial(first_kernel, count, chosen),
        out_shape=jax.ShapeDtypeStruct((fields, rows, lanes), jnp.float32),
        in_specs=[pl.BlockSpec(memory_space=pltpu.HBM)],
        out_specs=VMEM,
        scratch_shapes=[pltpu.SemaphoreType.DMA],
        compiler_params=pltpu.CompilerParams(vmem_limit_bytes=4 << 20),
        cost_estimate=pl.CostEstimate(
            flops=0, bytes_accessed=fields * rows * lanes * 8, transcendentals=0
        ),
    )(pltpu.with_memory_space_constraint(state, pltpu.HBM))


def pick_rest(state, flags, early, count, chosen):
    _, fields, planes, rows, lanes = state.shape
    shapes = [(fields, rows, lanes)] * len(chosen) + [(EDGES, planes, lanes)]
    hbm = pl.BlockSpec(memory_space=pltpu.HBM)
    return pl.pallas_call(
        functools.partial(rest_kernel, count, chosen),
        out_shape=[jax.ShapeDtypeStruct(x, jnp.float32) for x in shapes],
        in_specs=[hbm, hbm, VMEM],
        out_specs=[VMEM] * len(shapes),
        scratch_shapes=[
            pltpu.VMEM(flags.shape, flags.dtype),
            pltpu.SemaphoreType.DMA((len(chosen) + 1,)),
        ],
        compiler_params=pltpu.CompilerParams(vmem_limit_bytes=state.size * 4 + (3 << 20)),
        cost_estimate=pl.CostEstimate(flops=0, bytes_accessed=state.size * 8, transcendentals=0),
    )(*(pltpu.with_memory_space_constraint(x, pltpu.HBM) for x in (state, flags)), early)


def mixing(count, parity):
    weights = spectral_weights(count)
    table = []
    for shift in (0, 1 - 2 * parity, 2 * parity - 1):
        g = [weights[(2 * a + shift) % count] for a in range(4)]
        table += [0.5 * (g[0] + g[2]), 0.5 * (g[1] + g[3])]
        table += [0.5 * (g[0] - g[2]), 0.5 * (g[1] - g[3])]
    return table


def spectral_kernel(*refs):
    count = len(refs) // 2
    ins, outs = refs[:count], refs[count:]
    fields, rows, _ = ins[0].shape
    tiles = rows // TILE
    first = lax.rem(lax.axis_index("inst"), 2) == 0
    mix = [
        jnp.where(first, jnp.float32(a), jnp.float32(b))
        for a, b in zip(mixing(count, 0), mixing(count, 1))
    ]

    def step(index, _):
        f = index // tiles
        span = pl.ds(pl.multiple_of((index % tiles) * TILE, TILE), TILE)
        parts = []
        for dx in range(2):
            u = [ins[2 * dy + dx][f, span] for dy in range(4)]
            parts.append((u[0] + u[2], u[1] + u[3], u[0] - u[2], u[1] - u[3]))
        for ex in range(2):
            even, odd, even_next, odd_next = 0.0, 0.0, 0.0, 0.0
            for dx in range(2):
                kind = 0 if ex == dx else (1 if ex else 2)
                e0, e1, o0, o1 = mix[4 * kind : 4 * kind + 4]
                s0, s1, d0, d1 = parts[dx]
                even = even + (e0 * s0 + e1 * s1)
                odd = odd + (o0 * d0 + o1 * d1)
                even_next = even_next + (e1 * s0 + e0 * s1)
                odd_next = odd_next + (o1 * d0 - o0 * d1)
            outs[ex][f, span] = even + odd
            outs[4 + ex][f, span] = even - odd
            outs[2 + ex][f, span] = even_next + odd_next
            outs[6 + ex][f, span] = even_next - odd_next
        return 0

    lax.fori_loop(0, fields * tiles, step, 0, unroll=4)


def primitives(cells):
    density = cells[0] + cells[1]
    inverse = 1.0 / density
    vel_ax = cells[2] * inverse
    vel_circ = cells[3] * inverse
    vel_rad = cells[4] * inverse
    fraction = cells[6]
    gamma_term = fraction / (G_LIQ - 1.0) + (1.0 - fraction) / (G_GAS - 1.0)
    stiff_term = fraction * (G_LIQ * P_LIQ / (G_LIQ - 1.0))
    kinetic = 0.5 * density * (vel_ax * vel_ax + vel_circ * vel_circ + vel_rad * vel_rad)
    gamma_inv = 1.0 / gamma_term
    pressure = (cells[5] - kinetic - stiff_term) * gamma_inv
    sound_speed = jnp.sqrt(((1.0 + gamma_inv) * pressure + stiff_term * gamma_inv) * inverse)
    return vel_ax, vel_circ, pressure, sound_speed


def sharpen(lower_val, centre, upper_val, offset):
    average = 0.5 * (lower_val + upper_val)
    difference = upper_val - lower_val
    steepness = 2.0 * (centre - average) / (jnp.abs(difference) + EPSA)
    return average + 0.5 * difference * jnp.tanh(BETA * (steepness + offset))


def flux_kernel(
    state_ref, halo_ref, flag_ref, res_ref, coup_ref, inv_ref, v_ref, w_ref, keep_ref, send_ref
):
    planes = state_ref.shape[2]
    rows = state_ref.shape[3]
    last = planes - 1

    def plane(i, _):
        row = pl.ds(i, 1)
        quad = (TILE // 2, state_ref.shape[4])
        cells = []
        for f in range(FIELDS):
            upper, lower = halo_ref[f, row], halo_ref[FIELDS + f, row]
            if f < FIELDS - 1:
                edge = [jnp.broadcast_to(upper, quad), jnp.broadcast_to(lower, quad)]
            else:
                next_upper = halo_ref[2 * FIELDS, row]
                next_lower = halo_ref[2 * FIELDS + 1, row]
                edge = [upper] + [next_upper] * 3 + [next_lower] * 3 + [lower]
            cells.append(jnp.concatenate([state_ref[0, f, i]] + edge, axis=0))
        edge = jnp.broadcast_to(halo_ref[EDGES - 1, row], (TILE, state_ref.shape[4]))
        flags = jnp.concatenate([flag_ref[i], edge], axis=0)
        total = rows + TILE

        def below(x, by=1):
            return pltpu.roll(x, by, 0)

        def above(x):
            return pltpu.roll(x, total - 1, 0)

        vel_ax, vel_circ, pressure, sound = primitives(cells)
        coup_ref[i] = -ALPHA * (jnp.abs(vel_ax) + sound)[:rows]
        wave = jnp.abs(vel_circ) + sound
        half_speed = 0.5 * jnp.maximum(below(wave), wave)
        fraction = cells[6]
        back1 = below(fraction)
        sharp_left = sharpen(below(fraction, 2), back1, fraction, 1.0)
        sharp_right = sharpen(back1, fraction, above(fraction), -1.0)
        flagged = flags > 0.5
        frac_left = jnp.where(flagged, sharp_left, back1)
        frac_right = jnp.where(flagged, sharp_right, fraction)
        for f in range(FIELDS):
            if f < 6:
                flux = cells[f] * vel_circ
                if f == 3:
                    flux = flux + pressure
                elif f == 5:
                    flux = flux + pressure * vel_circ
                mean = 0.5 * (below(flux) + flux)
                jump = cells[f] - below(cells[f])
            else:
                mean = 0.5 * (frac_left * below(vel_circ) + frac_right * vel_circ)
                jump = frac_right - frac_left
            face = mean - half_speed * jump
            res_ref[i, f] = (above(face) - face)[:rows]
        return 0

    lax.fori_loop(0, planes, plane, 0)

    core = core_index()
    tiles = rows // TILE // 2
    for target_ref, side in ((keep_ref, core), (send_ref, 1 - core)):

        def factor(t, _, target_ref=target_ref, side=side):
            span = pl.ds(pl.multiple_of((side * tiles + t) * TILE, TILE), TILE)
            place = pl.ds(pl.multiple_of(t * TILE, TILE), TILE)
            coup = [coup_ref[i, span] for i in range(planes)]
            inv, ratio, v = [], [], []
            for i in range(last):
                pivot = DIAG0 - 2.0 * coup[i]
                if i:
                    pivot = pivot - coup[i] * ratio[-1]
                inv.append(1.0 / pivot)
                ratio.append(coup[i] * inv[-1])
                v.append(inv[-1] if i == 0 else -(ratio[-1] * v[-1]))
                inv_ref[i, span] = inv[-1]
            v_next, w_next = v[-1], inv[-1]
            v_last, w_last = v_next * coup[0], w_next * coup[last - 1]
            for i in range(last - 1, -1, -1):
                if i < last - 1:
                    v_next = v[i] - ratio[i] * v_next
                    w_next = -(ratio[i] * w_next)
                v_first, w_first = v_next * coup[0], w_next * coup[last - 1]
                v_ref[i, span] = v_first
                w_ref[i, span] = w_first
            sep = coup[last]
            target_ref[0, place] = -(sep * v_last)
            target_ref[1, place] = DIAG0 - 2.0 * sep - sep * w_last
            target_ref[2, place] = sep
            target_ref[3, place] = v_first
            target_ref[4, place] = w_first
            return 0

        lax.fori_loop(0, tiles, factor, 0)


def pair_kernel(keep_ref, got_ref, pair_ref, raw_ref, ends_ref):
    lower_core = core_index() == 0
    lower_a, diag_a, sep_a, v_a, w_a = (
        jnp.where(lower_core, keep_ref[k], got_ref[k]) for k in range(COEFS)
    )
    lower_b, diag_b, sep_b, v_b, w_b = (
        jnp.where(lower_core, got_ref[k], keep_ref[k]) for k in range(COEFS)
    )
    inv = 1.0 / (diag_a - sep_a * v_b)
    v = inv * lower_a
    w = -(inv * sep_a * w_b)
    for k, x in enumerate((inv, sep_a, w_a, lower_b, v, w)):
        pair_ref[k] = x
    raw_ref[0] = diag_b - lower_b * w
    raw_ref[1] = -(lower_b * v)
    raw_ref[2] = sep_b
    ends_ref[0] = v_a - w_a * v
    ends_ref[1] = -(w_a * w)


def link_kernel(raw_ref, ends_ref, link_ref, edge_ref):
    sep = raw_ref[2]
    scale = 1.0 / (raw_ref[0] - sep * ends_ref[0])
    link_ref[0] = scale
    link_ref[1] = raw_ref[1] * scale
    link_ref[2] = -(sep * ends_ref[1]) * scale
    edge_ref[0] = sep * scale


def join_kernel(link_ref, edge_ref, out_ref):
    for k in range(3):
        out_ref[k] = link_ref[k]
    out_ref[3] = edge_ref[0]


def half_of(mine):
    core = core_index()
    return core if mine else 1 - core


def sweep_kernel(mine, res_ref, coup_ref, inv_ref, *refs):
    count = len(refs) - 3
    specs = refs[:count]
    y_ref, target_ref, right_ref = refs[count:]
    planes, fields, rows, _ = res_ref.shape
    last = planes - 1
    tiles = rows // TILE // 2
    side = half_of(mine)
    index = lax.axis_index("inst")
    ring = count // 2
    places = [
        2 * lax.rem(index // 2 + ring - dy, ring) + lax.rem(lax.rem(index, 2) + dx, 2)
        for dy, dx in slots(count)
    ]

    def step(t, _):
        span = pl.ds(pl.multiple_of((side * tiles + t) * TILE, TILE), TILE)
        place = pl.ds(pl.multiple_of(t * TILE, TILE), TILE)
        for f in range(fields):
            for i, spec_ref in zip(places, specs):
                right_ref[f, i] = -(res_ref[i, f, span] + spec_ref[f, span])
        coup = [coup_ref[i, span] for i in range(planes)]
        inv = [inv_ref[i, span] for i in range(last)]
        ratio = [coup[i] * inv[i] for i in range(last)]
        for f in range(fields):
            value = []
            for i in range(last):
                right = right_ref[f, i]
                if i:
                    right = right - coup[i] * value[-1]
                value.append(right * inv[i])
            y = value[-1]
            y_last = y
            y_ref[last - 1, f, place] = y
            for i in range(last - 2, -1, -1):
                y = value[i] - ratio[i] * y
                y_ref[i, f, place] = y
            target_ref[f, place] = y
            target_ref[fields + f, place] = right_ref[f, last] - coup[last] * y_last
        return 0

    lax.fori_loop(0, tiles, step, 0)


def merge_kernel(keep_ref, got_ref, pair_ref, link_ref, inner_ref, out_ref):
    fields = inner_ref.shape[0]
    rows = inner_ref.shape[1]
    lower_core = core_index() == 0

    def step(t, _):
        span = pl.ds(pl.multiple_of(t * TILE, TILE), TILE)
        inv, sep_a, first_a, lower_b = (pair_ref[k, span] for k in range(4))
        scale, lower, upper, edge = (link_ref[k, span] for k in range(4))
        for f in range(fields):
            keep_y, got_y = keep_ref[f, span], got_ref[f, span]
            keep_own, got_own = keep_ref[fields + f, span], got_ref[fields + f, span]
            y_a = jnp.where(lower_core, keep_y, got_y)
            y_b = jnp.where(lower_core, got_y, keep_y)
            own_a = jnp.where(lower_core, keep_own, got_own)
            own_b = jnp.where(lower_core, got_own, keep_own)
            inner = inv * (own_a - sep_a * y_b)
            inner_ref[f, span] = inner
            for k, x in (
                (f, scale * (own_b - lower_b * inner)),
                (fields + f, edge * (y_a - first_a * inner)),
            ):
                out_ref[2 * t, k] = x[0:4]
                out_ref[2 * t + 1, k] = x[4:8]
        for k, x in ((2 * fields, lower), (2 * fields + 1, upper)):
            out_ref[2 * t, k] = x[0:4]
            out_ref[2 * t + 1, k] = x[4:8]
        return 0

    lax.fori_loop(0, rows // TILE, step, 0)


def reduced_kernel(rhs_ref, out_ref):
    count = rhs_ref.shape[0]
    fields = out_ref.shape[1] // 2
    ratio = []
    values = []
    for p in range(count):
        lower, upper = rhs_ref[p, 2 * fields], rhs_ref[p, 2 * fields + 1]
        more = p + 1 < count
        inv = 1.0 / (1.0 - lower * ratio[-1]) if p else jnp.ones_like(lower)
        ratio.append(upper * inv)
        row = []
        for f in range(fields):
            right = rhs_ref[p, f]
            if more:
                right = right - rhs_ref[p + 1, fields + f]
            if p:
                right = right - lower * values[-1][f]
            row.append(right * inv)
        values.append(row)
    solved = values[-1]
    for p in range(count - 1, -1, -1):
        if p < count - 1:
            solved = [values[p][f] - ratio[p] * solved[f] for f in range(fields)]
        for f in range(fields):
            out_ref[p, fields + f] = solved[f]
            if p < count - 1:
                out_ref[p + 1, f] = solved[f]
    for f in range(fields):
        out_ref[0, f] = jnp.zeros_like(solved[f])


def expand_kernel(solved_ref, inner_ref, pair_ref, keep_ref, send_ref):
    fields, rows, _ = inner_ref.shape
    lower_core = core_index() == 0

    def step(t, _):
        span = pl.ds(pl.multiple_of(t * TILE, TILE), TILE)
        v, w = pair_ref[4, span], pair_ref[5, span]
        for f in range(fields):
            prev = jnp.concatenate([solved_ref[2 * t, f], solved_ref[2 * t + 1, f]], axis=0)
            own = jnp.concatenate(
                [solved_ref[2 * t, fields + f], solved_ref[2 * t + 1, fields + f]], axis=0
            )
            inner = inner_ref[f, span] - v * prev - w * own
            keep_ref[f, span] = jnp.where(lower_core, prev, inner)
            keep_ref[fields + f, span] = jnp.where(lower_core, inner, own)
            send_ref[f, span] = jnp.where(lower_core, inner, prev)
            send_ref[fields + f, span] = jnp.where(lower_core, own, inner)
        return 0

    lax.fori_loop(0, rows // TILE, step, 0)


def finish_kernel(mine, state_ref, v_ref, w_ref, y_ref, ends_ref, *refs):
    out_ref, block_ref, sems = refs[-3:]
    fields, planes, rows = state_ref.shape[1:4]
    last = planes - 1
    tiles = rows // TILE // 2
    side = half_of(mine)
    lines = pl.ds(pl.multiple_of(side * (rows // 2), rows // 2), rows // 2)
    copies = []
    for f in range(fields):

        def tile(t, _, f=f):
            span = pl.ds(pl.multiple_of((side * tiles + t) * TILE, TILE), TILE)
            place = pl.ds(pl.multiple_of(t * TILE, TILE), TILE)
            prev, own = ends_ref[f, place], ends_ref[fields + f, place]
            for i in range(last):
                delta = y_ref[i, f, place] - v_ref[i, span] * prev - w_ref[i, span] * own
                block_ref[f, i, place] = state_ref[0, f, i, span] + delta
            block_ref[f, last, place] = state_ref[0, f, last, span] + own
            return 0

        lax.fori_loop(0, tiles, tile, 0, unroll=True)
        copy = pltpu.make_async_copy(block_ref.at[f], out_ref.at[0, f, :, lines], sems.at[f])
        copy.start()
        copies.append(copy)
    for copy in copies:
        copy.wait()


def finish(mine, state, v, w, y, ends, partial=None):
    fields, planes, rows, lanes = state.shape[1:]
    hbm = pl.BlockSpec(memory_space=pltpu.HBM)
    operands = [state, v, w, y, ends]
    specs = [VMEM] * len(operands)
    aliases = {}
    if partial is not None:
        aliases = {len(operands): 0}
        operands.append(partial)
        specs.append(hbm)
    return pl.pallas_call(
        functools.partial(finish_kernel, mine),
        out_shape=jax.ShapeDtypeStruct(state.shape, jnp.float32),
        in_specs=specs,
        out_specs=hbm,
        scratch_shapes=[
            pltpu.VMEM((fields, planes, rows // 2, lanes), jnp.float32),
            pltpu.SemaphoreType.DMA((fields,)),
        ],
        input_output_aliases=aliases,
        compiler_params=pltpu.CompilerParams(vmem_limit_bytes=state.size * 12),
        cost_estimate=pl.CostEstimate(
            flops=state.size * 2, bytes_accessed=state.size * 6, transcendentals=0
        ),
    )(*operands)


def flux_parts(state, halo, flag_cells):
    fields, planes, rows, lanes = state.shape[1:]
    grid = (rows, lanes)
    return call(
        flux_kernel,
        [
            (planes, fields) + grid,
            (planes,) + grid,
            (planes - 1,) + grid,
            (planes - 1,) + grid,
            (planes - 1,) + grid,
            (COEFS, rows // 2, lanes),
            (COEFS, rows // 2, lanes),
        ],
        state,
        halo,
        flag_cells,
        flops=state.size * 60,
    )


def exchange(x, axis, groups=None):
    return lax.all_to_all(x, axis, 0, 0, tiled=True, axis_index_groups=groups)


def body(flow_state, thinc_flags):
    own = flow_state[0]
    planes, rows, lanes = own.shape[1:]
    instances = lax.axis_size("inst")
    ax_count = lax.axis_size("ax")
    circ_count = lax.axis_size("circ")
    chips = ax_count // 2
    half = rows // 2
    piece = half // chips

    swap = [(i, i ^ 1) for i in range(ax_count)]
    groups = [list(range(c, ax_count, 2)) for c in range(2)]

    def partner(x):
        return lax.ppermute(x, "ax", swap)

    def neighbour(x, by):
        moves = [(i, i + 2 * by) for i in range(ax_count) if 0 <= i + 2 * by < ax_count]
        return lax.ppermute(x, "ax", moves)

    steps = slots(instances)
    order = ORDER
    rest = tuple(k for k in range(instances) if k != order[0])
    blocks = [None] * instances
    early = pick_first(flow_state, instances, order[0])
    *others, edges = pick_rest(flow_state, thinc_flags, early, instances, rest)
    blocks[order[0]] = early
    late_state, edges = lax.optimization_barrier((flow_state, edges))
    for k, block in zip(rest, others):
        blocks[k] = block
    halo = lax.ppermute(
        edges, "circ", [(i, (i + 1) % circ_count) for i in range(circ_count)]
    )
    for k in order:
        blocks[k] = lax.ppermute(blocks[k], "inst", route(*steps[k], instances))
    flags = (thinc_flags[0] > 0).astype(jnp.float32)
    flag_cells = jnp.broadcast_to(flags[:, :, None], (planes, rows, lanes))

    res, coup, inv, v, w, keep, send = flux_parts(late_state, halo, flag_cells)

    thin = (half, lanes)
    pair, raw, ends = call(
        pair_kernel, [(6,) + thin, (3,) + thin, (2,) + thin], keep, partner(send)
    )
    blocks, res, ends = lax.optimization_barrier((blocks, res, ends))
    specs = call(spectral_kernel, [blocks[0].shape] * instances, *blocks, flops=own.size * 9)
    for k in order:
        specs[k] = lax.ppermute(specs[k], "inst", route(*steps[k], instances))
    ends = neighbour(ends, -1)
    link, edge = call(link_kernel, [(3,) + thin, (1,) + thin], raw, ends)
    edge = neighbour(edge, 1)
    (link,) = call(join_kernel, [(4,) + thin], link, edge)
    shapes = [(planes - 1, FIELDS, half, lanes), (2 * FIELDS, half, lanes)]
    parts = []
    for mine in (False, True):
        parts.append(
            call(
                functools.partial(sweep_kernel, mine),
                shapes,
                res,
                coup,
                inv,
                *specs,
                flops=own.size * 4,
                scratch=[(FIELDS, planes, TILE, lanes)],
            )
        )
    (y_other, send), (y_mine, keep) = parts
    inner, rhs = call(
        merge_kernel,
        [(FIELDS, half, lanes), (chips, 2 * FIELDS + 2, piece, lanes)],
        keep,
        partner(send),
        pair,
        link,
        flops=send.size * 4,
    )
    rhs = exchange(rhs, "ax", groups)
    (solved,) = call(
        reduced_kernel, [(chips, 2 * FIELDS, piece, lanes)], rhs, flops=rhs.size * 8
    )
    solved = exchange(solved, "ax", groups)
    keep, send = call(
        expand_kernel,
        [(2 * FIELDS, half, lanes)] * 2,
        solved,
        inner,
        pair,
        flops=send.size * 4,
    )
    got = partner(send)
    out = finish(True, late_state, v, w, y_mine, keep)
    return finish(False, late_state, v, w, y_other, got, out)


def solution(mesh):
    return jax.shard_map(
        body,
        mesh=mesh,
        in_specs=(P("inst", None, "ax", "circ", None), P("inst", "ax", "circ")),
        out_specs=P("inst", None, "ax", "circ", None),
        check_vma=False,
    )
```

```python
import functools
import math

import jax
import jax.numpy as jnp
from jax import lax
from jax.experimental import pallas as pl
from jax.experimental.pallas import tpu as pltpu
from jax.sharding import PartitionSpec as P


G_LIQ = 4.4
P_LIQ = 6.0
G_GAS = 1.4
BETA = 1.6
EPSA = 0.1
ALPHA = 4.0
DIAG0 = 0.016
OMEGA = 1.0
NU_T = 0.25

FIELDS = 7
ORDER = (3, 4, 5, 7, 1, 2, 6)
EDGES = 2 * FIELDS + 3
COEFS = 5
TILE = 8


VMEM = pl.BlockSpec(memory_space=pltpu.VMEM)


def spectral_weights(count):
    table = []
    for k in range(count):
        if k == 0:
            first, second = 0.0, -(count * count + 2) / 12.0
        else:
            sign = 1.0 if k % 2 == 0 else -1.0
            angle = math.pi * k / count
            first = 0.5 * sign * math.cos(angle) / math.sin(angle)
            second = -sign / (2.0 * math.sin(angle) ** 2)
        table.append(OMEGA * first - NU_T * OMEGA * OMEGA * second)
    return table


def core_index():
    return lax.rem(lax.axis_index("ax"), 2)


def call(kernel, outs, *operands, flops=0, scratch=()):
    outs = [jax.ShapeDtypeStruct(shape, jnp.float32) for shape in outs]
    total = sum(x.size * 4 for x in operands) + sum(x.size * 4 for x in outs)
    run = pl.pallas_call(
        kernel,
        out_shape=outs,
        in_specs=[VMEM] * len(operands),
        out_specs=[VMEM] * len(outs),
        scratch_shapes=[pltpu.VMEM(x, jnp.float32) for x in scratch],
        compiler_params=pltpu.CompilerParams(
            vmem_limit_bytes=total + sum(math.prod(x) * 4 for x in scratch) + (2 << 20)
        ),
        cost_estimate=pl.CostEstimate(flops=flops, bytes_accessed=total, transcendentals=0),
    )
    return list(run(*operands))


def slots(count):
    steps = [(dy, dx) for dy in range(count // 2) for dx in range(2)]
    return steps


def route(dy, dx, count):
    ring = count // 2
    return [(i, 2 * ((i // 2 + dy) % ring) + ((i % 2) ^ dx)) for i in range(count)]


def places_of(count, chosen):
    index = lax.axis_index("inst")
    ring = count // 2
    steps = slots(count)
    return [
        2 * lax.rem(index // 2 + steps[k][0], ring) + lax.rem(lax.rem(index, 2) + steps[k][1], 2)
        for k in chosen
    ]


def first_kernel(count, chosen, state_ref, out_ref, sem):
    (place,) = places_of(count, (chosen,))
    copy = pltpu.make_async_copy(state_ref.at[0, :, place], out_ref, sem)
    copy.start()
    copy.wait()


def rest_kernel(count, chosen, state_ref, flag_ref, early_ref, *refs):
    outs = refs[: len(chosen)]
    edge_ref, held_ref, sems = refs[len(chosen) :]
    fields, rows = state_ref.shape[1], state_ref.shape[3]
    early = next(k for k in range(count) if k not in chosen)
    (early_place,), places = places_of(count, (early,)), places_of(count, chosen)
    copies = [
        pltpu.make_async_copy(state_ref.at[0, :, place], out, sems.at[k])
        for k, (place, out) in enumerate(zip(places, outs))
    ]
    for copy in copies:
        copy.start()
    flag_copy = pltpu.make_async_copy(flag_ref, held_ref, sems.at[len(chosen)])
    flag_copy.start()

    def edges(place, block):
        row = pl.ds(place, 1)
        for f in range(fields):
            edge_ref[f, row] = block[f, 0:1]
            edge_ref[fields + f, row] = block[f, rows - 1 : rows]
        edge_ref[2 * fields, row] = block[fields - 1, 1:2]
        edge_ref[2 * fields + 1, row] = block[fields - 1, rows - 2 : rows - 1]

    edges(early_place, early_ref)
    flag_copy.wait()
    flags = (held_ref[0] > 0).astype(jnp.float32)
    edge_ref[EDGES - 1] = jnp.broadcast_to(flags[:, 0:1], edge_ref.shape[1:])
    for copy, place, out in zip(copies, places, outs):
        copy.wait()
        edges(place, out)


def pick_first(state, count, chosen):
    _, fields, _, rows, lanes = state.shape
    return pl.pallas_call(
        functools.partial(first_kernel, count, chosen),
        out_shape=jax.ShapeDtypeStruct((fields, rows, lanes), jnp.float32),
        in_specs=[pl.BlockSpec(memory_space=pltpu.HBM)],
        out_specs=VMEM,
        scratch_shapes=[pltpu.SemaphoreType.DMA],
        compiler_params=pltpu.CompilerParams(vmem_limit_bytes=4 << 20),
        cost_estimate=pl.CostEstimate(
            flops=0, bytes_accessed=fields * rows * lanes * 8, transcendentals=0
        ),
    )(pltpu.with_memory_space_constraint(state, pltpu.HBM))


def pick_rest(state, flags, early, count, chosen):
    _, fields, planes, rows, lanes = state.shape
    shapes = [(fields, rows, lanes)] * len(chosen) + [(EDGES, planes, lanes)]
    hbm = pl.BlockSpec(memory_space=pltpu.HBM)
    return pl.pallas_call(
        functools.partial(rest_kernel, count, chosen),
        out_shape=[jax.ShapeDtypeStruct(x, jnp.float32) for x in shapes],
        in_specs=[hbm, hbm, VMEM],
        out_specs=[VMEM] * len(shapes),
        scratch_shapes=[
            pltpu.VMEM(flags.shape, flags.dtype),
            pltpu.SemaphoreType.DMA((len(chosen) + 1,)),
        ],
        compiler_params=pltpu.CompilerParams(vmem_limit_bytes=state.size * 4 + (3 << 20)),
        cost_estimate=pl.CostEstimate(flops=0, bytes_accessed=state.size * 8, transcendentals=0),
    )(*(pltpu.with_memory_space_constraint(x, pltpu.HBM) for x in (state, flags)), early)


def mixing(count, parity):
    weights = spectral_weights(count)
    table = []
    for shift in (0, 1 - 2 * parity, 2 * parity - 1):
        g = [weights[(2 * a + shift) % count] for a in range(4)]
        table += [0.5 * (g[0] + g[2]), 0.5 * (g[1] + g[3])]
        table += [0.5 * (g[0] - g[2]), 0.5 * (g[1] - g[3])]
    return table


def spectral_kernel(*refs):
    count = len(refs) // 2
    ins, outs = refs[:count], refs[count:]
    fields, rows, _ = ins[0].shape
    tiles = rows // TILE
    first = lax.rem(lax.axis_index("inst"), 2) == 0
    mix = [
        jnp.where(first, jnp.float32(a), jnp.float32(b))
        for a, b in zip(mixing(count, 0), mixing(count, 1))
    ]

    def step(index, _):
        f = index // tiles
        span = pl.ds(pl.multiple_of((index % tiles) * TILE, TILE), TILE)
        parts = []
        for dx in range(2):
            u = [ins[2 * dy + dx][f, span] for dy in range(4)]
            parts.append((u[0] + u[2], u[1] + u[3], u[0] - u[2], u[1] - u[3]))
        for ex in range(2):
            even, odd, even_next, odd_next = 0.0, 0.0, 0.0, 0.0
            for dx in range(2):
                kind = 0 if ex == dx else (1 if ex else 2)
                e0, e1, o0, o1 = mix[4 * kind : 4 * kind + 4]
                s0, s1, d0, d1 = parts[dx]
                even = even + (e0 * s0 + e1 * s1)
                odd = odd + (o0 * d0 + o1 * d1)
                even_next = even_next + (e1 * s0 + e0 * s1)
                odd_next = odd_next + (o1 * d0 - o0 * d1)
            outs[ex][f, span] = even + odd
            outs[4 + ex][f, span] = even - odd
            outs[2 + ex][f, span] = even_next + odd_next
            outs[6 + ex][f, span] = even_next - odd_next
        return 0

    lax.fori_loop(0, fields * tiles, step, 0, unroll=4)


def primitives(cells):
    density = cells[0] + cells[1]
    inverse = 1.0 / density
    vel_ax = cells[2] * inverse
    vel_circ = cells[3] * inverse
    vel_rad = cells[4] * inverse
    fraction = cells[6]
    gamma_term = fraction / (G_LIQ - 1.0) + (1.0 - fraction) / (G_GAS - 1.0)
    stiff_term = fraction * (G_LIQ * P_LIQ / (G_LIQ - 1.0))
    kinetic = 0.5 * density * (vel_ax * vel_ax + vel_circ * vel_circ + vel_rad * vel_rad)
    gamma_inv = 1.0 / gamma_term
    pressure = (cells[5] - kinetic - stiff_term) * gamma_inv
    sound_speed = jnp.sqrt(((1.0 + gamma_inv) * pressure + stiff_term * gamma_inv) * inverse)
    return vel_ax, vel_circ, pressure, sound_speed


def sharpen(lower_val, centre, upper_val, offset):
    average = 0.5 * (lower_val + upper_val)
    difference = upper_val - lower_val
    steepness = 2.0 * (centre - average) / (jnp.abs(difference) + EPSA)
    return average + 0.5 * difference * jnp.tanh(BETA * (steepness + offset))


def flux_kernel(
    source_ref,
    halo_ref,
    flag_ref,
    res_ref,
    coup_ref,
    inv_ref,
    v_ref,
    w_ref,
    keep_ref,
    send_ref,
    state_ref,
    sems,
):
    def fetch(i):
        return pltpu.make_async_copy(source_ref.at[0, :, i], state_ref.at[0, :, i], sems.at[i])

    for i in range(state_ref.shape[2]):
        fetch(i).start()

    planes = state_ref.shape[2]
    rows = state_ref.shape[3]
    last = planes - 1

    def plane(i, _):
        fetch(i).wait()
        row = pl.ds(i, 1)
        quad = (TILE // 2, state_ref.shape[4])
        cells = []
        for f in range(FIELDS):
            upper, lower = halo_ref[f, row], halo_ref[FIELDS + f, row]
            if f < FIELDS - 1:
                edge = [jnp.broadcast_to(upper, quad), jnp.broadcast_to(lower, quad)]
            else:
                next_upper = halo_ref[2 * FIELDS, row]
                next_lower = halo_ref[2 * FIELDS + 1, row]
                edge = [upper] + [next_upper] * 3 + [next_lower] * 3 + [lower]
            cells.append(jnp.concatenate([state_ref[0, f, i]] + edge, axis=0))
        edge = jnp.broadcast_to(halo_ref[EDGES - 1, row], (TILE, state_ref.shape[4]))
        flags = jnp.concatenate([flag_ref[i], edge], axis=0)
        total = rows + TILE

        def below(x, by=1):
            return pltpu.roll(x, by, 0)

        def above(x):
            return pltpu.roll(x, total - 1, 0)

        vel_ax, vel_circ, pressure, sound = primitives(cells)
        coup_ref[i] = -ALPHA * (jnp.abs(vel_ax) + sound)[:rows]
        wave = jnp.abs(vel_circ) + sound
        half_speed = 0.5 * jnp.maximum(below(wave), wave)
        fraction = cells[6]
        back1 = below(fraction)
        sharp_left = sharpen(below(fraction, 2), back1, fraction, 1.0)
        sharp_right = sharpen(back1, fraction, above(fraction), -1.0)
        flagged = flags > 0.5
        frac_left = jnp.where(flagged, sharp_left, back1)
        frac_right = jnp.where(flagged, sharp_right, fraction)
        for f in range(FIELDS):
            if f < 6:
                flux = cells[f] * vel_circ
                if f == 3:
                    flux = flux + pressure
                elif f == 5:
                    flux = flux + pressure * vel_circ
                mean = 0.5 * (below(flux) + flux)
                jump = cells[f] - below(cells[f])
            else:
                mean = 0.5 * (frac_left * below(vel_circ) + frac_right * vel_circ)
                jump = frac_right - frac_left
            face = mean - half_speed * jump
            res_ref[i, f] = (above(face) - face)[:rows]
        return 0

    lax.fori_loop(0, planes, plane, 0)

    core = core_index()
    tiles = rows // TILE // 2
    for target_ref, side in ((keep_ref, core), (send_ref, 1 - core)):

        def factor(t, _, target_ref=target_ref, side=side):
            span = pl.ds(pl.multiple_of((side * tiles + t) * TILE, TILE), TILE)
            place = pl.ds(pl.multiple_of(t * TILE, TILE), TILE)
            coup = [coup_ref[i, span] for i in range(planes)]
            inv, ratio, v = [], [], []
            for i in range(last):
                pivot = DIAG0 - 2.0 * coup[i]
                if i:
                    pivot = pivot - coup[i] * ratio[-1]
                inv.append(1.0 / pivot)
                ratio.append(coup[i] * inv[-1])
                v.append(inv[-1] if i == 0 else -(ratio[-1] * v[-1]))
                inv_ref[i, span] = inv[-1]
            v_next, w_next = v[-1], inv[-1]
            v_last, w_last = v_next * coup[0], w_next * coup[last - 1]
            for i in range(last - 1, -1, -1):
                if i < last - 1:
                    v_next = v[i] - ratio[i] * v_next
                    w_next = -(ratio[i] * w_next)
                v_first, w_first = v_next * coup[0], w_next * coup[last - 1]
                v_ref[i, span] = v_first
                w_ref[i, span] = w_first
            sep = coup[last]
            target_ref[0, place] = -(sep * v_last)
            target_ref[1, place] = DIAG0 - 2.0 * sep - sep * w_last
            target_ref[2, place] = sep
            target_ref[3, place] = v_first
            target_ref[4, place] = w_first
            return 0

        lax.fori_loop(0, tiles, factor, 0)


def pair_kernel(keep_ref, got_ref, pair_ref, raw_ref, ends_ref):
    lower_core = core_index() == 0
    lower_a, diag_a, sep_a, v_a, w_a = (
        jnp.where(lower_core, keep_ref[k], got_ref[k]) for k in range(COEFS)
    )
    lower_b, diag_b, sep_b, v_b, w_b = (
        jnp.where(lower_core, got_ref[k], keep_ref[k]) for k in range(COEFS)
    )
    inv = 1.0 / (diag_a - sep_a * v_b)
    v = inv * lower_a
    w = -(inv * sep_a * w_b)
    for k, x in enumerate((inv, sep_a, w_a, lower_b, v, w)):
        pair_ref[k] = x
    raw_ref[0] = diag_b - lower_b * w
    raw_ref[1] = -(lower_b * v)
    raw_ref[2] = sep_b
    ends_ref[0] = v_a - w_a * v
    ends_ref[1] = -(w_a * w)


def link_kernel(raw_ref, ends_ref, link_ref, edge_ref):
    sep = raw_ref[2]
    scale = 1.0 / (raw_ref[0] - sep * ends_ref[0])
    link_ref[0] = scale
    link_ref[1] = raw_ref[1] * scale
    link_ref[2] = -(sep * ends_ref[1]) * scale
    edge_ref[0] = sep * scale


def join_kernel(link_ref, edge_ref, out_ref):
    for k in range(3):
        out_ref[k] = link_ref[k]
    out_ref[3] = edge_ref[0]


def half_of(mine):
    core = core_index()
    return core if mine else 1 - core


def sweep_kernel(mine, res_ref, coup_ref, inv_ref, *refs):
    count = len(refs) - 3
    specs = refs[:count]
    y_ref, target_ref, right_ref = refs[count:]
    planes, fields, rows, _ = res_ref.shape
    last = planes - 1
    tiles = rows // TILE // 2
    side = half_of(mine)
    index = lax.axis_index("inst")
    ring = count // 2
    places = [
        2 * lax.rem(index // 2 + ring - dy, ring) + lax.rem(lax.rem(index, 2) + dx, 2)
        for dy, dx in slots(count)
    ]

    def step(t, _):
        span = pl.ds(pl.multiple_of((side * tiles + t) * TILE, TILE), TILE)
        place = pl.ds(pl.multiple_of(t * TILE, TILE), TILE)
        for f in range(fields):
            for i, spec_ref in zip(places, specs):
                right_ref[f, i] = -(res_ref[i, f, span] + spec_ref[f, span])
        coup = [coup_ref[i, span] for i in range(planes)]
        inv = [inv_ref[i, span] for i in range(last)]
        ratio = [coup[i] * inv[i] for i in range(last)]
        for f in range(fields):
            value = []
            for i in range(last):
                right = right_ref[f, i]
                if i:
                    right = right - coup[i] * value[-1]
                value.append(right * inv[i])
            y = value[-1]
            y_last = y
            y_ref[last - 1, f, place] = y
            for i in range(last - 2, -1, -1):
                y = value[i] - ratio[i] * y
                y_ref[i, f, place] = y
            target_ref[f, place] = y
            target_ref[fields + f, place] = right_ref[f, last] - coup[last] * y_last
        return 0

    lax.fori_loop(0, tiles, step, 0)


def merge_kernel(keep_ref, got_ref, pair_ref, link_ref, inner_ref, out_ref):
    fields = inner_ref.shape[0]
    rows = inner_ref.shape[1]
    lower_core = core_index() == 0

    def step(t, _):
        span = pl.ds(pl.multiple_of(t * TILE, TILE), TILE)
        inv, sep_a, first_a, lower_b = (pair_ref[k, span] for k in range(4))
        scale, lower, upper, edge = (link_ref[k, span] for k in range(4))
        for f in range(fields):
            keep_y, got_y = keep_ref[f, span], got_ref[f, span]
            keep_own, got_own = keep_ref[fields + f, span], got_ref[fields + f, span]
            y_a = jnp.where(lower_core, keep_y, got_y)
            y_b = jnp.where(lower_core, got_y, keep_y)
            own_a = jnp.where(lower_core, keep_own, got_own)
            own_b = jnp.where(lower_core, got_own, keep_own)
            inner = inv * (own_a - sep_a * y_b)
            inner_ref[f, span] = inner
            for k, x in (
                (f, scale * (own_b - lower_b * inner)),
                (fields + f, edge * (y_a - first_a * inner)),
            ):
                out_ref[2 * t, k] = x[0:4]
                out_ref[2 * t + 1, k] = x[4:8]
        for k, x in ((2 * fields, lower), (2 * fields + 1, upper)):
            out_ref[2 * t, k] = x[0:4]
            out_ref[2 * t + 1, k] = x[4:8]
        return 0

    lax.fori_loop(0, rows // TILE, step, 0)


def reduced_kernel(rhs_ref, out_ref):
    count = rhs_ref.shape[0]
    fields = out_ref.shape[1] // 2
    ratio = []
    values = []
    for p in range(count):
        lower, upper = rhs_ref[p, 2 * fields], rhs_ref[p, 2 * fields + 1]
        more = p + 1 < count
        inv = 1.0 / (1.0 - lower * ratio[-1]) if p else jnp.ones_like(lower)
        ratio.append(upper * inv)
        row = []
        for f in range(fields):
            right = rhs_ref[p, f]
            if more:
                right = right - rhs_ref[p + 1, fields + f]
            if p:
                right = right - lower * values[-1][f]
            row.append(right * inv)
        values.append(row)
    solved = values[-1]
    for p in range(count - 1, -1, -1):
        if p < count - 1:
            solved = [values[p][f] - ratio[p] * solved[f] for f in range(fields)]
        for f in range(fields):
            out_ref[p, fields + f] = solved[f]
            if p < count - 1:
                out_ref[p + 1, f] = solved[f]
    for f in range(fields):
        out_ref[0, f] = jnp.zeros_like(solved[f])


def expand_kernel(solved_ref, inner_ref, pair_ref, keep_ref, send_ref):
    fields, rows, _ = inner_ref.shape
    lower_core = core_index() == 0

    def step(t, _):
        span = pl.ds(pl.multiple_of(t * TILE, TILE), TILE)
        v, w = pair_ref[4, span], pair_ref[5, span]
        for f in range(fields):
            prev = jnp.concatenate([solved_ref[2 * t, f], solved_ref[2 * t + 1, f]], axis=0)
            own = jnp.concatenate(
                [solved_ref[2 * t, fields + f], solved_ref[2 * t + 1, fields + f]], axis=0
            )
            inner = inner_ref[f, span] - v * prev - w * own
            keep_ref[f, span] = jnp.where(lower_core, prev, inner)
            keep_ref[fields + f, span] = jnp.where(lower_core, inner, own)
            send_ref[f, span] = jnp.where(lower_core, inner, prev)
            send_ref[fields + f, span] = jnp.where(lower_core, own, inner)
        return 0

    lax.fori_loop(0, rows // TILE, step, 0)


def finish_kernel(mine, state_ref, v_ref, w_ref, y_ref, ends_ref, *refs):
    out_ref, block_ref, sems = refs[-3:]
    fields, planes, rows = state_ref.shape[1:4]
    last = planes - 1
    tiles = rows // TILE // 2
    side = half_of(mine)
    lines = pl.ds(pl.multiple_of(side * (rows // 2), rows // 2), rows // 2)
    copies = []
    for f in range(fields):

        def tile(t, _, f=f):
            span = pl.ds(pl.multiple_of((side * tiles + t) * TILE, TILE), TILE)
            place = pl.ds(pl.multiple_of(t * TILE, TILE), TILE)
            prev, own = ends_ref[f, place], ends_ref[fields + f, place]
            for i in range(last):
                delta = y_ref[i, f, place] - v_ref[i, span] * prev - w_ref[i, span] * own
                block_ref[f, i, place] = state_ref[0, f, i, span] + delta
            block_ref[f, last, place] = state_ref[0, f, last, span] + own
            return 0

        lax.fori_loop(0, tiles, tile, 0, unroll=True)
        copy = pltpu.make_async_copy(block_ref.at[f], out_ref.at[0, f, :, lines], sems.at[f])
        copy.start()
        copies.append(copy)
    for copy in copies:
        copy.wait()


def finish(mine, state, v, w, y, ends, partial=None):
    fields, planes, rows, lanes = state.shape[1:]
    hbm = pl.BlockSpec(memory_space=pltpu.HBM)
    operands = [state, v, w, y, ends]
    specs = [VMEM] * len(operands)
    aliases = {}
    if partial is not None:
        aliases = {len(operands): 0}
        operands.append(partial)
        specs.append(hbm)
    return pl.pallas_call(
        functools.partial(finish_kernel, mine),
        out_shape=jax.ShapeDtypeStruct(state.shape, jnp.float32),
        in_specs=specs,
        out_specs=hbm,
        scratch_shapes=[
            pltpu.VMEM((fields, planes, rows // 2, lanes), jnp.float32),
            pltpu.SemaphoreType.DMA((fields,)),
        ],
        input_output_aliases=aliases,
        compiler_params=pltpu.CompilerParams(vmem_limit_bytes=state.size * 12),
        cost_estimate=pl.CostEstimate(
            flops=state.size * 2, bytes_accessed=state.size * 6, transcendentals=0
        ),
    )(*operands)


def flux_parts(state, halo, flag_cells):
    fields, planes, rows, lanes = state.shape[1:]
    grid = (rows, lanes)
    shapes = [
        (planes, fields) + grid,
        (planes,) + grid,
        (planes - 1,) + grid,
        (planes - 1,) + grid,
        (planes - 1,) + grid,
        (COEFS, rows // 2, lanes),
        (COEFS, rows // 2, lanes),
        state.shape,
    ]
    return pl.pallas_call(
        flux_kernel,
        out_shape=[jax.ShapeDtypeStruct(x, jnp.float32) for x in shapes],
        in_specs=[pl.BlockSpec(memory_space=pltpu.HBM), VMEM, VMEM],
        out_specs=[VMEM] * len(shapes),
        scratch_shapes=[pltpu.SemaphoreType.DMA((planes,))],
        compiler_params=pltpu.CompilerParams(vmem_limit_bytes=state.size * 12),
        cost_estimate=pl.CostEstimate(
            flops=state.size * 60, bytes_accessed=state.size * 16, transcendentals=0
        ),
    )(pltpu.with_memory_space_constraint(state, pltpu.HBM), halo, flag_cells)


def exchange(x, axis, groups=None):
    return lax.all_to_all(x, axis, 0, 0, tiled=True, axis_index_groups=groups)


def body(flow_state, thinc_flags):
    own = flow_state[0]
    planes, rows, lanes = own.shape[1:]
    instances = lax.axis_size("inst")
    ax_count = lax.axis_size("ax")
    circ_count = lax.axis_size("circ")
    chips = ax_count // 2
    half = rows // 2
    piece = half // chips

    swap = [(i, i ^ 1) for i in range(ax_count)]
    groups = [list(range(c, ax_count, 2)) for c in range(2)]

    def partner(x):
        return lax.ppermute(x, "ax", swap)

    def neighbour(x, by):
        moves = [(i, i + 2 * by) for i in range(ax_count) if 0 <= i + 2 * by < ax_count]
        return lax.ppermute(x, "ax", moves)

    steps = slots(instances)
    order = ORDER
    rest = tuple(k for k in range(instances) if k != order[0])
    blocks = [None] * instances
    early = pick_first(flow_state, instances, order[0])
    *others, edges = pick_rest(flow_state, thinc_flags, early, instances, rest)
    blocks[order[0]] = early
    for k, block in zip(rest, others):
        blocks[k] = block
    halo = lax.ppermute(
        edges, "circ", [(i, (i + 1) % circ_count) for i in range(circ_count)]
    )
    for k in order:
        blocks[k] = lax.ppermute(blocks[k], "inst", route(*steps[k], instances))
    flags = (thinc_flags[0] > 0).astype(jnp.float32)
    flag_cells = jnp.broadcast_to(flags[:, :, None], (planes, rows, lanes))

    res, coup, inv, v, w, keep, send, held_state = flux_parts(flow_state, halo, flag_cells)

    thin = (half, lanes)
    pair, raw, ends = call(
        pair_kernel, [(6,) + thin, (3,) + thin, (2,) + thin], keep, partner(send)
    )
    ends = neighbour(ends, -1)
    link, edge = call(link_kernel, [(3,) + thin, (1,) + thin], raw, ends)
    specs = call(spectral_kernel, [blocks[0].shape] * instances, *blocks, flops=own.size * 9)
    for k in order:
        specs[k] = lax.ppermute(specs[k], "inst", route(*steps[k], instances))
    edge = neighbour(edge, 1)
    (link,) = call(join_kernel, [(4,) + thin], link, edge)
    shapes = [(planes - 1, FIELDS, half, lanes), (2 * FIELDS, half, lanes)]
    parts = []
    for mine in (False, True):
        parts.append(
            call(
                functools.partial(sweep_kernel, mine),
                shapes,
                res,
                coup,
                inv,
                *specs,
                flops=own.size * 4,
                scratch=[(FIELDS, planes, TILE, lanes)],
            )
        )
    (y_other, send), (y_mine, keep) = parts
    inner, rhs = call(
        merge_kernel,
        [(FIELDS, half, lanes), (chips, 2 * FIELDS + 2, piece, lanes)],
        keep,
        partner(send),
        pair,
        link,
        flops=send.size * 4,
    )
    rhs = exchange(rhs, "ax", groups)
    (solved,) = call(
        reduced_kernel, [(chips, 2 * FIELDS, piece, lanes)], rhs, flops=rhs.size * 8
    )
    solved = exchange(solved, "ax", groups)
    keep, send = call(
        expand_kernel,
        [(2 * FIELDS, half, lanes)] * 2,
        solved,
        inner,
        pair,
        flops=send.size * 4,
    )
    got = partner(send)
    out = finish(True, held_state, v, w, y_mine, keep)
    return finish(False, held_state, v, w, y_other, got, out)


def solution(mesh):
    return jax.shard_map(
        body,
        mesh=mesh,
        in_specs=(P("inst", None, "ax", "circ", None), P("inst", "ax", "circ")),
        out_specs=P("inst", None, "ax", "circ", None),
        check_vma=False,
    )
```

```python
import functools
import math

import jax
import jax.numpy as jnp
from jax import lax
from jax.experimental import pallas as pl
from jax.experimental.pallas import tpu as pltpu
from jax.sharding import PartitionSpec as P


G_LIQ = 4.4
P_LIQ = 6.0
G_GAS = 1.4
BETA = 1.6
EPSA = 0.1
ALPHA = 4.0
DIAG0 = 0.016
OMEGA = 1.0
NU_T = 0.25

FIELDS = 7
ORDER = (5, 7, 3, 4, 1, 2, 6)
EDGES = 2 * FIELDS + 3
COEFS = 5
TILE = 8


VMEM = pl.BlockSpec(memory_space=pltpu.VMEM)


def spectral_weights(count):
    table = []
    for k in range(count):
        if k == 0:
            first, second = 0.0, -(count * count + 2) / 12.0
        else:
            sign = 1.0 if k % 2 == 0 else -1.0
            angle = math.pi * k / count
            first = 0.5 * sign * math.cos(angle) / math.sin(angle)
            second = -sign / (2.0 * math.sin(angle) ** 2)
        table.append(OMEGA * first - NU_T * OMEGA * OMEGA * second)
    return table


def core_index():
    return lax.rem(lax.axis_index("ax"), 2)


def call(kernel, outs, *operands, flops=0, scratch=()):
    outs = [jax.ShapeDtypeStruct(shape, jnp.float32) for shape in outs]
    total = sum(x.size * 4 for x in operands) + sum(x.size * 4 for x in outs)
    run = pl.pallas_call(
        kernel,
        out_shape=outs,
        in_specs=[VMEM] * len(operands),
        out_specs=[VMEM] * len(outs),
        scratch_shapes=[pltpu.VMEM(x, jnp.float32) for x in scratch],
        compiler_params=pltpu.CompilerParams(
            vmem_limit_bytes=total + sum(math.prod(x) * 4 for x in scratch) + (2 << 20)
        ),
        cost_estimate=pl.CostEstimate(flops=flops, bytes_accessed=total, transcendentals=0),
    )
    return list(run(*operands))


def slots(count):
    steps = [(dy, dx) for dy in range(count // 2) for dx in range(2)]
    return steps


def route(dy, dx, count):
    ring = count // 2
    return [(i, 2 * ((i // 2 + dy) % ring) + ((i % 2) ^ dx)) for i in range(count)]


def places_of(count, chosen):
    index = lax.axis_index("inst")
    ring = count // 2
    steps = slots(count)
    return [
        2 * lax.rem(index // 2 + steps[k][0], ring) + lax.rem(lax.rem(index, 2) + steps[k][1], 2)
        for k in chosen
    ]


def first_kernel(count, chosen, state_ref, out_ref, sem):
    (place,) = places_of(count, (chosen,))
    copy = pltpu.make_async_copy(state_ref.at[0, :, place], out_ref, sem)
    copy.start()
    copy.wait()


def rest_kernel(count, chosen, state_ref, flag_ref, early_ref, *refs):
    outs = refs[: len(chosen)]
    edge_ref, held_ref, sems = refs[len(chosen) :]
    fields, rows = state_ref.shape[1], state_ref.shape[3]
    early = next(k for k in range(count) if k not in chosen)
    (early_place,), places = places_of(count, (early,)), places_of(count, chosen)
    copies = [
        pltpu.make_async_copy(state_ref.at[0, :, place], out, sems.at[k])
        for k, (place, out) in enumerate(zip(places, outs))
    ]
    for copy in copies:
        copy.start()
    flag_copy = pltpu.make_async_copy(flag_ref, held_ref, sems.at[len(chosen)])
    flag_copy.start()

    def edges(place, block):
        row = pl.ds(place, 1)
        for f in range(fields):
            edge_ref[f, row] = block[f, 0:1]
            edge_ref[fields + f, row] = block[f, rows - 1 : rows]
        edge_ref[2 * fields, row] = block[fields - 1, 1:2]
        edge_ref[2 * fields + 1, row] = block[fields - 1, rows - 2 : rows - 1]

    edges(early_place, early_ref)
    flag_copy.wait()
    flags = (held_ref[0] > 0).astype(jnp.float32)
    edge_ref[EDGES - 1] = jnp.broadcast_to(flags[:, 0:1], edge_ref.shape[1:])
    for copy, place, out in zip(copies, places, outs):
        copy.wait()
        edges(place, out)


def pick_first(state, count, chosen):
    _, fields, _, rows, lanes = state.shape
    return pl.pallas_call(
        functools.partial(first_kernel, count, chosen),
        out_shape=jax.ShapeDtypeStruct((fields, rows, lanes), jnp.float32),
        in_specs=[pl.BlockSpec(memory_space=pltpu.HBM)],
        out_specs=VMEM,
        scratch_shapes=[pltpu.SemaphoreType.DMA],
        compiler_params=pltpu.CompilerParams(vmem_limit_bytes=4 << 20),
        cost_estimate=pl.CostEstimate(
            flops=0, bytes_accessed=fields * rows * lanes * 8, transcendentals=0
        ),
    )(pltpu.with_memory_space_constraint(state, pltpu.HBM))


def pick_rest(state, flags, early, count, chosen):
    _, fields, planes, rows, lanes = state.shape
    shapes = [(fields, rows, lanes)] * len(chosen) + [(EDGES, planes, lanes)]
    hbm = pl.BlockSpec(memory_space=pltpu.HBM)
    return pl.pallas_call(
        functools.partial(rest_kernel, count, chosen),
        out_shape=[jax.ShapeDtypeStruct(x, jnp.float32) for x in shapes],
        in_specs=[hbm, hbm, VMEM],
        out_specs=[VMEM] * len(shapes),
        scratch_shapes=[
            pltpu.VMEM(flags.shape, flags.dtype),
            pltpu.SemaphoreType.DMA((len(chosen) + 1,)),
        ],
        compiler_params=pltpu.CompilerParams(vmem_limit_bytes=state.size * 4 + (3 << 20)),
        cost_estimate=pl.CostEstimate(flops=0, bytes_accessed=state.size * 8, transcendentals=0),
    )(*(pltpu.with_memory_space_constraint(x, pltpu.HBM) for x in (state, flags)), early)


def mixing(count, parity):
    weights = spectral_weights(count)
    table = []
    for shift in (0, 1 - 2 * parity, 2 * parity - 1):
        g = [weights[(2 * a + shift) % count] for a in range(4)]
        table += [0.5 * (g[0] + g[2]), 0.5 * (g[1] + g[3])]
        table += [0.5 * (g[0] - g[2]), 0.5 * (g[1] - g[3])]
    return table


def spectral_kernel(*refs):
    count = len(refs) // 2
    ins, outs = refs[:count], refs[count:]
    fields, rows, _ = ins[0].shape
    tiles = rows // TILE
    first = lax.rem(lax.axis_index("inst"), 2) == 0
    mix = [
        jnp.where(first, jnp.float32(a), jnp.float32(b))
        for a, b in zip(mixing(count, 0), mixing(count, 1))
    ]

    def step(index, _):
        f = index // tiles
        span = pl.ds(pl.multiple_of((index % tiles) * TILE, TILE), TILE)
        parts = []
        for dx in range(2):
            u = [ins[2 * dy + dx][f, span] for dy in range(4)]
            parts.append((u[0] + u[2], u[1] + u[3], u[0] - u[2], u[1] - u[3]))
        for ex in range(2):
            even, odd, even_next, odd_next = 0.0, 0.0, 0.0, 0.0
            for dx in range(2):
                kind = 0 if ex == dx else (1 if ex else 2)
                e0, e1, o0, o1 = mix[4 * kind : 4 * kind + 4]
                s0, s1, d0, d1 = parts[dx]
                even = even + (e0 * s0 + e1 * s1)
                odd = odd + (o0 * d0 + o1 * d1)
                even_next = even_next + (e1 * s0 + e0 * s1)
                odd_next = odd_next + (o1 * d0 - o0 * d1)
            outs[ex][f, span] = even + odd
            outs[4 + ex][f, span] = even - odd
            outs[2 + ex][f, span] = even_next + odd_next
            outs[6 + ex][f, span] = even_next - odd_next
        return 0

    lax.fori_loop(0, fields * tiles, step, 0, unroll=4)


def primitives(cells):
    density = cells[0] + cells[1]
    inverse = 1.0 / density
    vel_ax = cells[2] * inverse
    vel_circ = cells[3] * inverse
    vel_rad = cells[4] * inverse
    fraction = cells[6]
    gamma_term = fraction / (G_LIQ - 1.0) + (1.0 - fraction) / (G_GAS - 1.0)
    stiff_term = fraction * (G_LIQ * P_LIQ / (G_LIQ - 1.0))
    kinetic = 0.5 * density * (vel_ax * vel_ax + vel_circ * vel_circ + vel_rad * vel_rad)
    gamma_inv = 1.0 / gamma_term
    pressure = (cells[5] - kinetic - stiff_term) * gamma_inv
    sound_speed = jnp.sqrt(((1.0 + gamma_inv) * pressure + stiff_term * gamma_inv) * inverse)
    return vel_ax, vel_circ, pressure, sound_speed


def sharpen(lower_val, centre, upper_val, offset):
    average = 0.5 * (lower_val + upper_val)
    difference = upper_val - lower_val
    steepness = 2.0 * (centre - average) / (jnp.abs(difference) + EPSA)
    return average + 0.5 * difference * jnp.tanh(BETA * (steepness + offset))


def flux_kernel(
    source_ref,
    halo_ref,
    flag_ref,
    res_ref,
    coup_ref,
    inv_ref,
    v_ref,
    w_ref,
    keep_ref,
    send_ref,
    state_ref,
    sems,
):
    def fetch(i):
        return pltpu.make_async_copy(source_ref.at[0, :, i], state_ref.at[0, :, i], sems.at[i])

    for i in range(state_ref.shape[2]):
        fetch(i).start()

    planes = state_ref.shape[2]
    rows = state_ref.shape[3]
    last = planes - 1

    def plane(i, _):
        fetch(i).wait()
        row = pl.ds(i, 1)
        quad = (TILE // 2, state_ref.shape[4])
        cells = []
        for f in range(FIELDS):
            upper, lower = halo_ref[f, row], halo_ref[FIELDS + f, row]
            if f < FIELDS - 1:
                edge = [jnp.broadcast_to(upper, quad), jnp.broadcast_to(lower, quad)]
            else:
                next_upper = halo_ref[2 * FIELDS, row]
                next_lower = halo_ref[2 * FIELDS + 1, row]
                edge = [upper] + [next_upper] * 3 + [next_lower] * 3 + [lower]
            cells.append(jnp.concatenate([state_ref[0, f, i]] + edge, axis=0))
        edge = jnp.broadcast_to(halo_ref[EDGES - 1, row], (TILE, state_ref.shape[4]))
        flags = jnp.concatenate([flag_ref[i], edge], axis=0)
        total = rows + TILE

        def below(x, by=1):
            return pltpu.roll(x, by, 0)

        def above(x):
            return pltpu.roll(x, total - 1, 0)

        vel_ax, vel_circ, pressure, sound = primitives(cells)
        coup_ref[i] = -ALPHA * (jnp.abs(vel_ax) + sound)[:rows]
        wave = jnp.abs(vel_circ) + sound
        half_speed = 0.5 * jnp.maximum(below(wave), wave)
        fraction = cells[6]
        back1 = below(fraction)
        sharp_left = sharpen(below(fraction, 2), back1, fraction, 1.0)
        sharp_right = sharpen(back1, fraction, above(fraction), -1.0)
        flagged = flags > 0.5
        frac_left = jnp.where(flagged, sharp_left, back1)
        frac_right = jnp.where(flagged, sharp_right, fraction)
        for f in range(FIELDS):
            if f < 6:
                flux = cells[f] * vel_circ
                if f == 3:
                    flux = flux + pressure
                elif f == 5:
                    flux = flux + pressure * vel_circ
                mean = 0.5 * (below(flux) + flux)
                jump = cells[f] - below(cells[f])
            else:
                mean = 0.5 * (frac_left * below(vel_circ) + frac_right * vel_circ)
                jump = frac_right - frac_left
            face = mean - half_speed * jump
            res_ref[i, f] = (above(face) - face)[:rows]
        return 0

    lax.fori_loop(0, planes, plane, 0)

    core = core_index()
    tiles = rows // TILE // 2
    for target_ref, side in ((keep_ref, core), (send_ref, 1 - core)):

        def factor(t, _, target_ref=target_ref, side=side):
            span = pl.ds(pl.multiple_of((side * tiles + t) * TILE, TILE), TILE)
            place = pl.ds(pl.multiple_of(t * TILE, TILE), TILE)
            coup = [coup_ref[i, span] for i in range(planes)]
            inv, ratio, v = [], [], []
            for i in range(last):
                pivot = DIAG0 - 2.0 * coup[i]
                if i:
                    pivot = pivot - coup[i] * ratio[-1]
                inv.append(1.0 / pivot)
                ratio.append(coup[i] * inv[-1])
                v.append(inv[-1] if i == 0 else -(ratio[-1] * v[-1]))
                inv_ref[i, span] = inv[-1]
            v_next, w_next = v[-1], inv[-1]
            v_last, w_last = v_next * coup[0], w_next * coup[last - 1]
            for i in range(last - 1, -1, -1):
                if i < last - 1:
                    v_next = v[i] - ratio[i] * v_next
                    w_next = -(ratio[i] * w_next)
                v_first, w_first = v_next * coup[0], w_next * coup[last - 1]
                v_ref[i, span] = v_first
                w_ref[i, span] = w_first
            sep = coup[last]
            target_ref[0, place] = -(sep * v_last)
            target_ref[1, place] = DIAG0 - 2.0 * sep - sep * w_last
            target_ref[2, place] = sep
            target_ref[3, place] = v_first
            target_ref[4, place] = w_first
            return 0

        lax.fori_loop(0, tiles, factor, 0)


def pair_kernel(keep_ref, got_ref, pair_ref, raw_ref, ends_ref):
    lower_core = core_index() == 0
    lower_a, diag_a, sep_a, v_a, w_a = (
        jnp.where(lower_core, keep_ref[k], got_ref[k]) for k in range(COEFS)
    )
    lower_b, diag_b, sep_b, v_b, w_b = (
        jnp.where(lower_core, got_ref[k], keep_ref[k]) for k in range(COEFS)
    )
    inv = 1.0 / (diag_a - sep_a * v_b)
    v = inv * lower_a
    w = -(inv * sep_a * w_b)
    for k, x in enumerate((inv, sep_a, w_a, lower_b, v, w)):
        pair_ref[k] = x
    raw_ref[0] = diag_b - lower_b * w
    raw_ref[1] = -(lower_b * v)
    raw_ref[2] = sep_b
    ends_ref[0] = v_a - w_a * v
    ends_ref[1] = -(w_a * w)


def link_kernel(raw_ref, ends_ref, link_ref, edge_ref, table_ref):
    count, _, piece, _ = table_ref.shape
    sep = raw_ref[2]
    scale = 1.0 / (raw_ref[0] - sep * ends_ref[0])
    link_ref[0] = scale
    edge_ref[0] = sep * scale
    lower, upper = raw_ref[1] * scale, -(sep * ends_ref[1]) * scale
    for q in range(count):
        table_ref[q, 0] = lower[q * piece : (q + 1) * piece]
        table_ref[q, 1] = upper[q * piece : (q + 1) * piece]


def factor_kernel(table_ref, out_ref):
    ratio = None
    for p in range(table_ref.shape[0]):
        lower, upper = table_ref[p, 0], table_ref[p, 1]
        inv = 1.0 / (1.0 - lower * ratio) if p else jnp.ones_like(lower)
        ratio = upper * inv
        out_ref[p, 0] = lower
        out_ref[p, 1] = inv
        out_ref[p, 2] = ratio


def join_kernel(link_ref, edge_ref, out_ref):
    out_ref[0] = link_ref[0]
    out_ref[1] = edge_ref[0]


def half_of(mine):
    core = core_index()
    return core if mine else 1 - core


def sweep_kernel(mine, res_ref, coup_ref, inv_ref, *refs):
    count = len(refs) - 3
    specs = refs[:count]
    y_ref, target_ref, right_ref = refs[count:]
    planes, fields, rows, _ = res_ref.shape
    last = planes - 1
    tiles = rows // TILE // 2
    side = half_of(mine)
    index = lax.axis_index("inst")
    ring = count // 2
    places = [
        2 * lax.rem(index // 2 + ring - dy, ring) + lax.rem(lax.rem(index, 2) + dx, 2)
        for dy, dx in slots(count)
    ]

    def step(t, _):
        span = pl.ds(pl.multiple_of((side * tiles + t) * TILE, TILE), TILE)
        place = pl.ds(pl.multiple_of(t * TILE, TILE), TILE)
        for f in range(fields):
            for i, spec_ref in zip(places, specs):
                right_ref[f, i] = -(res_ref[i, f, span] + spec_ref[f, span])
        coup = [coup_ref[i, span] for i in range(planes)]
        inv = [inv_ref[i, span] for i in range(last)]
        ratio = [coup[i] * inv[i] for i in range(last)]
        for f in range(fields):
            value = []
            for i in range(last):
                right = right_ref[f, i]
                if i:
                    right = right - coup[i] * value[-1]
                value.append(right * inv[i])
            y = value[-1]
            y_last = y
            y_ref[last - 1, f, place] = y
            for i in range(last - 2, -1, -1):
                y = value[i] - ratio[i] * y
                y_ref[i, f, place] = y
            target_ref[f, place] = y
            target_ref[fields + f, place] = right_ref[f, last] - coup[last] * y_last
        return 0

    lax.fori_loop(0, tiles, step, 0)


def merge_kernel(keep_ref, got_ref, pair_ref, link_ref, inner_ref, out_ref):
    fields = inner_ref.shape[0]
    rows = inner_ref.shape[1]
    lower_core = core_index() == 0

    def step(t, _):
        span = pl.ds(pl.multiple_of(t * TILE, TILE), TILE)
        inv, sep_a, first_a, lower_b = (pair_ref[k, span] for k in range(4))
        scale, edge = link_ref[0, span], link_ref[1, span]
        for f in range(fields):
            keep_y, got_y = keep_ref[f, span], got_ref[f, span]
            keep_own, got_own = keep_ref[fields + f, span], got_ref[fields + f, span]
            y_a = jnp.where(lower_core, keep_y, got_y)
            y_b = jnp.where(lower_core, got_y, keep_y)
            own_a = jnp.where(lower_core, keep_own, got_own)
            own_b = jnp.where(lower_core, got_own, keep_own)
            inner = inv * (own_a - sep_a * y_b)
            inner_ref[f, span] = inner
            for k, x in (
                (f, scale * (own_b - lower_b * inner)),
                (fields + f, edge * (y_a - first_a * inner)),
            ):
                out_ref[2 * t, k] = x[0:4]
                out_ref[2 * t + 1, k] = x[4:8]
        return 0

    lax.fori_loop(0, rows // TILE, step, 0)


def reduced_kernel(table_ref, rhs_ref, out_ref):
    count = rhs_ref.shape[0]
    fields = out_ref.shape[1] // 2
    ratio = [table_ref[p, 2] for p in range(count)]
    values = []
    for p in range(count):
        lower, inv = table_ref[p, 0], table_ref[p, 1]
        row = []
        for f in range(fields):
            right = rhs_ref[p, f]
            if p + 1 < count:
                right = right - rhs_ref[p + 1, fields + f]
            if p:
                right = right - lower * values[-1][f]
            row.append(right * inv)
        values.append(row)
    solved = values[-1]
    for p in range(count - 1, -1, -1):
        if p < count - 1:
            solved = [values[p][f] - ratio[p] * solved[f] for f in range(fields)]
        for f in range(fields):
            out_ref[p, fields + f] = solved[f]
            if p < count - 1:
                out_ref[p + 1, f] = solved[f]
    for f in range(fields):
        out_ref[0, f] = jnp.zeros_like(solved[f])


def expand_kernel(solved_ref, inner_ref, pair_ref, keep_ref, send_ref):
    fields, rows, _ = inner_ref.shape
    lower_core = core_index() == 0

    def step(t, _):
        span = pl.ds(pl.multiple_of(t * TILE, TILE), TILE)
        v, w = pair_ref[4, span], pair_ref[5, span]
        for f in range(fields):
            prev = jnp.concatenate([solved_ref[2 * t, f], solved_ref[2 * t + 1, f]], axis=0)
            own = jnp.concatenate(
                [solved_ref[2 * t, fields + f], solved_ref[2 * t + 1, fields + f]], axis=0
            )
            inner = inner_ref[f, span] - v * prev - w * own
            keep_ref[f, span] = jnp.where(lower_core, prev, inner)
            keep_ref[fields + f, span] = jnp.where(lower_core, inner, own)
            send_ref[f, span] = jnp.where(lower_core, inner, prev)
            send_ref[fields + f, span] = jnp.where(lower_core, own, inner)
        return 0

    lax.fori_loop(0, rows // TILE, step, 0)


def finish_kernel(mine, state_ref, v_ref, w_ref, y_ref, ends_ref, *refs):
    out_ref, block_ref, sems = refs[-3:]
    fields, planes, rows = state_ref.shape[1:4]
    last = planes - 1
    tiles = rows // TILE // 2
    side = half_of(mine)
    lines = pl.ds(pl.multiple_of(side * (rows // 2), rows // 2), rows // 2)
    copies = []
    for f in range(fields):

        def tile(t, _, f=f):
            span = pl.ds(pl.multiple_of((side * tiles + t) * TILE, TILE), TILE)
            place = pl.ds(pl.multiple_of(t * TILE, TILE), TILE)
            prev, own = ends_ref[f, place], ends_ref[fields + f, place]
            for i in range(last):
                delta = y_ref[i, f, place] - v_ref[i, span] * prev - w_ref[i, span] * own
                block_ref[f, i, place] = state_ref[0, f, i, span] + delta
            block_ref[f, last, place] = state_ref[0, f, last, span] + own
            return 0

        lax.fori_loop(0, tiles, tile, 0, unroll=True)
        copy = pltpu.make_async_copy(block_ref.at[f], out_ref.at[0, f, :, lines], sems.at[f])
        copy.start()
        copies.append(copy)
    for copy in copies:
        copy.wait()


def finish(mine, state, v, w, y, ends, partial=None):
    fields, planes, rows, lanes = state.shape[1:]
    hbm = pl.BlockSpec(memory_space=pltpu.HBM)
    operands = [state, v, w, y, ends]
    specs = [VMEM] * len(operands)
    aliases = {}
    if partial is not None:
        aliases = {len(operands): 0}
        operands.append(partial)
        specs.append(hbm)
    return pl.pallas_call(
        functools.partial(finish_kernel, mine),
        out_shape=jax.ShapeDtypeStruct(state.shape, jnp.float32),
        in_specs=specs,
        out_specs=hbm,
        scratch_shapes=[
            pltpu.VMEM((fields, planes, rows // 2, lanes), jnp.float32),
            pltpu.SemaphoreType.DMA((fields,)),
        ],
        input_output_aliases=aliases,
        compiler_params=pltpu.CompilerParams(vmem_limit_bytes=state.size * 12),
        cost_estimate=pl.CostEstimate(
            flops=state.size * 2, bytes_accessed=state.size * 6, transcendentals=0
        ),
    )(*operands)


def flux_parts(state, halo, flag_cells):
    fields, planes, rows, lanes = state.shape[1:]
    grid = (rows, lanes)
    shapes = [
        (planes, fields) + grid,
        (planes,) + grid,
        (planes - 1,) + grid,
        (planes - 1,) + grid,
        (planes - 1,) + grid,
        (COEFS, rows // 2, lanes),
        (COEFS, rows // 2, lanes),
        state.shape,
    ]
    return pl.pallas_call(
        flux_kernel,
        out_shape=[jax.ShapeDtypeStruct(x, jnp.float32) for x in shapes],
        in_specs=[pl.BlockSpec(memory_space=pltpu.HBM), VMEM, VMEM],
        out_specs=[VMEM] * len(shapes),
        scratch_shapes=[pltpu.SemaphoreType.DMA((planes,))],
        compiler_params=pltpu.CompilerParams(vmem_limit_bytes=state.size * 12),
        cost_estimate=pl.CostEstimate(
            flops=state.size * 60, bytes_accessed=state.size * 16, transcendentals=0
        ),
    )(pltpu.with_memory_space_constraint(state, pltpu.HBM), halo, flag_cells)


def exchange(x, axis, groups=None):
    return lax.all_to_all(x, axis, 0, 0, tiled=True, axis_index_groups=groups)


def body(flow_state, thinc_flags):
    own = flow_state[0]
    planes, rows, lanes = own.shape[1:]
    instances = lax.axis_size("inst")
    ax_count = lax.axis_size("ax")
    circ_count = lax.axis_size("circ")
    chips = ax_count // 2
    half = rows // 2
    piece = half // chips

    swap = [(i, i ^ 1) for i in range(ax_count)]
    groups = [list(range(c, ax_count, 2)) for c in range(2)]

    def partner(x):
        return lax.ppermute(x, "ax", swap)

    def neighbour(x, by):
        moves = [(i, i + 2 * by) for i in range(ax_count) if 0 <= i + 2 * by < ax_count]
        return lax.ppermute(x, "ax", moves)

    steps = slots(instances)
    order = ORDER
    rest = tuple(k for k in range(instances) if k != order[0])
    blocks = [None] * instances
    early = pick_first(flow_state, instances, order[0])
    *others, edges = pick_rest(flow_state, thinc_flags, early, instances, rest)
    blocks[order[0]] = early
    for k, block in zip(rest, others):
        blocks[k] = block
    halo = lax.ppermute(
        edges, "circ", [(i, (i + 1) % circ_count) for i in range(circ_count)]
    )
    for k in order:
        blocks[k] = lax.ppermute(blocks[k], "inst", route(*steps[k], instances))
    flags = (thinc_flags[0] > 0).astype(jnp.float32)
    flag_cells = jnp.broadcast_to(flags[:, :, None], (planes, rows, lanes))

    res, coup, inv, v, w, keep, send, held_state = flux_parts(flow_state, halo, flag_cells)

    thin = (half, lanes)
    pair, raw, ends = call(
        pair_kernel, [(6,) + thin, (3,) + thin, (2,) + thin], keep, partner(send)
    )
    ends = neighbour(ends, -1)
    link, edge, table = call(
        link_kernel, [(1,) + thin, (1,) + thin, (chips, 2, piece, lanes)], raw, ends
    )
    specs = call(spectral_kernel, [blocks[0].shape] * instances, *blocks, flops=own.size * 9)
    for k in order:
        specs[k] = lax.ppermute(specs[k], "inst", route(*steps[k], instances))
    table = exchange(table, "ax", groups)
    (table,) = call(factor_kernel, [(chips, 3, piece, lanes)], table)
    edge = neighbour(edge, 1)
    (link,) = call(join_kernel, [(2,) + thin], link, edge)
    shapes = [(planes - 1, FIELDS, half, lanes), (2 * FIELDS, half, lanes)]
    parts = []
    for mine in (False, True):
        parts.append(
            call(
                functools.partial(sweep_kernel, mine),
                shapes,
                res,
                coup,
                inv,
                *specs,
                flops=own.size * 4,
                scratch=[(FIELDS, planes, TILE, lanes)],
            )
        )
    (y_other, send), (y_mine, keep) = parts
    inner, rhs = call(
        merge_kernel,
        [(FIELDS, half, lanes), (chips, 2 * FIELDS, piece, lanes)],
        keep,
        partner(send),
        pair,
        link,
        flops=send.size * 4,
    )
    rhs = exchange(rhs, "ax", groups)
    (solved,) = call(
        reduced_kernel, [(chips, 2 * FIELDS, piece, lanes)], table, rhs, flops=rhs.size * 8
    )
    solved = exchange(solved, "ax", groups)
    keep, send = call(
        expand_kernel,
        [(2 * FIELDS, half, lanes)] * 2,
        solved,
        inner,
        pair,
        flops=send.size * 4,
    )
    got = partner(send)
    out = finish(True, held_state, v, w, y_mine, keep)
    return finish(False, held_state, v, w, y_other, got, out)


def solution(mesh):
    return jax.shard_map(
        body,
        mesh=mesh,
        in_specs=(P("inst", None, "ax", "circ", None), P("inst", "ax", "circ")),
        out_specs=P("inst", None, "ax", "circ", None),
        check_vma=False,
    )
```

```python
import functools
import math

import jax
import jax.numpy as jnp
from jax import lax
from jax.experimental import pallas as pl
from jax.experimental.pallas import tpu as pltpu
from jax.sharding import PartitionSpec as P


G_LIQ = 4.4
P_LIQ = 6.0
G_GAS = 1.4
BETA = 1.6
EPSA = 0.1
ALPHA = 4.0
DIAG0 = 0.016
OMEGA = 1.0
NU_T = 0.25

FIELDS = 7
ORDER = (5, 7, 3, 4, 1, 2, 6)
RETURN = (3, 4, 5, 7, 1, 2, 6)
EDGES = 2 * FIELDS + 3
COEFS = 5
TILE = 8


VMEM = pl.BlockSpec(memory_space=pltpu.VMEM)


def spectral_weights(count):
    table = []
    for k in range(count):
        if k == 0:
            first, second = 0.0, -(count * count + 2) / 12.0
        else:
            sign = 1.0 if k % 2 == 0 else -1.0
            angle = math.pi * k / count
            first = 0.5 * sign * math.cos(angle) / math.sin(angle)
            second = -sign / (2.0 * math.sin(angle) ** 2)
        table.append(OMEGA * first - NU_T * OMEGA * OMEGA * second)
    return table


def core_index():
    return lax.rem(lax.axis_index("ax"), 2)


def call(kernel, outs, *operands, flops=0, scratch=()):
    outs = [jax.ShapeDtypeStruct(shape, jnp.float32) for shape in outs]
    total = sum(x.size * 4 for x in operands) + sum(x.size * 4 for x in outs)
    run = pl.pallas_call(
        kernel,
        out_shape=outs,
        in_specs=[VMEM] * len(operands),
        out_specs=[VMEM] * len(outs),
        scratch_shapes=[pltpu.VMEM(x, jnp.float32) for x in scratch],
        compiler_params=pltpu.CompilerParams(
            vmem_limit_bytes=total + sum(math.prod(x) * 4 for x in scratch) + (2 << 20)
        ),
        cost_estimate=pl.CostEstimate(flops=flops, bytes_accessed=total, transcendentals=0),
    )
    return list(run(*operands))


def slots(count):
    steps = [(dy, dx) for dy in range(count // 2) for dx in range(2)]
    return steps


def route(dy, dx, count):
    ring = count // 2
    return [(i, 2 * ((i // 2 + dy) % ring) + ((i % 2) ^ dx)) for i in range(count)]


def places_of(count, chosen):
    index = lax.axis_index("inst")
    ring = count // 2
    steps = slots(count)
    return [
        2 * lax.rem(index // 2 + steps[k][0], ring) + lax.rem(lax.rem(index, 2) + steps[k][1], 2)
        for k in chosen
    ]


def first_kernel(count, chosen, state_ref, out_ref, sem):
    (place,) = places_of(count, (chosen,))
    copy = pltpu.make_async_copy(state_ref.at[0, :, place], out_ref, sem)
    copy.start()
    copy.wait()


def rest_kernel(count, chosen, state_ref, flag_ref, early_ref, *refs):
    outs = refs[: len(chosen)]
    edge_ref, held_ref, sems = refs[len(chosen) :]
    fields, rows = state_ref.shape[1], state_ref.shape[3]
    early = next(k for k in range(count) if k not in chosen)
    (early_place,), places = places_of(count, (early,)), places_of(count, chosen)
    copies = [
        pltpu.make_async_copy(state_ref.at[0, :, place], out, sems.at[k])
        for k, (place, out) in enumerate(zip(places, outs))
    ]
    for copy in copies:
        copy.start()
    flag_copy = pltpu.make_async_copy(flag_ref, held_ref, sems.at[len(chosen)])
    flag_copy.start()

    def edges(place, block):
        row = pl.ds(place, 1)
        for f in range(fields):
            edge_ref[f, row] = block[f, 0:1]
            edge_ref[fields + f, row] = block[f, rows - 1 : rows]
        edge_ref[2 * fields, row] = block[fields - 1, 1:2]
        edge_ref[2 * fields + 1, row] = block[fields - 1, rows - 2 : rows - 1]

    edges(early_place, early_ref)
    flag_copy.wait()
    flags = (held_ref[0] > 0).astype(jnp.float32)
    edge_ref[EDGES - 1] = jnp.broadcast_to(flags[:, 0:1], edge_ref.shape[1:])
    for copy, place, out in zip(copies, places, outs):
        copy.wait()
        edges(place, out)


def pick_first(state, count, chosen):
    _, fields, _, rows, lanes = state.shape
    return pl.pallas_call(
        functools.partial(first_kernel, count, chosen),
        out_shape=jax.ShapeDtypeStruct((fields, rows, lanes), jnp.float32),
        in_specs=[pl.BlockSpec(memory_space=pltpu.HBM)],
        out_specs=VMEM,
        scratch_shapes=[pltpu.SemaphoreType.DMA],
        compiler_params=pltpu.CompilerParams(vmem_limit_bytes=4 << 20),
        cost_estimate=pl.CostEstimate(
            flops=0, bytes_accessed=fields * rows * lanes * 8, transcendentals=0
        ),
    )(pltpu.with_memory_space_constraint(state, pltpu.HBM))


def pick_rest(state, flags, early, count, chosen):
    _, fields, planes, rows, lanes = state.shape
    shapes = [(fields, rows, lanes)] * len(chosen) + [(EDGES, planes, lanes)]
    hbm = pl.BlockSpec(memory_space=pltpu.HBM)
    return pl.pallas_call(
        functools.partial(rest_kernel, count, chosen),
        out_shape=[jax.ShapeDtypeStruct(x, jnp.float32) for x in shapes],
        in_specs=[hbm, hbm, VMEM],
        out_specs=[VMEM] * len(shapes),
        scratch_shapes=[
            pltpu.VMEM(flags.shape, flags.dtype),
            pltpu.SemaphoreType.DMA((len(chosen) + 1,)),
        ],
        compiler_params=pltpu.CompilerParams(vmem_limit_bytes=state.size * 4 + (3 << 20)),
        cost_estimate=pl.CostEstimate(flops=0, bytes_accessed=state.size * 8, transcendentals=0),
    )(*(pltpu.with_memory_space_constraint(x, pltpu.HBM) for x in (state, flags)), early)


def mixing(count, parity):
    weights = spectral_weights(count)
    table = []
    for shift in (0, 1 - 2 * parity, 2 * parity - 1):
        g = [weights[(2 * a + shift) % count] for a in range(4)]
        table += [0.5 * (g[0] + g[2]), 0.5 * (g[1] + g[3])]
        table += [0.5 * (g[0] - g[2]), 0.5 * (g[1] - g[3])]
    return table


def spectral_kernel(*refs):
    count = len(refs) // 2
    ins, outs = refs[:count], refs[count:]
    fields, rows, _ = ins[0].shape
    tiles = rows // TILE
    first = lax.rem(lax.axis_index("inst"), 2) == 0
    mix = [
        jnp.where(first, jnp.float32(a), jnp.float32(b))
        for a, b in zip(mixing(count, 0), mixing(count, 1))
    ]

    def step(index, _):
        f = index // tiles
        span = pl.ds(pl.multiple_of((index % tiles) * TILE, TILE), TILE)
        parts = []
        for dx in range(2):
            u = [ins[2 * dy + dx][f, span] for dy in range(4)]
            parts.append((u[0] + u[2], u[1] + u[3], u[0] - u[2], u[1] - u[3]))
        for ex in range(2):
            even, odd, even_next, odd_next = 0.0, 0.0, 0.0, 0.0
            for dx in range(2):
                kind = 0 if ex == dx else (1 if ex else 2)
                e0, e1, o0, o1 = mix[4 * kind : 4 * kind + 4]
                s0, s1, d0, d1 = parts[dx]
                even = even + (e0 * s0 + e1 * s1)
                odd = odd + (o0 * d0 + o1 * d1)
                even_next = even_next + (e1 * s0 + e0 * s1)
                odd_next = odd_next + (o1 * d0 - o0 * d1)
            outs[ex][f, span] = even + odd
            outs[4 + ex][f, span] = even - odd
            outs[2 + ex][f, span] = even_next + odd_next
            outs[6 + ex][f, span] = even_next - odd_next
        return 0

    lax.fori_loop(0, fields * tiles, step, 0, unroll=4)


def primitives(cells):
    density = cells[0] + cells[1]
    inverse = 1.0 / density
    vel_ax = cells[2] * inverse
    vel_circ = cells[3] * inverse
    vel_rad = cells[4] * inverse
    fraction = cells[6]
    gamma_term = fraction / (G_LIQ - 1.0) + (1.0 - fraction) / (G_GAS - 1.0)
    stiff_term = fraction * (G_LIQ * P_LIQ / (G_LIQ - 1.0))
    kinetic = 0.5 * density * (vel_ax * vel_ax + vel_circ * vel_circ + vel_rad * vel_rad)
    gamma_inv = 1.0 / gamma_term
    pressure = (cells[5] - kinetic - stiff_term) * gamma_inv
    sound_speed = jnp.sqrt(((1.0 + gamma_inv) * pressure + stiff_term * gamma_inv) * inverse)
    return vel_ax, vel_circ, pressure, sound_speed


def sharpen(lower_val, centre, upper_val, offset):
    average = 0.5 * (lower_val + upper_val)
    difference = upper_val - lower_val
    steepness = 2.0 * (centre - average) / (jnp.abs(difference) + EPSA)
    return average + 0.5 * difference * jnp.tanh(BETA * (steepness + offset))


def flux_kernel(
    source_ref,
    halo_ref,
    flag_ref,
    res_ref,
    coup_ref,
    inv_ref,
    v_ref,
    w_ref,
    keep_ref,
    send_ref,
    state_ref,
    sems,
):
    def fetch(i):
        return pltpu.make_async_copy(source_ref.at[0, :, i], state_ref.at[0, :, i], sems.at[i])

    for i in range(state_ref.shape[2]):
        fetch(i).start()

    planes = state_ref.shape[2]
    rows = state_ref.shape[3]
    last = planes - 1

    def plane(i, _):
        fetch(i).wait()
        row = pl.ds(i, 1)
        quad = (TILE // 2, state_ref.shape[4])
        cells = []
        for f in range(FIELDS):
            upper, lower = halo_ref[f, row], halo_ref[FIELDS + f, row]
            if f < FIELDS - 1:
                edge = [jnp.broadcast_to(upper, quad), jnp.broadcast_to(lower, quad)]
            else:
                next_upper = halo_ref[2 * FIELDS, row]
                next_lower = halo_ref[2 * FIELDS + 1, row]
                edge = [upper] + [next_upper] * 3 + [next_lower] * 3 + [lower]
            cells.append(jnp.concatenate([state_ref[0, f, i]] + edge, axis=0))
        edge = jnp.broadcast_to(halo_ref[EDGES - 1, row], (TILE, state_ref.shape[4]))
        flags = jnp.concatenate([flag_ref[i], edge], axis=0)
        total = rows + TILE

        def below(x, by=1):
            return pltpu.roll(x, by, 0)

        def above(x):
            return pltpu.roll(x, total - 1, 0)

        vel_ax, vel_circ, pressure, sound = primitives(cells)
        coup_ref[i] = -ALPHA * (jnp.abs(vel_ax) + sound)[:rows]
        wave = jnp.abs(vel_circ) + sound
        half_speed = 0.5 * jnp.maximum(below(wave), wave)
        fraction = cells[6]
        back1 = below(fraction)
        sharp_left = sharpen(below(fraction, 2), back1, fraction, 1.0)
        sharp_right = sharpen(back1, fraction, above(fraction), -1.0)
        flagged = flags > 0.5
        frac_left = jnp.where(flagged, sharp_left, back1)
        frac_right = jnp.where(flagged, sharp_right, fraction)
        for f in range(FIELDS):
            if f < 6:
                flux = cells[f] * vel_circ
                if f == 3:
                    flux = flux + pressure
                elif f == 5:
                    flux = flux + pressure * vel_circ
                mean = 0.5 * (below(flux) + flux)
                jump = cells[f] - below(cells[f])
            else:
                mean = 0.5 * (frac_left * below(vel_circ) + frac_right * vel_circ)
                jump = frac_right - frac_left
            face = mean - half_speed * jump
            res_ref[i, f] = (above(face) - face)[:rows]
        return 0

    lax.fori_loop(0, planes, plane, 0)

    core = core_index()
    tiles = rows // TILE // 2
    for target_ref, side in ((keep_ref, core), (send_ref, 1 - core)):

        def factor(t, _, target_ref=target_ref, side=side):
            span = pl.ds(pl.multiple_of((side * tiles + t) * TILE, TILE), TILE)
            place = pl.ds(pl.multiple_of(t * TILE, TILE), TILE)
            coup = [coup_ref[i, span] for i in range(planes)]
            inv, ratio, v = [], [], []
            for i in range(last):
                pivot = DIAG0 - 2.0 * coup[i]
                if i:
                    pivot = pivot - coup[i] * ratio[-1]
                inv.append(1.0 / pivot)
                ratio.append(coup[i] * inv[-1])
                v.append(inv[-1] if i == 0 else -(ratio[-1] * v[-1]))
                inv_ref[i, span] = inv[-1]
            v_next, w_next = v[-1], inv[-1]
            v_last, w_last = v_next * coup[0], w_next * coup[last - 1]
            for i in range(last - 1, -1, -1):
                if i < last - 1:
                    v_next = v[i] - ratio[i] * v_next
                    w_next = -(ratio[i] * w_next)
                v_first, w_first = v_next * coup[0], w_next * coup[last - 1]
                v_ref[i, span] = v_first
                w_ref[i, span] = w_first
            sep = coup[last]
            target_ref[0, place] = -(sep * v_last)
            target_ref[1, place] = DIAG0 - 2.0 * sep - sep * w_last
            target_ref[2, place] = sep
            target_ref[3, place] = v_first
            target_ref[4, place] = w_first
            return 0

        lax.fori_loop(0, tiles, factor, 0)


def pair_kernel(keep_ref, got_ref, pair_ref, raw_ref, ends_ref):
    lower_core = core_index() == 0
    lower_a, diag_a, sep_a, v_a, w_a = (
        jnp.where(lower_core, keep_ref[k], got_ref[k]) for k in range(COEFS)
    )
    lower_b, diag_b, sep_b, v_b, w_b = (
        jnp.where(lower_core, got_ref[k], keep_ref[k]) for k in range(COEFS)
    )
    inv = 1.0 / (diag_a - sep_a * v_b)
    v = inv * lower_a
    w = -(inv * sep_a * w_b)
    for k, x in enumerate((inv, sep_a, w_a, lower_b, v, w)):
        pair_ref[k] = x
    raw_ref[0] = diag_b - lower_b * w
    raw_ref[1] = -(lower_b * v)
    raw_ref[2] = sep_b
    ends_ref[0] = v_a - w_a * v
    ends_ref[1] = -(w_a * w)


def link_kernel(raw_ref, ends_ref, link_ref, edge_ref):
    sep = raw_ref[2]
    scale = 1.0 / (raw_ref[0] - sep * ends_ref[0])
    link_ref[0] = scale
    link_ref[1] = raw_ref[1] * scale
    link_ref[2] = -(sep * ends_ref[1]) * scale
    edge_ref[0] = sep * scale


def join_kernel(link_ref, edge_ref, out_ref):
    for k in range(3):
        out_ref[k] = link_ref[k]
    out_ref[3] = edge_ref[0]


def half_of(mine):
    core = core_index()
    return core if mine else 1 - core


def sweep_kernel(mine, res_ref, coup_ref, inv_ref, *refs):
    count = len(refs) - 3
    specs = refs[:count]
    y_ref, target_ref, right_ref = refs[count:]
    planes, fields, rows, _ = res_ref.shape
    last = planes - 1
    tiles = rows // TILE // 2
    side = half_of(mine)
    index = lax.axis_index("inst")
    ring = count // 2
    places = [
        2 * lax.rem(index // 2 + ring - dy, ring) + lax.rem(lax.rem(index, 2) + dx, 2)
        for dy, dx in slots(count)
    ]

    def step(t, _):
        span = pl.ds(pl.multiple_of((side * tiles + t) * TILE, TILE), TILE)
        place = pl.ds(pl.multiple_of(t * TILE, TILE), TILE)
        for f in range(fields):
            for i, spec_ref in zip(places, specs):
                right_ref[f, i] = -(res_ref[i, f, span] + spec_ref[f, span])
        coup = [coup_ref[i, span] for i in range(planes)]
        inv = [inv_ref[i, span] for i in range(last)]
        ratio = [coup[i] * inv[i] for i in range(last)]
        for f in range(fields):
            value = []
            for i in range(last):
                right = right_ref[f, i]
                if i:
                    right = right - coup[i] * value[-1]
                value.append(right * inv[i])
            y = value[-1]
            y_last = y
            y_ref[last - 1, f, place] = y
            for i in range(last - 2, -1, -1):
                y = value[i] - ratio[i] * y
                y_ref[i, f, place] = y
            target_ref[f, place] = y
            target_ref[fields + f, place] = right_ref[f, last] - coup[last] * y_last
        return 0

    lax.fori_loop(0, tiles, step, 0)


def merge_kernel(keep_ref, got_ref, pair_ref, link_ref, inner_ref, out_ref):
    fields = inner_ref.shape[0]
    rows = inner_ref.shape[1]
    lower_core = core_index() == 0

    def step(t, _):
        span = pl.ds(pl.multiple_of(t * TILE, TILE), TILE)
        inv, sep_a, first_a, lower_b = (pair_ref[k, span] for k in range(4))
        scale, lower, upper, edge = (link_ref[k, span] for k in range(4))
        for f in range(fields):
            keep_y, got_y = keep_ref[f, span], got_ref[f, span]
            keep_own, got_own = keep_ref[fields + f, span], got_ref[fields + f, span]
            y_a = jnp.where(lower_core, keep_y, got_y)
            y_b = jnp.where(lower_core, got_y, keep_y)
            own_a = jnp.where(lower_core, keep_own, got_own)
            own_b = jnp.where(lower_core, got_own, keep_own)
            inner = inv * (own_a - sep_a * y_b)
            inner_ref[f, span] = inner
            for k, x in (
                (f, scale * (own_b - lower_b * inner)),
                (fields + f, edge * (y_a - first_a * inner)),
            ):
                out_ref[2 * t, k] = x[0:4]
                out_ref[2 * t + 1, k] = x[4:8]
        for k, x in ((2 * fields, lower), (2 * fields + 1, upper)):
            out_ref[2 * t, k] = x[0:4]
            out_ref[2 * t + 1, k] = x[4:8]
        return 0

    lax.fori_loop(0, rows // TILE, step, 0)


def reduced_kernel(rhs_ref, out_ref):
    count = rhs_ref.shape[0]
    fields = out_ref.shape[1] // 2
    ratio = []
    values = []
    for p in range(count):
        lower, upper = rhs_ref[p, 2 * fields], rhs_ref[p, 2 * fields + 1]
        more = p + 1 < count
        inv = 1.0 / (1.0 - lower * ratio[-1]) if p else jnp.ones_like(lower)
        ratio.append(upper * inv)
        row = []
        for f in range(fields):
            right = rhs_ref[p, f]
            if more:
                right = right - rhs_ref[p + 1, fields + f]
            if p:
                right = right - lower * values[-1][f]
            row.append(right * inv)
        values.append(row)
    solved = values[-1]
    for p in range(count - 1, -1, -1):
        if p < count - 1:
            solved = [values[p][f] - ratio[p] * solved[f] for f in range(fields)]
        for f in range(fields):
            out_ref[p, fields + f] = solved[f]
            if p < count - 1:
                out_ref[p + 1, f] = solved[f]
    for f in range(fields):
        out_ref[0, f] = jnp.zeros_like(solved[f])


def expand_kernel(solved_ref, inner_ref, pair_ref, keep_ref, send_ref):
    fields, rows, _ = inner_ref.shape
    lower_core = core_index() == 0

    def step(t, _):
        span = pl.ds(pl.multiple_of(t * TILE, TILE), TILE)
        v, w = pair_ref[4, span], pair_ref[5, span]
        for f in range(fields):
            prev = jnp.concatenate([solved_ref[2 * t, f], solved_ref[2 * t + 1, f]], axis=0)
            own = jnp.concatenate(
                [solved_ref[2 * t, fields + f], solved_ref[2 * t + 1, fields + f]], axis=0
            )
            inner = inner_ref[f, span] - v * prev - w * own
            keep_ref[f, span] = jnp.where(lower_core, prev, inner)
            keep_ref[fields + f, span] = jnp.where(lower_core, inner, own)
            send_ref[f, span] = jnp.where(lower_core, inner, prev)
            send_ref[fields + f, span] = jnp.where(lower_core, own, inner)
        return 0

    lax.fori_loop(0, rows // TILE, step, 0)


def finish_kernel(mine, state_ref, v_ref, w_ref, y_ref, ends_ref, *refs):
    out_ref, block_ref, sems = refs[-3:]
    fields, planes, rows = state_ref.shape[1:4]
    last = planes - 1
    tiles = rows // TILE // 2
    side = half_of(mine)
    lines = pl.ds(pl.multiple_of(side * (rows // 2), rows // 2), rows // 2)
    copies = []
    for f in range(fields):

        def tile(t, _, f=f):
            span = pl.ds(pl.multiple_of((side * tiles + t) * TILE, TILE), TILE)
            place = pl.ds(pl.multiple_of(t * TILE, TILE), TILE)
            prev, own = ends_ref[f, place], ends_ref[fields + f, place]
            for i in range(last):
                delta = y_ref[i, f, place] - v_ref[i, span] * prev - w_ref[i, span] * own
                block_ref[f, i, place] = state_ref[0, f, i, span] + delta
            block_ref[f, last, place] = state_ref[0, f, last, span] + own
            return 0

        lax.fori_loop(0, tiles, tile, 0, unroll=True)
        copy = pltpu.make_async_copy(block_ref.at[f], out_ref.at[0, f, :, lines], sems.at[f])
        copy.start()
        copies.append(copy)
    for copy in copies:
        copy.wait()


def finish(mine, state, v, w, y, ends, partial=None):
    fields, planes, rows, lanes = state.shape[1:]
    hbm = pl.BlockSpec(memory_space=pltpu.HBM)
    operands = [state, v, w, y, ends]
    specs = [VMEM] * len(operands)
    aliases = {}
    if partial is not None:
        aliases = {len(operands): 0}
        operands.append(partial)
        specs.append(hbm)
    return pl.pallas_call(
        functools.partial(finish_kernel, mine),
        out_shape=jax.ShapeDtypeStruct(state.shape, jnp.float32),
        in_specs=specs,
        out_specs=hbm,
        scratch_shapes=[
            pltpu.VMEM((fields, planes, rows // 2, lanes), jnp.float32),
            pltpu.SemaphoreType.DMA((fields,)),
        ],
        input_output_aliases=aliases,
        compiler_params=pltpu.CompilerParams(vmem_limit_bytes=state.size * 12),
        cost_estimate=pl.CostEstimate(
            flops=state.size * 2, bytes_accessed=state.size * 6, transcendentals=0
        ),
    )(*operands)


def flux_parts(state, halo, flag_cells):
    fields, planes, rows, lanes = state.shape[1:]
    grid = (rows, lanes)
    shapes = [
        (planes, fields) + grid,
        (planes,) + grid,
        (planes - 1,) + grid,
        (planes - 1,) + grid,
        (planes - 1,) + grid,
        (COEFS, rows // 2, lanes),
        (COEFS, rows // 2, lanes),
        state.shape,
    ]
    return pl.pallas_call(
        flux_kernel,
        out_shape=[jax.ShapeDtypeStruct(x, jnp.float32) for x in shapes],
        in_specs=[pl.BlockSpec(memory_space=pltpu.HBM), VMEM, VMEM],
        out_specs=[VMEM] * len(shapes),
        scratch_shapes=[pltpu.SemaphoreType.DMA((planes,))],
        compiler_params=pltpu.CompilerParams(vmem_limit_bytes=state.size * 12),
        cost_estimate=pl.CostEstimate(
            flops=state.size * 60, bytes_accessed=state.size * 16, transcendentals=0
        ),
    )(pltpu.with_memory_space_constraint(state, pltpu.HBM), halo, flag_cells)


def exchange(x, axis, groups=None):
    return lax.all_to_all(x, axis, 0, 0, tiled=True, axis_index_groups=groups)


def body(flow_state, thinc_flags):
    own = flow_state[0]
    planes, rows, lanes = own.shape[1:]
    instances = lax.axis_size("inst")
    ax_count = lax.axis_size("ax")
    circ_count = lax.axis_size("circ")
    chips = ax_count // 2
    half = rows // 2
    piece = half // chips

    swap = [(i, i ^ 1) for i in range(ax_count)]
    groups = [list(range(c, ax_count, 2)) for c in range(2)]

    def partner(x):
        return lax.ppermute(x, "ax", swap)

    def neighbour(x, by):
        moves = [(i, i + 2 * by) for i in range(ax_count) if 0 <= i + 2 * by < ax_count]
        return lax.ppermute(x, "ax", moves)

    steps = slots(instances)
    order = ORDER
    rest = tuple(k for k in range(instances) if k != order[0])
    blocks = [None] * instances
    early = pick_first(flow_state, instances, order[0])
    *others, edges = pick_rest(flow_state, thinc_flags, early, instances, rest)
    blocks[order[0]] = early
    for k, block in zip(rest, others):
        blocks[k] = block
    halo = lax.ppermute(
        edges, "circ", [(i, (i + 1) % circ_count) for i in range(circ_count)]
    )
    for k in order:
        blocks[k] = lax.ppermute(blocks[k], "inst", route(*steps[k], instances))
    flags = (thinc_flags[0] > 0).astype(jnp.float32)
    flag_cells = jnp.broadcast_to(flags[:, :, None], (planes, rows, lanes))

    res, coup, inv, v, w, keep, send, held_state = flux_parts(flow_state, halo, flag_cells)

    thin = (half, lanes)
    pair, raw, ends = call(
        pair_kernel, [(6,) + thin, (3,) + thin, (2,) + thin], keep, partner(send)
    )
    ends = neighbour(ends, -1)
    link, edge = call(link_kernel, [(3,) + thin, (1,) + thin], raw, ends)
    specs = call(spectral_kernel, [blocks[0].shape] * instances, *blocks, flops=own.size * 9)
    for k in RETURN:
        specs[k] = lax.ppermute(specs[k], "inst", route(*steps[k], instances))
    edge = neighbour(edge, 1)
    (link,) = call(join_kernel, [(4,) + thin], link, edge)
    shapes = [(planes - 1, FIELDS, half, lanes), (2 * FIELDS, half, lanes)]
    parts = []
    for mine in (False, True):
        parts.append(
            call(
                functools.partial(sweep_kernel, mine),
                shapes,
                res,
                coup,
                inv,
                *specs,
                flops=own.size * 4,
                scratch=[(FIELDS, planes, TILE, lanes)],
            )
        )
    (y_other, send), (y_mine, keep) = parts
    inner, rhs = call(
        merge_kernel,
        [(FIELDS, half, lanes), (chips, 2 * FIELDS + 2, piece, lanes)],
        keep,
        partner(send),
        pair,
        link,
        flops=send.size * 4,
    )
    rhs = exchange(rhs, "ax", groups)
    (solved,) = call(
        reduced_kernel, [(chips, 2 * FIELDS, piece, lanes)], rhs, flops=rhs.size * 8
    )
    solved = exchange(solved, "ax", groups)
    keep, send = call(
        expand_kernel,
        [(2 * FIELDS, half, lanes)] * 2,
        solved,
        inner,
        pair,
        flops=send.size * 4,
    )
    got = partner(send)
    out = finish(True, held_state, v, w, y_mine, keep)
    return finish(False, held_state, v, w, y_other, got, out)


def solution(mesh):
    return jax.shard_map(
        body,
        mesh=mesh,
        in_specs=(P("inst", None, "ax", "circ", None), P("inst", "ax", "circ")),
        out_specs=P("inst", None, "ax", "circ", None),
        check_vma=False,
    )
```

```python
import functools
import math

import jax
import jax.numpy as jnp
from jax import lax
from jax.experimental import pallas as pl
from jax.experimental.pallas import tpu as pltpu
from jax.sharding import PartitionSpec as P


G_LIQ = 4.4
P_LIQ = 6.0
G_GAS = 1.4
BETA = 1.6
EPSA = 0.1
ALPHA = 4.0
DIAG0 = 0.016
OMEGA = 1.0
NU_T = 0.25

FIELDS = 7
ORDER = (5, 7, 3, 4, 1, 2, 6)
RETURN = (3, 4, 5, 7, 1, 2, 6)
EDGES = 2 * FIELDS + 3
COEFS = 5
TILE = 8


VMEM = pl.BlockSpec(memory_space=pltpu.VMEM)


def spectral_weights(count):
    table = []
    for k in range(count):
        if k == 0:
            first, second = 0.0, -(count * count + 2) / 12.0
        else:
            sign = 1.0 if k % 2 == 0 else -1.0
            angle = math.pi * k / count
            first = 0.5 * sign * math.cos(angle) / math.sin(angle)
            second = -sign / (2.0 * math.sin(angle) ** 2)
        table.append(OMEGA * first - NU_T * OMEGA * OMEGA * second)
    return table


def core_index():
    return lax.rem(lax.axis_index("ax"), 2)


def call(kernel, outs, *operands, flops=0, scratch=()):
    outs = [jax.ShapeDtypeStruct(shape, jnp.float32) for shape in outs]
    total = sum(x.size * 4 for x in operands) + sum(x.size * 4 for x in outs)
    run = pl.pallas_call(
        kernel,
        out_shape=outs,
        in_specs=[VMEM] * len(operands),
        out_specs=[VMEM] * len(outs),
        scratch_shapes=[pltpu.VMEM(x, jnp.float32) for x in scratch],
        compiler_params=pltpu.CompilerParams(
            vmem_limit_bytes=total + sum(math.prod(x) * 4 for x in scratch) + (2 << 20)
        ),
        cost_estimate=pl.CostEstimate(flops=flops, bytes_accessed=total, transcendentals=0),
    )
    return list(run(*operands))


def slots(count):
    steps = [(dy, dx) for dy in range(count // 2) for dx in range(2)]
    return steps


def route(dy, dx, count):
    ring = count // 2
    return [(i, 2 * ((i // 2 + dy) % ring) + ((i % 2) ^ dx)) for i in range(count)]


def places_of(count, chosen):
    index = lax.axis_index("inst")
    ring = count // 2
    steps = slots(count)
    return [
        2 * lax.rem(index // 2 + steps[k][0], ring) + lax.rem(lax.rem(index, 2) + steps[k][1], 2)
        for k in chosen
    ]


def first_kernel(count, chosen, state_ref, out_ref, sem):
    (place,) = places_of(count, (chosen,))
    copy = pltpu.make_async_copy(state_ref.at[0, :, place], out_ref, sem)
    copy.start()
    copy.wait()


def rest_kernel(count, chosen, state_ref, flag_ref, early_ref, *refs):
    outs = refs[: len(chosen)]
    edge_ref, held_ref, sems = refs[len(chosen) :]
    fields, rows = state_ref.shape[1], state_ref.shape[3]
    early = next(k for k in range(count) if k not in chosen)
    (early_place,), places = places_of(count, (early,)), places_of(count, chosen)
    copies = [
        pltpu.make_async_copy(state_ref.at[0, :, place], out, sems.at[k])
        for k, (place, out) in enumerate(zip(places, outs))
    ]
    for copy in copies:
        copy.start()
    flag_copy = pltpu.make_async_copy(flag_ref, held_ref, sems.at[len(chosen)])
    flag_copy.start()

    def edges(place, block):
        row = pl.ds(place, 1)
        for f in range(fields):
            edge_ref[f, row] = block[f, 0:1]
            edge_ref[fields + f, row] = block[f, rows - 1 : rows]
        edge_ref[2 * fields, row] = block[fields - 1, 1:2]
        edge_ref[2 * fields + 1, row] = block[fields - 1, rows - 2 : rows - 1]

    edges(early_place, early_ref)
    flag_copy.wait()
    flags = (held_ref[0] > 0).astype(jnp.float32)
    edge_ref[EDGES - 1] = jnp.broadcast_to(flags[:, 0:1], edge_ref.shape[1:])
    for copy, place, out in zip(copies, places, outs):
        copy.wait()
        edges(place, out)


def pick_first(state, count, chosen):
    _, fields, _, rows, lanes = state.shape
    return pl.pallas_call(
        functools.partial(first_kernel, count, chosen),
        out_shape=jax.ShapeDtypeStruct((fields, rows, lanes), jnp.float32),
        in_specs=[pl.BlockSpec(memory_space=pltpu.HBM)],
        out_specs=VMEM,
        scratch_shapes=[pltpu.SemaphoreType.DMA],
        compiler_params=pltpu.CompilerParams(vmem_limit_bytes=4 << 20),
        cost_estimate=pl.CostEstimate(
            flops=0, bytes_accessed=fields * rows * lanes * 8, transcendentals=0
        ),
    )(pltpu.with_memory_space_constraint(state, pltpu.HBM))


def pick_rest(state, flags, early, count, chosen):
    _, fields, planes, rows, lanes = state.shape
    shapes = [(fields, rows, lanes)] * len(chosen) + [(EDGES, planes, lanes)]
    hbm = pl.BlockSpec(memory_space=pltpu.HBM)
    return pl.pallas_call(
        functools.partial(rest_kernel, count, chosen),
        out_shape=[jax.ShapeDtypeStruct(x, jnp.float32) for x in shapes],
        in_specs=[hbm, hbm, VMEM],
        out_specs=[VMEM] * len(shapes),
        scratch_shapes=[
            pltpu.VMEM(flags.shape, flags.dtype),
            pltpu.SemaphoreType.DMA((len(chosen) + 1,)),
        ],
        compiler_params=pltpu.CompilerParams(vmem_limit_bytes=state.size * 4 + (3 << 20)),
        cost_estimate=pl.CostEstimate(flops=0, bytes_accessed=state.size * 8, transcendentals=0),
    )(*(pltpu.with_memory_space_constraint(x, pltpu.HBM) for x in (state, flags)), early)


def mixing(count, parity):
    weights = spectral_weights(count)
    table = []
    for shift in (0, 1 - 2 * parity, 2 * parity - 1):
        g = [weights[(2 * a + shift) % count] for a in range(4)]
        table += [0.5 * (g[0] + g[2]), 0.5 * (g[1] + g[3])]
        table += [0.5 * (g[0] - g[2]), 0.5 * (g[1] - g[3])]
    return table


def spectral_kernel(count, chosen, *refs):
    ins, outs = refs[:count], dict(zip(chosen, refs[count:]))
    fields, rows, _ = ins[0].shape
    tiles = rows // TILE
    first = lax.rem(lax.axis_index("inst"), 2) == 0
    mix = [
        jnp.where(first, jnp.float32(a), jnp.float32(b))
        for a, b in zip(mixing(count, 0), mixing(count, 1))
    ]

    def step(index, _):
        f = index // tiles
        span = pl.ds(pl.multiple_of((index % tiles) * TILE, TILE), TILE)
        parts = []
        for dx in range(2):
            u = [ins[2 * dy + dx][f, span] for dy in range(4)]
            parts.append((u[0] + u[2], u[1] + u[3], u[0] - u[2], u[1] - u[3]))
        for ex in range(2):
            even, odd, even_next, odd_next = 0.0, 0.0, 0.0, 0.0
            for dx in range(2):
                kind = 0 if ex == dx else (1 if ex else 2)
                e0, e1, o0, o1 = mix[4 * kind : 4 * kind + 4]
                s0, s1, d0, d1 = parts[dx]
                even = even + (e0 * s0 + e1 * s1)
                odd = odd + (o0 * d0 + o1 * d1)
                even_next = even_next + (e1 * s0 + e0 * s1)
                odd_next = odd_next + (o1 * d0 - o0 * d1)
            for k, value in (
                (ex, even + odd),
                (4 + ex, even - odd),
                (2 + ex, even_next + odd_next),
                (6 + ex, even_next - odd_next),
            ):
                if k in outs:
                    outs[k][f, span] = value
        return 0

    lax.fori_loop(0, fields * tiles, step, 0, unroll=4)


def primitives(cells):
    density = cells[0] + cells[1]
    inverse = 1.0 / density
    vel_ax = cells[2] * inverse
    vel_circ = cells[3] * inverse
    vel_rad = cells[4] * inverse
    fraction = cells[6]
    gamma_term = fraction / (G_LIQ - 1.0) + (1.0 - fraction) / (G_GAS - 1.0)
    stiff_term = fraction * (G_LIQ * P_LIQ / (G_LIQ - 1.0))
    kinetic = 0.5 * density * (vel_ax * vel_ax + vel_circ * vel_circ + vel_rad * vel_rad)
    gamma_inv = 1.0 / gamma_term
    pressure = (cells[5] - kinetic - stiff_term) * gamma_inv
    sound_speed = jnp.sqrt(((1.0 + gamma_inv) * pressure + stiff_term * gamma_inv) * inverse)
    return vel_ax, vel_circ, pressure, sound_speed


def sharpen(lower_val, centre, upper_val, offset):
    average = 0.5 * (lower_val + upper_val)
    difference = upper_val - lower_val
    steepness = 2.0 * (centre - average) / (jnp.abs(difference) + EPSA)
    return average + 0.5 * difference * jnp.tanh(BETA * (steepness + offset))


def flux_kernel(
    source_ref,
    halo_ref,
    flag_ref,
    res_ref,
    coup_ref,
    inv_ref,
    v_ref,
    w_ref,
    keep_ref,
    send_ref,
    state_ref,
    sems,
):
    def fetch(i):
        return pltpu.make_async_copy(source_ref.at[0, :, i], state_ref.at[0, :, i], sems.at[i])

    for i in range(state_ref.shape[2]):
        fetch(i).start()

    planes = state_ref.shape[2]
    rows = state_ref.shape[3]
    last = planes - 1

    def plane(i, _):
        fetch(i).wait()
        row = pl.ds(i, 1)
        quad = (TILE // 2, state_ref.shape[4])
        cells = []
        for f in range(FIELDS):
            upper, lower = halo_ref[f, row], halo_ref[FIELDS + f, row]
            if f < FIELDS - 1:
                edge = [jnp.broadcast_to(upper, quad), jnp.broadcast_to(lower, quad)]
            else:
                next_upper = halo_ref[2 * FIELDS, row]
                next_lower = halo_ref[2 * FIELDS + 1, row]
                edge = [upper] + [next_upper] * 3 + [next_lower] * 3 + [lower]
            cells.append(jnp.concatenate([state_ref[0, f, i]] + edge, axis=0))
        edge = jnp.broadcast_to(halo_ref[EDGES - 1, row], (TILE, state_ref.shape[4]))
        flags = jnp.concatenate([flag_ref[i], edge], axis=0)
        total = rows + TILE

        def below(x, by=1):
            return pltpu.roll(x, by, 0)

        def above(x):
            return pltpu.roll(x, total - 1, 0)

        vel_ax, vel_circ, pressure, sound = primitives(cells)
        coup_ref[i] = -ALPHA * (jnp.abs(vel_ax) + sound)[:rows]
        wave = jnp.abs(vel_circ) + sound
        half_speed = 0.5 * jnp.maximum(below(wave), wave)
        fraction = cells[6]
        back1 = below(fraction)
        sharp_left = sharpen(below(fraction, 2), back1, fraction, 1.0)
        sharp_right = sharpen(back1, fraction, above(fraction), -1.0)
        flagged = flags > 0.5
        frac_left = jnp.where(flagged, sharp_left, back1)
        frac_right = jnp.where(flagged, sharp_right, fraction)
        for f in range(FIELDS):
            if f < 6:
                flux = cells[f] * vel_circ
                if f == 3:
                    flux = flux + pressure
                elif f == 5:
                    flux = flux + pressure * vel_circ
                mean = 0.5 * (below(flux) + flux)
                jump = cells[f] - below(cells[f])
            else:
                mean = 0.5 * (frac_left * below(vel_circ) + frac_right * vel_circ)
                jump = frac_right - frac_left
            face = mean - half_speed * jump
            res_ref[i, f] = (above(face) - face)[:rows]
        return 0

    lax.fori_loop(0, planes, plane, 0)

    core = core_index()
    tiles = rows // TILE // 2
    for target_ref, side in ((keep_ref, core), (send_ref, 1 - core)):

        def factor(t, _, target_ref=target_ref, side=side):
            span = pl.ds(pl.multiple_of((side * tiles + t) * TILE, TILE), TILE)
            place = pl.ds(pl.multiple_of(t * TILE, TILE), TILE)
            coup = [coup_ref[i, span] for i in range(planes)]
            inv, ratio, v = [], [], []
            for i in range(last):
                pivot = DIAG0 - 2.0 * coup[i]
                if i:
                    pivot = pivot - coup[i] * ratio[-1]
                inv.append(1.0 / pivot)
                ratio.append(coup[i] * inv[-1])
                v.append(inv[-1] if i == 0 else -(ratio[-1] * v[-1]))
                inv_ref[i, span] = inv[-1]
            v_next, w_next = v[-1], inv[-1]
            v_last, w_last = v_next * coup[0], w_next * coup[last - 1]
            for i in range(last - 1, -1, -1):
                if i < last - 1:
                    v_next = v[i] - ratio[i] * v_next
                    w_next = -(ratio[i] * w_next)
                v_first, w_first = v_next * coup[0], w_next * coup[last - 1]
                v_ref[i, span] = v_first
                w_ref[i, span] = w_first
            sep = coup[last]
            target_ref[0, place] = -(sep * v_last)
            target_ref[1, place] = DIAG0 - 2.0 * sep - sep * w_last
            target_ref[2, place] = sep
            target_ref[3, place] = v_first
            target_ref[4, place] = w_first
            return 0

        lax.fori_loop(0, tiles, factor, 0)


def pair_kernel(keep_ref, got_ref, pair_ref, raw_ref, ends_ref):
    lower_core = core_index() == 0
    lower_a, diag_a, sep_a, v_a, w_a = (
        jnp.where(lower_core, keep_ref[k], got_ref[k]) for k in range(COEFS)
    )
    lower_b, diag_b, sep_b, v_b, w_b = (
        jnp.where(lower_core, got_ref[k], keep_ref[k]) for k in range(COEFS)
    )
    inv = 1.0 / (diag_a - sep_a * v_b)
    v = inv * lower_a
    w = -(inv * sep_a * w_b)
    for k, x in enumerate((inv, sep_a, w_a, lower_b, v, w)):
        pair_ref[k] = x
    raw_ref[0] = diag_b - lower_b * w
    raw_ref[1] = -(lower_b * v)
    raw_ref[2] = sep_b
    ends_ref[0] = v_a - w_a * v
    ends_ref[1] = -(w_a * w)


def link_kernel(raw_ref, ends_ref, link_ref, edge_ref):
    sep = raw_ref[2]
    scale = 1.0 / (raw_ref[0] - sep * ends_ref[0])
    link_ref[0] = scale
    link_ref[1] = raw_ref[1] * scale
    link_ref[2] = -(sep * ends_ref[1]) * scale
    edge_ref[0] = sep * scale


def join_kernel(link_ref, edge_ref, out_ref):
    for k in range(3):
        out_ref[k] = link_ref[k]
    out_ref[3] = edge_ref[0]


def half_of(mine):
    core = core_index()
    return core if mine else 1 - core


def sweep_kernel(mine, res_ref, coup_ref, inv_ref, *refs):
    count = len(refs) - 3
    specs = refs[:count]
    y_ref, target_ref, right_ref = refs[count:]
    planes, fields, rows, _ = res_ref.shape
    last = planes - 1
    tiles = rows // TILE // 2
    side = half_of(mine)
    index = lax.axis_index("inst")
    ring = count // 2
    places = [
        2 * lax.rem(index // 2 + ring - dy, ring) + lax.rem(lax.rem(index, 2) + dx, 2)
        for dy, dx in slots(count)
    ]

    def step(t, _):
        span = pl.ds(pl.multiple_of((side * tiles + t) * TILE, TILE), TILE)
        place = pl.ds(pl.multiple_of(t * TILE, TILE), TILE)
        for f in range(fields):
            for i, spec_ref in zip(places, specs):
                right_ref[f, i] = -(res_ref[i, f, span] + spec_ref[f, span])
        coup = [coup_ref[i, span] for i in range(planes)]
        inv = [inv_ref[i, span] for i in range(last)]
        ratio = [coup[i] * inv[i] for i in range(last)]
        for f in range(fields):
            value = []
            for i in range(last):
                right = right_ref[f, i]
                if i:
                    right = right - coup[i] * value[-1]
                value.append(right * inv[i])
            y = value[-1]
            y_last = y
            y_ref[last - 1, f, place] = y
            for i in range(last - 2, -1, -1):
                y = value[i] - ratio[i] * y
                y_ref[i, f, place] = y
            target_ref[f, place] = y
            target_ref[fields + f, place] = right_ref[f, last] - coup[last] * y_last
        return 0

    lax.fori_loop(0, tiles, step, 0)


def merge_kernel(keep_ref, got_ref, pair_ref, link_ref, inner_ref, out_ref):
    fields = inner_ref.shape[0]
    rows = inner_ref.shape[1]
    lower_core = core_index() == 0

    def step(t, _):
        span = pl.ds(pl.multiple_of(t * TILE, TILE), TILE)
        inv, sep_a, first_a, lower_b = (pair_ref[k, span] for k in range(4))
        scale, lower, upper, edge = (link_ref[k, span] for k in range(4))
        for f in range(fields):
            keep_y, got_y = keep_ref[f, span], got_ref[f, span]
            keep_own, got_own = keep_ref[fields + f, span], got_ref[fields + f, span]
            y_a = jnp.where(lower_core, keep_y, got_y)
            y_b = jnp.where(lower_core, got_y, keep_y)
            own_a = jnp.where(lower_core, keep_own, got_own)
            own_b = jnp.where(lower_core, got_own, keep_own)
            inner = inv * (own_a - sep_a * y_b)
            inner_ref[f, span] = inner
            for k, x in (
                (f, scale * (own_b - lower_b * inner)),
                (fields + f, edge * (y_a - first_a * inner)),
            ):
                out_ref[2 * t, k] = x[0:4]
                out_ref[2 * t + 1, k] = x[4:8]
        for k, x in ((2 * fields, lower), (2 * fields + 1, upper)):
            out_ref[2 * t, k] = x[0:4]
            out_ref[2 * t + 1, k] = x[4:8]
        return 0

    lax.fori_loop(0, rows // TILE, step, 0)


def reduced_kernel(rhs_ref, out_ref):
    count = rhs_ref.shape[0]
    fields = out_ref.shape[1] // 2
    ratio = []
    values = []
    for p in range(count):
        lower, upper = rhs_ref[p, 2 * fields], rhs_ref[p, 2 * fields + 1]
        more = p + 1 < count
        inv = 1.0 / (1.0 - lower * ratio[-1]) if p else jnp.ones_like(lower)
        ratio.append(upper * inv)
        row = []
        for f in range(fields):
            right = rhs_ref[p, f]
            if more:
                right = right - rhs_ref[p + 1, fields + f]
            if p:
                right = right - lower * values[-1][f]
            row.append(right * inv)
        values.append(row)
    solved = values[-1]
    for p in range(count - 1, -1, -1):
        if p < count - 1:
            solved = [values[p][f] - ratio[p] * solved[f] for f in range(fields)]
        for f in range(fields):
            out_ref[p, fields + f] = solved[f]
            if p < count - 1:
                out_ref[p + 1, f] = solved[f]
    for f in range(fields):
        out_ref[0, f] = jnp.zeros_like(solved[f])


def expand_kernel(solved_ref, inner_ref, pair_ref, keep_ref, send_ref):
    fields, rows, _ = inner_ref.shape
    lower_core = core_index() == 0

    def step(t, _):
        span = pl.ds(pl.multiple_of(t * TILE, TILE), TILE)
        v, w = pair_ref[4, span], pair_ref[5, span]
        for f in range(fields):
            prev = jnp.concatenate([solved_ref[2 * t, f], solved_ref[2 * t + 1, f]], axis=0)
            own = jnp.concatenate(
                [solved_ref[2 * t, fields + f], solved_ref[2 * t + 1, fields + f]], axis=0
            )
            inner = inner_ref[f, span] - v * prev - w * own
            keep_ref[f, span] = jnp.where(lower_core, prev, inner)
            keep_ref[fields + f, span] = jnp.where(lower_core, inner, own)
            send_ref[f, span] = jnp.where(lower_core, inner, prev)
            send_ref[fields + f, span] = jnp.where(lower_core, own, inner)
        return 0

    lax.fori_loop(0, rows // TILE, step, 0)


def finish_kernel(mine, state_ref, v_ref, w_ref, y_ref, ends_ref, *refs):
    out_ref, block_ref, sems = refs[-3:]
    fields, planes, rows = state_ref.shape[1:4]
    last = planes - 1
    tiles = rows // TILE // 2
    side = half_of(mine)
    lines = pl.ds(pl.multiple_of(side * (rows // 2), rows // 2), rows // 2)
    copies = []
    for f in range(fields):

        def tile(t, _, f=f):
            span = pl.ds(pl.multiple_of((side * tiles + t) * TILE, TILE), TILE)
            place = pl.ds(pl.multiple_of(t * TILE, TILE), TILE)
            prev, own = ends_ref[f, place], ends_ref[fields + f, place]
            for i in range(last):
                delta = y_ref[i, f, place] - v_ref[i, span] * prev - w_ref[i, span] * own
                block_ref[f, i, place] = state_ref[0, f, i, span] + delta
            block_ref[f, last, place] = state_ref[0, f, last, span] + own
            return 0

        lax.fori_loop(0, tiles, tile, 0, unroll=True)
        copy = pltpu.make_async_copy(block_ref.at[f], out_ref.at[0, f, :, lines], sems.at[f])
        copy.start()
        copies.append(copy)
    for copy in copies:
        copy.wait()


def finish(mine, state, v, w, y, ends, partial=None):
    fields, planes, rows, lanes = state.shape[1:]
    hbm = pl.BlockSpec(memory_space=pltpu.HBM)
    operands = [state, v, w, y, ends]
    specs = [VMEM] * len(operands)
    aliases = {}
    if partial is not None:
        aliases = {len(operands): 0}
        operands.append(partial)
        specs.append(hbm)
    return pl.pallas_call(
        functools.partial(finish_kernel, mine),
        out_shape=jax.ShapeDtypeStruct(state.shape, jnp.float32),
        in_specs=specs,
        out_specs=hbm,
        scratch_shapes=[
            pltpu.VMEM((fields, planes, rows // 2, lanes), jnp.float32),
            pltpu.SemaphoreType.DMA((fields,)),
        ],
        input_output_aliases=aliases,
        compiler_params=pltpu.CompilerParams(vmem_limit_bytes=state.size * 12),
        cost_estimate=pl.CostEstimate(
            flops=state.size * 2, bytes_accessed=state.size * 6, transcendentals=0
        ),
    )(*operands)


def flux_parts(state, halo, flag_cells):
    fields, planes, rows, lanes = state.shape[1:]
    grid = (rows, lanes)
    shapes = [
        (planes, fields) + grid,
        (planes,) + grid,
        (planes - 1,) + grid,
        (planes - 1,) + grid,
        (planes - 1,) + grid,
        (COEFS, rows // 2, lanes),
        (COEFS, rows // 2, lanes),
        state.shape,
    ]
    return pl.pallas_call(
        flux_kernel,
        out_shape=[jax.ShapeDtypeStruct(x, jnp.float32) for x in shapes],
        in_specs=[pl.BlockSpec(memory_space=pltpu.HBM), VMEM, VMEM],
        out_specs=[VMEM] * len(shapes),
        scratch_shapes=[pltpu.SemaphoreType.DMA((planes,))],
        compiler_params=pltpu.CompilerParams(vmem_limit_bytes=state.size * 12),
        cost_estimate=pl.CostEstimate(
            flops=state.size * 60, bytes_accessed=state.size * 16, transcendentals=0
        ),
    )(pltpu.with_memory_space_constraint(state, pltpu.HBM), halo, flag_cells)


def exchange(x, axis, groups=None):
    return lax.all_to_all(x, axis, 0, 0, tiled=True, axis_index_groups=groups)


def body(flow_state, thinc_flags):
    own = flow_state[0]
    planes, rows, lanes = own.shape[1:]
    instances = lax.axis_size("inst")
    ax_count = lax.axis_size("ax")
    circ_count = lax.axis_size("circ")
    chips = ax_count // 2
    half = rows // 2
    piece = half // chips

    swap = [(i, i ^ 1) for i in range(ax_count)]
    groups = [list(range(c, ax_count, 2)) for c in range(2)]

    def partner(x):
        return lax.ppermute(x, "ax", swap)

    def neighbour(x, by):
        moves = [(i, i + 2 * by) for i in range(ax_count) if 0 <= i + 2 * by < ax_count]
        return lax.ppermute(x, "ax", moves)

    steps = slots(instances)
    order = ORDER
    rest = tuple(k for k in range(instances) if k != order[0])
    blocks = [None] * instances
    early = pick_first(flow_state, instances, order[0])
    *others, edges = pick_rest(flow_state, thinc_flags, early, instances, rest)
    blocks[order[0]] = early
    for k, block in zip(rest, others):
        blocks[k] = block
    halo = lax.ppermute(
        edges, "circ", [(i, (i + 1) % circ_count) for i in range(circ_count)]
    )
    for k in order:
        blocks[k] = lax.ppermute(blocks[k], "inst", route(*steps[k], instances))
    flags = (thinc_flags[0] > 0).astype(jnp.float32)
    flag_cells = jnp.broadcast_to(flags[:, :, None], (planes, rows, lanes))

    res, coup, inv, v, w, keep, send, held_state = flux_parts(flow_state, halo, flag_cells)

    thin = (half, lanes)
    pair, raw, ends = call(
        pair_kernel, [(6,) + thin, (3,) + thin, (2,) + thin], keep, partner(send)
    )
    ends = neighbour(ends, -1)
    link, edge = call(link_kernel, [(3,) + thin, (1,) + thin], raw, ends)
    head = RETURN[0]
    others = tuple(k for k in range(instances) if k != head)
    specs = [None] * instances
    for chosen in ((head,), others):
        parts = call(
            functools.partial(spectral_kernel, instances, chosen),
            [blocks[0].shape] * len(chosen),
            *blocks,
            flops=own.size * len(chosen),
        )
        for k, part in zip(chosen, parts):
            specs[k] = part
    for k in RETURN:
        specs[k] = lax.ppermute(specs[k], "inst", route(*steps[k], instances))
    edge = neighbour(edge, 1)
    (link,) = call(join_kernel, [(4,) + thin], link, edge)
    shapes = [(planes - 1, FIELDS, half, lanes), (2 * FIELDS, half, lanes)]
    parts = []
    for mine in (False, True):
        parts.append(
            call(
                functools.partial(sweep_kernel, mine),
                shapes,
                res,
                coup,
                inv,
                *specs,
                flops=own.size * 4,
                scratch=[(FIELDS, planes, TILE, lanes)],
            )
        )
    (y_other, send), (y_mine, keep) = parts
    inner, rhs = call(
        merge_kernel,
        [(FIELDS, half, lanes), (chips, 2 * FIELDS + 2, piece, lanes)],
        keep,
        partner(send),
        pair,
        link,
        flops=send.size * 4,
    )
    rhs = exchange(rhs, "ax", groups)
    (solved,) = call(
        reduced_kernel, [(chips, 2 * FIELDS, piece, lanes)], rhs, flops=rhs.size * 8
    )
    solved = exchange(solved, "ax", groups)
    keep, send = call(
        expand_kernel,
        [(2 * FIELDS, half, lanes)] * 2,
        solved,
        inner,
        pair,
        flops=send.size * 4,
    )
    got = partner(send)
    out = finish(True, held_state, v, w, y_mine, keep)
    return finish(False, held_state, v, w, y_other, got, out)


def solution(mesh):
    return jax.shard_map(
        body,
        mesh=mesh,
        in_specs=(P("inst", None, "ax", "circ", None), P("inst", "ax", "circ")),
        out_specs=P("inst", None, "ax", "circ", None),
        check_vma=False,
    )
```

```python
import functools
import math

import jax
import jax.numpy as jnp
from jax import lax
from jax.experimental import pallas as pl
from jax.experimental.pallas import tpu as pltpu
from jax.sharding import PartitionSpec as P


G_LIQ = 4.4
P_LIQ = 6.0
G_GAS = 1.4
BETA = 1.6
EPSA = 0.1
ALPHA = 4.0
DIAG0 = 0.016
OMEGA = 1.0
NU_T = 0.25

FIELDS = 7
ORDER = (5, 7, 3, 4, 1, 2, 6)
RETURN = (3, 7, 4, 5, 1, 2, 6)
EDGES = 2 * FIELDS + 3
COEFS = 5
TILE = 8


VMEM = pl.BlockSpec(memory_space=pltpu.VMEM)


def spectral_weights(count):
    table = []
    for k in range(count):
        if k == 0:
            first, second = 0.0, -(count * count + 2) / 12.0
        else:
            sign = 1.0 if k % 2 == 0 else -1.0
            angle = math.pi * k / count
            first = 0.5 * sign * math.cos(angle) / math.sin(angle)
            second = -sign / (2.0 * math.sin(angle) ** 2)
        table.append(OMEGA * first - NU_T * OMEGA * OMEGA * second)
    return table


def core_index():
    return lax.rem(lax.axis_index("ax"), 2)


def call(kernel, outs, *operands, flops=0, scratch=()):
    outs = [jax.ShapeDtypeStruct(shape, jnp.float32) for shape in outs]
    total = sum(x.size * 4 for x in operands) + sum(x.size * 4 for x in outs)
    run = pl.pallas_call(
        kernel,
        out_shape=outs,
        in_specs=[VMEM] * len(operands),
        out_specs=[VMEM] * len(outs),
        scratch_shapes=[pltpu.VMEM(x, jnp.float32) for x in scratch],
        compiler_params=pltpu.CompilerParams(
            vmem_limit_bytes=total + sum(math.prod(x) * 4 for x in scratch) + (2 << 20)
        ),
        cost_estimate=pl.CostEstimate(flops=flops, bytes_accessed=total, transcendentals=0),
    )
    return list(run(*operands))


def slots(count):
    steps = [(dy, dx) for dy in range(count // 2) for dx in range(2)]
    return steps


def route(dy, dx, count):
    ring = count // 2
    return [(i, 2 * ((i // 2 + dy) % ring) + ((i % 2) ^ dx)) for i in range(count)]


def places_of(count, chosen):
    index = lax.axis_index("inst")
    ring = count // 2
    steps = slots(count)
    return [
        2 * lax.rem(index // 2 + steps[k][0], ring) + lax.rem(lax.rem(index, 2) + steps[k][1], 2)
        for k in chosen
    ]


def first_kernel(count, chosen, state_ref, out_ref, sems):
    (place,) = places_of(count, (chosen,))
    copies = [
        pltpu.make_async_copy(state_ref.at[0, f, place], out_ref.at[f], sems.at[f])
        for f in range(out_ref.shape[0])
    ]
    for copy in copies:
        copy.start()
    for copy in copies:
        copy.wait()


def rest_kernel(count, chosen, state_ref, flag_ref, early_ref, *refs):
    outs = refs[: len(chosen)]
    edge_ref, held_ref, sems = refs[len(chosen) :]
    fields, rows = state_ref.shape[1], state_ref.shape[3]
    early = next(k for k in range(count) if k not in chosen)
    (early_place,), places = places_of(count, (early,)), places_of(count, chosen)
    copies = [
        pltpu.make_async_copy(state_ref.at[0, :, place], out, sems.at[k])
        for k, (place, out) in enumerate(zip(places, outs))
    ]
    for copy in copies:
        copy.start()
    flag_copy = pltpu.make_async_copy(flag_ref, held_ref, sems.at[len(chosen)])
    flag_copy.start()

    def edges(place, block):
        row = pl.ds(place, 1)
        for f in range(fields):
            edge_ref[f, row] = block[f, 0:1]
            edge_ref[fields + f, row] = block[f, rows - 1 : rows]
        edge_ref[2 * fields, row] = block[fields - 1, 1:2]
        edge_ref[2 * fields + 1, row] = block[fields - 1, rows - 2 : rows - 1]

    edges(early_place, early_ref)
    flag_copy.wait()
    flags = (held_ref[0] > 0).astype(jnp.float32)
    edge_ref[EDGES - 1] = jnp.broadcast_to(flags[:, 0:1], edge_ref.shape[1:])
    for copy, place, out in zip(copies, places, outs):
        copy.wait()
        edges(place, out)


def pick_first(state, count, chosen):
    _, fields, _, rows, lanes = state.shape
    return pl.pallas_call(
        functools.partial(first_kernel, count, chosen),
        out_shape=jax.ShapeDtypeStruct((fields, rows, lanes), jnp.float32),
        in_specs=[pl.BlockSpec(memory_space=pltpu.HBM)],
        out_specs=VMEM,
        scratch_shapes=[pltpu.SemaphoreType.DMA((fields,))],
        compiler_params=pltpu.CompilerParams(vmem_limit_bytes=4 << 20),
        cost_estimate=pl.CostEstimate(
            flops=0, bytes_accessed=fields * rows * lanes * 8, transcendentals=0
        ),
    )(pltpu.with_memory_space_constraint(state, pltpu.HBM))


def pick_rest(state, flags, early, count, chosen):
    _, fields, planes, rows, lanes = state.shape
    shapes = [(fields, rows, lanes)] * len(chosen) + [(EDGES, planes, lanes)]
    hbm = pl.BlockSpec(memory_space=pltpu.HBM)
    return pl.pallas_call(
        functools.partial(rest_kernel, count, chosen),
        out_shape=[jax.ShapeDtypeStruct(x, jnp.float32) for x in shapes],
        in_specs=[hbm, hbm, VMEM],
        out_specs=[VMEM] * len(shapes),
        scratch_shapes=[
            pltpu.VMEM(flags.shape, flags.dtype),
            pltpu.SemaphoreType.DMA((len(chosen) + 1,)),
        ],
        compiler_params=pltpu.CompilerParams(vmem_limit_bytes=state.size * 4 + (3 << 20)),
        cost_estimate=pl.CostEstimate(flops=0, bytes_accessed=state.size * 8, transcendentals=0),
    )(*(pltpu.with_memory_space_constraint(x, pltpu.HBM) for x in (state, flags)), early)


def mixing(count, parity):
    weights = spectral_weights(count)
    table = []
    for shift in (0, 1 - 2 * parity, 2 * parity - 1):
        g = [weights[(2 * a + shift) % count] for a in range(4)]
        table += [0.5 * (g[0] + g[2]), 0.5 * (g[1] + g[3])]
        table += [0.5 * (g[0] - g[2]), 0.5 * (g[1] - g[3])]
    return table


def spectral_kernel(count, chosen, *refs):
    ins, outs = refs[:count], dict(zip(chosen, refs[count:]))
    fields, rows, _ = ins[0].shape
    tiles = rows // TILE
    first = lax.rem(lax.axis_index("inst"), 2) == 0
    mix = [
        jnp.where(first, jnp.float32(a), jnp.float32(b))
        for a, b in zip(mixing(count, 0), mixing(count, 1))
    ]

    def step(index, _):
        f = index // tiles
        span = pl.ds(pl.multiple_of((index % tiles) * TILE, TILE), TILE)
        parts = []
        for dx in range(2):
            u = [ins[2 * dy + dx][f, span] for dy in range(4)]
            parts.append((u[0] + u[2], u[1] + u[3], u[0] - u[2], u[1] - u[3]))
        for ex in range(2):
            even, odd, even_next, odd_next = 0.0, 0.0, 0.0, 0.0
            for dx in range(2):
                kind = 0 if ex == dx else (1 if ex else 2)
                e0, e1, o0, o1 = mix[4 * kind : 4 * kind + 4]
                s0, s1, d0, d1 = parts[dx]
                even = even + (e0 * s0 + e1 * s1)
                odd = odd + (o0 * d0 + o1 * d1)
                even_next = even_next + (e1 * s0 + e0 * s1)
                odd_next = odd_next + (o1 * d0 - o0 * d1)
            for k, value in (
                (ex, even + odd),
                (4 + ex, even - odd),
                (2 + ex, even_next + odd_next),
                (6 + ex, even_next - odd_next),
            ):
                if k in outs:
                    outs[k][f, span] = value
        return 0

    lax.fori_loop(0, fields * tiles, step, 0, unroll=4)


def primitives(cells):
    density = cells[0] + cells[1]
    inverse = 1.0 / density
    vel_ax = cells[2] * inverse
    vel_circ = cells[3] * inverse
    vel_rad = cells[4] * inverse
    fraction = cells[6]
    gamma_term = fraction / (G_LIQ - 1.0) + (1.0 - fraction) / (G_GAS - 1.0)
    stiff_term = fraction * (G_LIQ * P_LIQ / (G_LIQ - 1.0))
    kinetic = 0.5 * density * (vel_ax * vel_ax + vel_circ * vel_circ + vel_rad * vel_rad)
    gamma_inv = 1.0 / gamma_term
    pressure = (cells[5] - kinetic - stiff_term) * gamma_inv
    sound_speed = jnp.sqrt(((1.0 + gamma_inv) * pressure + stiff_term * gamma_inv) * inverse)
    return vel_ax, vel_circ, pressure, sound_speed


def sharpen(lower_val, centre, upper_val, offset):
    average = 0.5 * (lower_val + upper_val)
    difference = upper_val - lower_val
    steepness = 2.0 * (centre - average) / (jnp.abs(difference) + EPSA)
    return average + 0.5 * difference * jnp.tanh(BETA * (steepness + offset))


def flux_kernel(
    source_ref,
    halo_ref,
    flag_ref,
    res_ref,
    coup_ref,
    inv_ref,
    v_ref,
    w_ref,
    keep_ref,
    send_ref,
    state_ref,
    sems,
):
    def fetch(i):
        return pltpu.make_async_copy(source_ref.at[0, :, i], state_ref.at[0, :, i], sems.at[i])

    for i in range(state_ref.shape[2]):
        fetch(i).start()

    planes = state_ref.shape[2]
    rows = state_ref.shape[3]
    last = planes - 1

    def plane(i, _):
        fetch(i).wait()
        row = pl.ds(i, 1)
        quad = (TILE // 2, state_ref.shape[4])
        cells = []
        for f in range(FIELDS):
            upper, lower = halo_ref[f, row], halo_ref[FIELDS + f, row]
            if f < FIELDS - 1:
                edge = [jnp.broadcast_to(upper, quad), jnp.broadcast_to(lower, quad)]
            else:
                next_upper = halo_ref[2 * FIELDS, row]
                next_lower = halo_ref[2 * FIELDS + 1, row]
                edge = [upper] + [next_upper] * 3 + [next_lower] * 3 + [lower]
            cells.append(jnp.concatenate([state_ref[0, f, i]] + edge, axis=0))
        edge = jnp.broadcast_to(halo_ref[EDGES - 1, row], (TILE, state_ref.shape[4]))
        flags = jnp.concatenate([flag_ref[i], edge], axis=0)
        total = rows + TILE

        def below(x, by=1):
            return pltpu.roll(x, by, 0)

        def above(x):
            return pltpu.roll(x, total - 1, 0)

        vel_ax, vel_circ, pressure, sound = primitives(cells)
        coup_ref[i] = -ALPHA * (jnp.abs(vel_ax) + sound)[:rows]
        wave = jnp.abs(vel_circ) + sound
        half_speed = 0.5 * jnp.maximum(below(wave), wave)
        fraction = cells[6]
        back1 = below(fraction)
        sharp_left = sharpen(below(fraction, 2), back1, fraction, 1.0)
        sharp_right = sharpen(back1, fraction, above(fraction), -1.0)
        flagged = flags > 0.5
        frac_left = jnp.where(flagged, sharp_left, back1)
        frac_right = jnp.where(flagged, sharp_right, fraction)
        for f in range(FIELDS):
            if f < 6:
                flux = cells[f] * vel_circ
                if f == 3:
                    flux = flux + pressure
                elif f == 5:
                    flux = flux + pressure * vel_circ
                mean = 0.5 * (below(flux) + flux)
                jump = cells[f] - below(cells[f])
            else:
                mean = 0.5 * (frac_left * below(vel_circ) + frac_right * vel_circ)
                jump = frac_right - frac_left
            face = mean - half_speed * jump
            res_ref[i, f] = (above(face) - face)[:rows]
        return 0

    lax.fori_loop(0, planes, plane, 0)

    core = core_index()
    tiles = rows // TILE // 2
    for target_ref, side in ((keep_ref, core), (send_ref, 1 - core)):

        def factor(t, _, target_ref=target_ref, side=side):
            span = pl.ds(pl.multiple_of((side * tiles + t) * TILE, TILE), TILE)
            place = pl.ds(pl.multiple_of(t * TILE, TILE), TILE)
            coup = [coup_ref[i, span] for i in range(planes)]
            inv, ratio, v = [], [], []
            for i in range(last):
                pivot = DIAG0 - 2.0 * coup[i]
                if i:
                    pivot = pivot - coup[i] * ratio[-1]
                inv.append(1.0 / pivot)
                ratio.append(coup[i] * inv[-1])
                v.append(inv[-1] if i == 0 else -(ratio[-1] * v[-1]))
                inv_ref[i, span] = inv[-1]
            v_next, w_next = v[-1], inv[-1]
            v_last, w_last = v_next * coup[0], w_next * coup[last - 1]
            for i in range(last - 1, -1, -1):
                if i < last - 1:
                    v_next = v[i] - ratio[i] * v_next
                    w_next = -(ratio[i] * w_next)
                v_first, w_first = v_next * coup[0], w_next * coup[last - 1]
                v_ref[i, span] = v_first
                w_ref[i, span] = w_first
            sep = coup[last]
            target_ref[0, place] = -(sep * v_last)
            target_ref[1, place] = DIAG0 - 2.0 * sep - sep * w_last
            target_ref[2, place] = sep
            target_ref[3, place] = v_first
            target_ref[4, place] = w_first
            return 0

        lax.fori_loop(0, tiles, factor, 0)


def pair_kernel(keep_ref, got_ref, pair_ref, raw_ref, ends_ref):
    lower_core = core_index() == 0
    lower_a, diag_a, sep_a, v_a, w_a = (
        jnp.where(lower_core, keep_ref[k], got_ref[k]) for k in range(COEFS)
    )
    lower_b, diag_b, sep_b, v_b, w_b = (
        jnp.where(lower_core, got_ref[k], keep_ref[k]) for k in range(COEFS)
    )
    inv = 1.0 / (diag_a - sep_a * v_b)
    v = inv * lower_a
    w = -(inv * sep_a * w_b)
    for k, x in enumerate((inv, sep_a, w_a, lower_b, v, w)):
        pair_ref[k] = x
    raw_ref[0] = diag_b - lower_b * w
    raw_ref[1] = -(lower_b * v)
    raw_ref[2] = sep_b
    ends_ref[0] = v_a - w_a * v
    ends_ref[1] = -(w_a * w)


def link_kernel(raw_ref, ends_ref, link_ref, edge_ref):
    sep = raw_ref[2]
    scale = 1.0 / (raw_ref[0] - sep * ends_ref[0])
    link_ref[0] = scale
    link_ref[1] = raw_ref[1] * scale
    link_ref[2] = -(sep * ends_ref[1]) * scale
    edge_ref[0] = sep * scale


def join_kernel(link_ref, edge_ref, out_ref):
    for k in range(3):
        out_ref[k] = link_ref[k]
    out_ref[3] = edge_ref[0]


def half_of(mine):
    core = core_index()
    return core if mine else 1 - core


def sweep_kernel(mine, res_ref, coup_ref, inv_ref, *refs):
    count = len(refs) - 3
    specs = refs[:count]
    y_ref, target_ref, right_ref = refs[count:]
    planes, fields, rows, _ = res_ref.shape
    last = planes - 1
    tiles = rows // TILE // 2
    side = half_of(mine)
    index = lax.axis_index("inst")
    ring = count // 2
    places = [
        2 * lax.rem(index // 2 + ring - dy, ring) + lax.rem(lax.rem(index, 2) + dx, 2)
        for dy, dx in slots(count)
    ]

    def step(t, _):
        span = pl.ds(pl.multiple_of((side * tiles + t) * TILE, TILE), TILE)
        place = pl.ds(pl.multiple_of(t * TILE, TILE), TILE)
        for f in range(fields):
            for i, spec_ref in zip(places, specs):
                right_ref[f, i] = -(res_ref[i, f, span] + spec_ref[f, span])
        coup = [coup_ref[i, span] for i in range(planes)]
        inv = [inv_ref[i, span] for i in range(last)]
        ratio = [coup[i] * inv[i] for i in range(last)]
        for f in range(fields):
            value = []
            for i in range(last):
                right = right_ref[f, i]
                if i:
                    right = right - coup[i] * value[-1]
                value.append(right * inv[i])
            y = value[-1]
            y_last = y
            y_ref[last - 1, f, place] = y
            for i in range(last - 2, -1, -1):
                y = value[i] - ratio[i] * y
                y_ref[i, f, place] = y
            target_ref[f, place] = y
            target_ref[fields + f, place] = right_ref[f, last] - coup[last] * y_last
        return 0

    lax.fori_loop(0, tiles, step, 0)


def merge_kernel(keep_ref, got_ref, pair_ref, link_ref, inner_ref, out_ref):
    fields = inner_ref.shape[0]
    rows = inner_ref.shape[1]
    lower_core = core_index() == 0

    def step(t, _):
        span = pl.ds(pl.multiple_of(t * TILE, TILE), TILE)
        inv, sep_a, first_a, lower_b = (pair_ref[k, span] for k in range(4))
        scale, lower, upper, edge = (link_ref[k, span] for k in range(4))
        for f in range(fields):
            keep_y, got_y = keep_ref[f, span], got_ref[f, span]
            keep_own, got_own = keep_ref[fields + f, span], got_ref[fields + f, span]
            y_a = jnp.where(lower_core, keep_y, got_y)
            y_b = jnp.where(lower_core, got_y, keep_y)
            own_a = jnp.where(lower_core, keep_own, got_own)
            own_b = jnp.where(lower_core, got_own, keep_own)
            inner = inv * (own_a - sep_a * y_b)
            inner_ref[f, span] = inner
            for k, x in (
                (f, scale * (own_b - lower_b * inner)),
                (fields + f, edge * (y_a - first_a * inner)),
            ):
                out_ref[2 * t, k] = x[0:4]
                out_ref[2 * t + 1, k] = x[4:8]
        for k, x in ((2 * fields, lower), (2 * fields + 1, upper)):
            out_ref[2 * t, k] = x[0:4]
            out_ref[2 * t + 1, k] = x[4:8]
        return 0

    lax.fori_loop(0, rows // TILE, step, 0)


def reduced_kernel(rhs_ref, out_ref):
    count = rhs_ref.shape[0]
    fields = out_ref.shape[1] // 2
    ratio = []
    values = []
    for p in range(count):
        lower, upper = rhs_ref[p, 2 * fields], rhs_ref[p, 2 * fields + 1]
        more = p + 1 < count
        inv = 1.0 / (1.0 - lower * ratio[-1]) if p else jnp.ones_like(lower)
        ratio.append(upper * inv)
        row = []
        for f in range(fields):
            right = rhs_ref[p, f]
            if more:
                right = right - rhs_ref[p + 1, fields + f]
            if p:
                right = right - lower * values[-1][f]
            row.append(right * inv)
        values.append(row)
    solved = values[-1]
    for p in range(count - 1, -1, -1):
        if p < count - 1:
            solved = [values[p][f] - ratio[p] * solved[f] for f in range(fields)]
        for f in range(fields):
            out_ref[p, fields + f] = solved[f]
            if p < count - 1:
                out_ref[p + 1, f] = solved[f]
    for f in range(fields):
        out_ref[0, f] = jnp.zeros_like(solved[f])


def expand_kernel(solved_ref, inner_ref, pair_ref, keep_ref, send_ref):
    fields, rows, _ = inner_ref.shape
    lower_core = core_index() == 0

    def step(t, _):
        span = pl.ds(pl.multiple_of(t * TILE, TILE), TILE)
        v, w = pair_ref[4, span], pair_ref[5, span]
        for f in range(fields):
            prev = jnp.concatenate([solved_ref[2 * t, f], solved_ref[2 * t + 1, f]], axis=0)
            own = jnp.concatenate(
                [solved_ref[2 * t, fields + f], solved_ref[2 * t + 1, fields + f]], axis=0
            )
            inner = inner_ref[f, span] - v * prev - w * own
            keep_ref[f, span] = jnp.where(lower_core, prev, inner)
            keep_ref[fields + f, span] = jnp.where(lower_core, inner, own)
            send_ref[f, span] = jnp.where(lower_core, inner, prev)
            send_ref[fields + f, span] = jnp.where(lower_core, own, inner)
        return 0

    lax.fori_loop(0, rows // TILE, step, 0)


def finish_kernel(mine, state_ref, v_ref, w_ref, y_ref, ends_ref, *refs):
    out_ref, block_ref, sems = refs[-3:]
    fields, planes, rows = state_ref.shape[1:4]
    last = planes - 1
    tiles = rows // TILE // 2
    side = half_of(mine)
    lines = pl.ds(pl.multiple_of(side * (rows // 2), rows // 2), rows // 2)
    copies = []
    for f in range(fields):

        def tile(t, _, f=f):
            span = pl.ds(pl.multiple_of((side * tiles + t) * TILE, TILE), TILE)
            place = pl.ds(pl.multiple_of(t * TILE, TILE), TILE)
            prev, own = ends_ref[f, place], ends_ref[fields + f, place]
            for i in range(last):
                delta = y_ref[i, f, place] - v_ref[i, span] * prev - w_ref[i, span] * own
                block_ref[f, i, place] = state_ref[0, f, i, span] + delta
            block_ref[f, last, place] = state_ref[0, f, last, span] + own
            return 0

        lax.fori_loop(0, tiles, tile, 0, unroll=True)
        copy = pltpu.make_async_copy(block_ref.at[f], out_ref.at[0, f, :, lines], sems.at[f])
        copy.start()
        copies.append(copy)
    for copy in copies:
        copy.wait()


def finish(mine, state, v, w, y, ends, partial=None):
    fields, planes, rows, lanes = state.shape[1:]
    hbm = pl.BlockSpec(memory_space=pltpu.HBM)
    operands = [state, v, w, y, ends]
    specs = [VMEM] * len(operands)
    aliases = {}
    if partial is not None:
        aliases = {len(operands): 0}
        operands.append(partial)
        specs.append(hbm)
    return pl.pallas_call(
        functools.partial(finish_kernel, mine),
        out_shape=jax.ShapeDtypeStruct(state.shape, jnp.float32),
        in_specs=specs,
        out_specs=hbm,
        scratch_shapes=[
            pltpu.VMEM((fields, planes, rows // 2, lanes), jnp.float32),
            pltpu.SemaphoreType.DMA((fields,)),
        ],
        input_output_aliases=aliases,
        compiler_params=pltpu.CompilerParams(vmem_limit_bytes=state.size * 12),
        cost_estimate=pl.CostEstimate(
            flops=state.size * 2, bytes_accessed=state.size * 6, transcendentals=0
        ),
    )(*operands)


def flux_parts(state, halo, flag_cells):
    fields, planes, rows, lanes = state.shape[1:]
    grid = (rows, lanes)
    shapes = [
        (planes, fields) + grid,
        (planes,) + grid,
        (planes - 1,) + grid,
        (planes - 1,) + grid,
        (planes - 1,) + grid,
        (COEFS, rows // 2, lanes),
        (COEFS, rows // 2, lanes),
        state.shape,
    ]
    return pl.pallas_call(
        flux_kernel,
        out_shape=[jax.ShapeDtypeStruct(x, jnp.float32) for x in shapes],
        in_specs=[pl.BlockSpec(memory_space=pltpu.HBM), VMEM, VMEM],
        out_specs=[VMEM] * len(shapes),
        scratch_shapes=[pltpu.SemaphoreType.DMA((planes,))],
        compiler_params=pltpu.CompilerParams(vmem_limit_bytes=state.size * 12),
        cost_estimate=pl.CostEstimate(
            flops=state.size * 60, bytes_accessed=state.size * 16, transcendentals=0
        ),
    )(pltpu.with_memory_space_constraint(state, pltpu.HBM), halo, flag_cells)


def exchange(x, axis, groups=None):
    return lax.all_to_all(x, axis, 0, 0, tiled=True, axis_index_groups=groups)


def body(flow_state, thinc_flags):
    own = flow_state[0]
    planes, rows, lanes = own.shape[1:]
    instances = lax.axis_size("inst")
    ax_count = lax.axis_size("ax")
    circ_count = lax.axis_size("circ")
    chips = ax_count // 2
    half = rows // 2
    piece = half // chips

    swap = [(i, i ^ 1) for i in range(ax_count)]
    groups = [list(range(c, ax_count, 2)) for c in range(2)]

    def partner(x):
        return lax.ppermute(x, "ax", swap)

    def neighbour(x, by):
        moves = [(i, i + 2 * by) for i in range(ax_count) if 0 <= i + 2 * by < ax_count]
        return lax.ppermute(x, "ax", moves)

    steps = slots(instances)
    order = ORDER
    rest = tuple(k for k in range(instances) if k != order[0])
    blocks = [None] * instances
    early = pick_first(flow_state, instances, order[0])
    *others, edges = pick_rest(flow_state, thinc_flags, early, instances, rest)
    blocks[order[0]] = early
    for k, block in zip(rest, others):
        blocks[k] = block
    halo = lax.ppermute(
        edges, "circ", [(i, (i + 1) % circ_count) for i in range(circ_count)]
    )
    for k in order:
        blocks[k] = lax.ppermute(blocks[k], "inst", route(*steps[k], instances))
    flags = (thinc_flags[0] > 0).astype(jnp.float32)
    flag_cells = jnp.broadcast_to(flags[:, :, None], (planes, rows, lanes))

    res, coup, inv, v, w, keep, send, held_state = flux_parts(flow_state, halo, flag_cells)

    thin = (half, lanes)
    pair, raw, ends = call(
        pair_kernel, [(6,) + thin, (3,) + thin, (2,) + thin], keep, partner(send)
    )
    ends = neighbour(ends, -1)
    link, edge = call(link_kernel, [(3,) + thin, (1,) + thin], raw, ends)
    head = RETURN[0]
    others = tuple(k for k in range(instances) if k != head)
    specs = [None] * instances
    for chosen in ((head,), others):
        parts = call(
            functools.partial(spectral_kernel, instances, chosen),
            [blocks[0].shape] * len(chosen),
            *blocks,
            flops=own.size * len(chosen),
        )
        for k, part in zip(chosen, parts):
            specs[k] = part
    for k in RETURN:
        specs[k] = lax.ppermute(specs[k], "inst", route(*steps[k], instances))
    edge = neighbour(edge, 1)
    (link,) = call(join_kernel, [(4,) + thin], link, edge)
    shapes = [(planes - 1, FIELDS, half, lanes), (2 * FIELDS, half, lanes)]
    parts = []
    for mine in (False, True):
        parts.append(
            call(
                functools.partial(sweep_kernel, mine),
                shapes,
                res,
                coup,
                inv,
                *specs,
                flops=own.size * 4,
                scratch=[(FIELDS, planes, TILE, lanes)],
            )
        )
    (y_other, send), (y_mine, keep) = parts
    inner, rhs = call(
        merge_kernel,
        [(FIELDS, half, lanes), (chips, 2 * FIELDS + 2, piece, lanes)],
        keep,
        partner(send),
        pair,
        link,
        flops=send.size * 4,
    )
    rhs = exchange(rhs, "ax", groups)
    (solved,) = call(
        reduced_kernel, [(chips, 2 * FIELDS, piece, lanes)], rhs, flops=rhs.size * 8
    )
    solved = exchange(solved, "ax", groups)
    keep, send = call(
        expand_kernel,
        [(2 * FIELDS, half, lanes)] * 2,
        solved,
        inner,
        pair,
        flops=send.size * 4,
    )
    got = partner(send)
    out = finish(True, held_state, v, w, y_mine, keep)
    return finish(False, held_state, v, w, y_other, got, out)


def solution(mesh):
    return jax.shard_map(
        body,
        mesh=mesh,
        in_specs=(P("inst", None, "ax", "circ", None), P("inst", "ax", "circ")),
        out_specs=P("inst", None, "ax", "circ", None),
        check_vma=False,
    )
```
